32 devices in a mesh: expert: 8 (over z, y), wshard: 4 (over x, core).
Axes of the slice: x: 2, y: 2, z: 4, core: 2. Of those that a mesh axis runs over, the one named last changes fastest.
Arguments:
- tokens: bfloat16 [4096, 2048], P(('expert', 'wshard')), may hold values from -6 to 6
- doc_lengths: int32 [32, 4], P(('expert', 'wshard')), may hold values from 1 to 64, 128 in all within a row
- expert_ids: int32 [4096, 8], P(('expert', 'wshard')), may hold values from 0 to 15, all different within a row; in each aligned block of 128 rows (0 to 127, 128 to 255, ...) at most 128 rows name the same one
- attn_gain: bfloat16 [2048], P('wshard'), may hold values from 0.5 to 1.5
- query_weight: bfloat16 [2048, 2048], P('wshard'), may hold values from -0.125 to 0.125
- key_weight: bfloat16 [2048, 2048], P('wshard'), may hold values from -0.125 to 0.125
- value_weight: bfloat16 [2048, 2048], P('wshard'), may hold values from -0.125 to 0.125
- query_gain: bfloat16 [2048], P('wshard'), may hold values from 0.5 to 1.5
- key_gain: bfloat16 [2048], P('wshard'), may hold values from 0.5 to 1.5
- output_weight: bfloat16 [2048, 2048], P('wshard'), may hold values from -0.5 to 0.5
- ffn_gain: bfloat16 [2048], P('wshard'), may hold values from 0.5 to 1.5
- router_weight: bfloat16 [2048, 16], P('wshard'), may hold values from -0.03125 to 0.03125
- gate_weight: bfloat16 [16, 2048, 1024], P('expert', 'wshard'), may hold values from -0.125 to 0.125
- up_weight: bfloat16 [16, 2048, 1024], P('expert', 'wshard'), may hold values from -0.125 to 0.125
- down_weight: bfloat16 [16, 1024, 2048], P('expert', None, 'wshard'), may hold values from -3 to 3
- cotangent: float32 [4096, 2048], P(('expert', 'wshard')), may hold values from -6 to 6
Outputs:
- block_output: float32 [4096, 2048], P(('expert', 'wshard'))
- tokens_grad: float32 [4096, 2048], P(('expert', 'wshard'))
- attn_gain_grad: float32 [2048], P(('expert', 'wshard'))
- query_weight_grad: float32 [2048, 2048], P(('expert', 'wshard'))
- key_weight_grad: float32 [2048, 2048], P(('expert', 'wshard'))
- value_weight_grad: float32 [2048, 2048], P(('expert', 'wshard'))
- query_gain_grad: float32 [2048], P(('expert', 'wshard'))
- key_gain_grad: float32 [2048], P(('expert', 'wshard'))
- output_weight_grad: float32 [2048, 2048], P(('expert', 'wshard'))
- ffn_gain_grad: float32 [2048], P(('expert', 'wshard'))
- router_weight_grad: float32 [2048, 16], P(('expert', 'wshard'))
- gate_weight_grad: float32 [16, 2048, 1024], P('expert', 'wshard')
- up_weight_grad: float32 [16, 2048, 1024], P('expert', 'wshard')
- down_weight_grad: float32 [16, 1024, 2048], P('expert', None, 'wshard')
The draws below stay inside these ranges and needn't reach their ends.
Inputs may be any that keep to these rules, and one draw needn't show every extreme that they name: `doc_lengths`: each device's row of lengths sums to 128, and its largest length is half of 128. `expert_ids`: each token names 8 different experts; within the rows of one device no expert is named more than 128 times, and in every draw some device names some expert exactly 128 times.
All inputs are finite; a program needn't handle non-finite values.
Results may differ from the reference program's by a relative error of at most 0.017.
Values may be sent and summed in bfloat16 or wider, within the bound.
No kernel may reach another device: no remote copies, remote signals or barrier semaphores. Data moves between devices by JAX's collectives and lax.ppermute only.
A program may use at most 384 MiB of HBM per device.

```python
import math
import jax
import jax.numpy as jnp
import numpy as np
from jax import lax

D = 2048
HEADS = 16
HEAD_DIM = 128
FF = 1024
TOP = 8
DOCS = 4
TOK_DEV = 128
SHARDS = 32
TOKENS = 4096
EXPERTS = 16
CAP = 128


def steps_of(rng, extent, pieces, smallest, largest):
    level = 1.0
    for axis_at, shards_of in pieces:
        steps = jax.random.uniform(jax.random.fold_in(jax.random.fold_in(rng, 6), axis_at), (shards_of,), jnp.float32, smallest / len(pieces), largest / len(pieces))
        level = level * jnp.repeat(jnp.exp(steps), extent[axis_at] // shards_of).reshape((-1,) + (1,) * (len(extent) - 1 - axis_at))
    return level


def split_up(count, total, limit, slope):
    portions = [(1 << 20) // math.isqrt(standing ** slope) + 1 for standing in range(2, count + 1)]
    rest, given = total - limit - (count - 1), [1] * (count - 1)
    while rest > 0:
        free = [i for i in range(count - 1) if given[i] < limit]
        pool, remaining = sum([portions[i] for i in free]), rest
        for i in free:
            addition = min(limit - given[i], max(1, remaining * portions[i] // pool), rest)
            given[i] = given[i] + addition
            rest = rest - addition
    return np.array([limit] + given)


def ragged(rng, number_of, total, most, slope):
    if number_of == 2:
        one = jax.random.randint(rng, (), max(1, total - most), min(most, total - 1) + 1)
        return jnp.stack([one, total - one])
    sizes = jnp.asarray(split_up(number_of, total, most, slope), jnp.int32)
    twos = (number_of - 1) // 2
    donor, taker = sizes[1:1 + 2 * twos:2], sizes[2:2 + 2 * twos:2]
    slack = jnp.minimum(donor - 1, most - taker)
    moved = jax.random.randint(jax.random.fold_in(rng, 1), (twos,), 0, 1 << 20) % (slack + 1)
    sizes = sizes.at[1:1 + 2 * twos:2].set(donor - moved).at[2:2 + 2 * twos:2].set(taker + moved)
    return sizes[jax.random.permutation(jax.random.fold_in(rng, 2), number_of)]


def assign_block(stream_key, own, number, rows, amount, top, reach, slope):
    sequence = jax.random.permutation(stream_key, amount)
    heavy_load, ordinary = portions_of(amount, rows * top, reach, slope, True), portions_of(amount, rows * top, reach, slope, False)
    places = jnp.arange(amount)

    def named(lengths, offset_by):
        used = int((lengths > 0).sum())
        fixed = max(1, used // 4)
        moved = fixed + (places - fixed + offset_by * (used - fixed)) % max(1, amount - fixed)
        return jnp.zeros((amount,), jnp.int32).at[sequence[jnp.where(places < fixed, places, moved)]].set(jnp.asarray(lengths, jnp.int32))

    lengths = jnp.where(number % 4 == 0, named(heavy_load, number // 4), named(ordinary, number - number // 4 - 1))
    mixed = jax.random.permutation(jax.random.fold_in(own, 3), amount)
    source_of, receiver = mixed[0:amount // 2 * 2:2], mixed[1:amount // 2 * 2:2]
    room = jnp.minimum(lengths[source_of] - 1, reach - lengths[receiver]) // 2
    room = jnp.where((source_of == sequence[0]) | (receiver == sequence[0]) | (lengths[receiver] == 0), 0, jnp.maximum(room, 0))
    moved = jax.random.randint(jax.random.fold_in(own, 4), (amount // 2,), 0, 1 << 20) % (room + 1)
    lengths = lengths.at[source_of].add(-moved).at[receiver].add(moved)
    items = jnp.searchsorted(jnp.cumsum(lengths), jnp.arange(rows * top), side="right").astype(jnp.int32)
    listing = items.reshape(top, rows).T
    listing = listing[jax.random.permutation(jax.random.fold_in(own, 1), rows)]
    offset_by = jax.random.randint(jax.random.fold_in(own, 2), (rows, 1), 0, top)
    return jnp.take_along_axis(listing, (jnp.arange(top)[None, :] + offset_by) % top, axis=1)


def portions_of(amount, total, reach, skew, full):
    weights = [(1 << 20) // math.isqrt(rank ** skew) + 1 for rank in range(1, amount + 1)]
    largest = reach if full else min(reach, max(-(-total // amount), total * weights[0] // sum(weights)))
    least = 1 if total - largest >= amount - 1 else 0
    counts, surplus = [largest] + [least] * (amount - 1), total - largest - least * (amount - 1)
    while surplus > 0:
        movable = [i for i in range(1, amount) if counts[i] < largest] or [i for i in range(1, amount) if counts[i] < reach]
        mass, budget = sum([weights[i] for i in movable]), surplus
        for i in movable:
            extra = min(reach - counts[i], max(1, budget * weights[i] // mass), surplus)
            counts[i] = counts[i] + extra
            surplus = surplus - extra
    return np.array(counts)


def scatter_about(key, shape, scale, limit, shards=(), kind=jnp.bfloat16):
    loudness = steps_of(key, shape, shards, -0.22, 0.18) if shards else 1.0
    entries = jax.random.normal(key, shape, jnp.float32) * scale * loudness
    return jnp.minimum(jnp.maximum(entries, -limit), limit).astype(kind)


def setup_inputs(seed: int = 0) -> dict:
    key_of = jax.random.split(jax.random.key(seed), 17)
    tokens = scatter_about(key_of[0], (TOKENS, D), 1.0, 6.0, ((0, 32),))
    doc_lengths = jax.vmap(lambda own: ragged(own, DOCS, TOK_DEV, TOK_DEV // 2, 2))(jax.random.split(key_of[1], SHARDS)).reshape((SHARDS, DOCS)).astype(jnp.int32)
    expert_ids_keys = jax.random.split(jax.random.fold_in(key_of[2], 1), TOKENS // TOK_DEV)
    expert_ids_turns = jax.random.permutation(jax.random.fold_in(key_of[2], 3), TOKENS // TOK_DEV)
    expert_ids = jax.vmap(lambda own, number: assign_block(jax.random.fold_in(key_of[2], 2), own, number, TOK_DEV, EXPERTS, TOP, CAP, 1))(expert_ids_keys, expert_ids_turns).reshape((TOKENS, TOP))
    attn_gain = jnp.clip(1.0 + 0.1 * jax.random.normal(key_of[3], (D,), jnp.float32), 0.5, 1.5).astype(jnp.bfloat16)
    query_weight = scatter_about(key_of[4], (D, D), D ** -0.5, 0.125, ((0, 4),))
    key_weight = scatter_about(key_of[5], (D, D), D ** -0.5, 0.125, ((0, 4),))
    value_weight = scatter_about(key_of[6], (D, D), D ** -0.5, 0.125, ((0, 4),))
    query_gain = jnp.clip(1.0 + 0.1 * jax.random.normal(key_of[7], (D,), jnp.float32), 0.5, 1.5).astype(jnp.bfloat16)
    key_gain = jnp.clip(1.0 + 0.1 * jax.random.normal(key_of[8], (D,), jnp.float32), 0.5, 1.5).astype(jnp.bfloat16)
    output_weight = scatter_about(key_of[9], (D, D), (D // 16) ** -0.5, 0.5, ((0, 4),))
    ffn_gain = jnp.clip(1.0 + 0.1 * jax.random.normal(key_of[10], (D,), jnp.float32), 0.5, 1.5).astype(jnp.bfloat16)
    router_weight = scatter_about(key_of[11], (D, EXPERTS), (D * 16) ** -0.5, 0.03125, ((0, 4),))
    gate_weight = scatter_about(key_of[12], (EXPERTS, D, FF), D ** -0.5, 0.125, ((0, 8), (1, 4)))
    up_weight = scatter_about(key_of[13], (EXPERTS, D, FF), D ** -0.5, 0.125, ((0, 8), (1, 4)))
    down_weight = scatter_about(key_of[14], (EXPERTS, FF, D), (max(FF // 256, 1)) ** -0.5, 3.0, ((0, 8), (2, 4)))
    cotangent = scatter_about(key_of[15], (TOKENS, D), 1.0, 6.0, ((0, 32),), jnp.float32)
    return dict(tokens=tokens, doc_lengths=doc_lengths, expert_ids=expert_ids, attn_gain=attn_gain, query_weight=query_weight, key_weight=key_weight, value_weight=value_weight, query_gain=query_gain, key_gain=key_gain, output_weight=output_weight, ffn_gain=ffn_gain, router_weight=router_weight, gate_weight=gate_weight, up_weight=up_weight, down_weight=down_weight, cotangent=cotangent)


epsilon = 1e-05
theta_base = 10000.0

def rms_forward(activation, gain):
    inverse = lax.rsqrt(lax.optimization_barrier(jnp.mean(activation * activation, axis=-1, keepdims=True)) + epsilon)
    normed = activation * inverse
    return (normed * gain.astype(jnp.float32), normed, inverse)

def rms_backward(grad_out, normed, inverse, gain):
    gain_grad = lax.optimization_barrier(jnp.sum(grad_out * normed, axis=0))
    grad_normed = grad_out * gain.astype(jnp.float32)
    centred = grad_normed - normed * lax.optimization_barrier(jnp.mean(grad_normed * normed, axis=-1, keepdims=True))
    return (inverse * centred, gain_grad)

def segment_info(doc_lengths, row_count):
    doc_ends = jnp.cumsum(doc_lengths).astype(jnp.int32)
    row_index = jnp.arange(row_count, dtype=jnp.int32)
    passed = (row_index[:, None] >= doc_ends[None, :]).astype(jnp.int32)
    doc_start = lax.optimization_barrier(jnp.sum(passed * doc_lengths[None, :], axis=1)).astype(jnp.int32)
    allowed = (row_index[None, :] <= row_index[:, None]) & (row_index[None, :] >= doc_start[:, None])
    return (row_index - doc_start, allowed)

def rope_tables(offsets):
    half_dim = HEAD_DIM // 2
    frequency = theta_base ** (-2.0 * jnp.arange(half_dim, dtype=jnp.float32) / HEAD_DIM)
    angles = offsets.astype(jnp.float32)[:, None] * frequency[None, :]
    return (jnp.cos(angles)[:, None, :], jnp.sin(angles)[:, None, :])

def rotate(head_rows, cosine, sine_table):
    half_dim = HEAD_DIM // 2
    first_half = head_rows[..., :half_dim]
    second_half = head_rows[..., half_dim:]
    return jnp.concatenate([first_half * cosine - second_half * sine_table, second_half * cosine + first_half * sine_table], axis=-1)

def unrotate(head_grads, cosine, sine_table):
    half_dim = HEAD_DIM // 2
    first_half = head_grads[..., :half_dim]
    second_half = head_grads[..., half_dim:]
    return jnp.concatenate([first_half * cosine + second_half * sine_table, second_half * cosine - first_half * sine_table], axis=-1)

def masked_scores(queries, key_rows, allowed):
    scale_factor = HEAD_DIM ** (-0.5)
    scores = jnp.einsum('qhd,khd->hqk', queries.astype(jnp.float32), key_rows.astype(jnp.float32)) * scale_factor
    return jnp.where(allowed[None, :, :], scores, -1e+30)

def attend_forward(queries, key_rows, value_rows, allowed):
    scores = masked_scores(queries, key_rows, allowed)
    row_max = lax.optimization_barrier(jnp.max(scores, axis=-1, keepdims=True))
    log_total = row_max + jnp.log(lax.optimization_barrier(jnp.sum(jnp.exp(scores - row_max), axis=-1, keepdims=True)))
    probs_b = jnp.exp(scores - log_total).astype(jnp.bfloat16)
    mixed_heads = jnp.einsum('hqk,khd->qhd', probs_b.astype(jnp.float32), value_rows.astype(jnp.float32))
    return (mixed_heads.astype(jnp.bfloat16), log_total)

def attend_backward(queries, key_rows, value_rows, allowed, log_total, mixed_b, grad_b):
    scale_factor = HEAD_DIM ** (-0.5)
    probs = jnp.exp(masked_scores(queries, key_rows, allowed) - log_total)
    probs_b = probs.astype(jnp.bfloat16)
    grad_f = grad_b.astype(jnp.float32)
    delta_rows = lax.optimization_barrier(jnp.sum(grad_f * mixed_b.astype(jnp.float32), axis=-1))
    grad_probs = jnp.einsum('qhd,khd->hqk', grad_f, value_rows.astype(jnp.float32))
    score_grad = (probs * (grad_probs - delta_rows.T[:, :, None])).astype(jnp.bfloat16).astype(jnp.float32)
    grad_queries = jnp.einsum('hqk,khd->qhd', score_grad, key_rows.astype(jnp.float32)) * scale_factor
    grad_keys = jnp.einsum('hqk,qhd->khd', score_grad, queries.astype(jnp.float32)) * scale_factor
    grad_values = jnp.einsum('hqk,qhd->khd', probs_b.astype(jnp.float32), grad_f)
    return (grad_queries, grad_keys, grad_values)

def softmax_rows(logits):
    row_max = lax.optimization_barrier(jnp.max(logits, axis=-1, keepdims=True))
    shifted = jnp.exp(logits - row_max)
    return shifted / lax.optimization_barrier(jnp.sum(shifted, axis=-1, keepdims=True))

def reference(tokens, doc_lengths, expert_ids, attn_gain, query_weight, key_weight, value_weight, query_gain, key_gain, output_weight, ffn_gain, router_weight, gate_weight, up_weight, down_weight, cotangent):
    residual = tokens.astype(jnp.float32)
    normed_in, unit_one, inverse_one = rms_forward(residual, attn_gain)
    attn_in = normed_in.astype(jnp.bfloat16)
    query_lin = jnp.dot(attn_in, query_weight, preferred_element_type=jnp.float32)
    key_lin = jnp.dot(attn_in, key_weight, preferred_element_type=jnp.float32)
    value_lin = jnp.dot(attn_in, value_weight, preferred_element_type=jnp.float32)
    query_normed, query_unit, query_inverse = rms_forward(query_lin, query_gain)
    key_normed, key_unit, key_inverse = rms_forward(key_lin, key_gain)
    value_b = value_lin.astype(jnp.bfloat16)
    head_shape = (TOK_DEV, HEADS, HEAD_DIM)

    def forward_block(packed):
        query_block, key_block, value_block, lengths_row = packed
        offsets, allowed = segment_info(lengths_row, TOK_DEV)
        cosine, sine_table = rope_tables(offsets)
        queries = rotate(query_block.reshape(head_shape), cosine, sine_table).astype(jnp.bfloat16)
        key_rows = rotate(key_block.reshape(head_shape), cosine, sine_table).astype(jnp.bfloat16)
        mixed_b, log_total = attend_forward(queries, key_rows, value_block.reshape(head_shape), allowed)
        return (queries, key_rows, mixed_b.reshape(TOK_DEV, D), log_total)
    block_shape = (SHARDS, TOK_DEV, D)
    queries_all, keys_all, mixed_all, totals_all = lax.map(forward_block, (query_normed.reshape(block_shape), key_normed.reshape(block_shape), value_b.reshape(block_shape), doc_lengths))
    attn_mix = mixed_all.reshape(TOKENS, D)
    middle = residual + jnp.dot(attn_mix, output_weight, preferred_element_type=jnp.float32)
    ffn_normed, unit_two, inverse_two = rms_forward(middle, ffn_gain)
    ffn_in = ffn_normed.astype(jnp.bfloat16)
    router_probs = softmax_rows(jnp.dot(ffn_in, router_weight, preferred_element_type=jnp.float32))
    route_weights = jnp.take_along_axis(router_probs, expert_ids, axis=1)
    assign_count = TOKENS * TOP
    flat_ids = expert_ids.reshape(SHARDS, TOK_DEV * TOP)
    expert_range = jnp.arange(EXPERTS, dtype=jnp.int32)
    one_hot = (flat_ids[:, :, None] == expert_range[None, None, :]).astype(jnp.int32)
    earlier = (jnp.cumsum(one_hot, axis=1) - one_hot).astype(jnp.int32)
    slot_index = lax.optimization_barrier(jnp.sum(earlier * one_hot, axis=2)).astype(jnp.int32)
    shard_index = jnp.arange(SHARDS, dtype=jnp.int32)[:, None]
    slot_place = (shard_index * CAP + slot_index).reshape(-1).astype(jnp.int32)
    slot_table = jnp.full((EXPERTS, SHARDS * CAP), assign_count, dtype=jnp.int32)
    slot_table = slot_table.at[flat_ids.reshape(-1), slot_place].set(jnp.arange(assign_count, dtype=jnp.int32))
    flat_weights = route_weights.reshape(-1)

    def expert_step(carry, packed):
        moe_sum, row_grads, weight_grads = carry
        assign, gate_w, up_w, down_w = packed
        occupied = assign < assign_count
        safe_assign = jnp.where(occupied, assign, 0).astype(jnp.int32)
        token_row = (safe_assign // TOP).astype(jnp.int32)
        picked = jnp.where(occupied[:, None], ffn_in[token_row], jnp.zeros((), jnp.bfloat16))
        gate_lin = jnp.dot(picked, gate_w, preferred_element_type=jnp.float32)
        up_lin = jnp.dot(picked, up_w, preferred_element_type=jnp.float32)
        sigmoid_gate = jax.nn.sigmoid(gate_lin)
        swish = gate_lin * sigmoid_gate
        hidden_b = (swish * up_lin).astype(jnp.bfloat16)
        expert_out = jnp.dot(hidden_b, down_w, preferred_element_type=jnp.float32).astype(jnp.bfloat16)
        expert_f = expert_out.astype(jnp.float32)
        weight_here = jnp.where(occupied, flat_weights[safe_assign], 0.0)
        grad_here = cotangent[token_row]
        moe_sum = moe_sum.at[token_row].add(weight_here[:, None] * expert_f)
        weight_grads = weight_grads.at[safe_assign].add(jnp.where(occupied, lax.optimization_barrier(jnp.sum(expert_f * grad_here, axis=1)), 0.0))
        out_grad = (weight_here[:, None] * grad_here).astype(jnp.bfloat16)
        hidden_grad = jnp.dot(out_grad, down_w.T, preferred_element_type=jnp.float32)
        down_grad = jnp.dot(hidden_b.T, out_grad, preferred_element_type=jnp.float32)
        gate_grad_b = (hidden_grad * up_lin * sigmoid_gate * (1.0 + gate_lin * (1.0 - sigmoid_gate))).astype(jnp.bfloat16)
        up_grad_b = (hidden_grad * swish).astype(jnp.bfloat16)
        gate_grad = jnp.dot(picked.T, gate_grad_b, preferred_element_type=jnp.float32)
        up_grad = jnp.dot(picked.T, up_grad_b, preferred_element_type=jnp.float32)
        picked_grad = (jnp.dot(gate_grad_b, gate_w.T, preferred_element_type=jnp.float32) + jnp.dot(up_grad_b, up_w.T, preferred_element_type=jnp.float32)).astype(jnp.bfloat16)
        row_grads = row_grads.at[token_row].add(picked_grad.astype(jnp.float32))
        return ((moe_sum, row_grads, weight_grads), (gate_grad, up_grad, down_grad))
    start_carry = (jnp.zeros((TOKENS, D), jnp.float32), jnp.zeros((TOKENS, D), jnp.float32), jnp.zeros((assign_count,), jnp.float32))
    (moe_sum, row_grads, weight_grads), (gate_weight_grad, up_weight_grad, down_weight_grad) = lax.scan(expert_step, start_carry, (slot_table, gate_weight, up_weight, down_weight))
    block_output = middle + moe_sum
    route_grad = weight_grads.reshape(TOKENS, TOP)
    hot_table = (expert_ids[:, :, None] == expert_range[None, None, :]).astype(jnp.float32)
    prob_grad = lax.optimization_barrier(jnp.sum(hot_table * route_grad[:, :, None], axis=1))
    logit_grad = router_probs * (prob_grad - lax.optimization_barrier(jnp.sum(router_probs * prob_grad, axis=1, keepdims=True)))
    logit_grad_b = logit_grad.astype(jnp.bfloat16)
    router_weight_grad = jnp.dot(ffn_in.T, logit_grad_b, preferred_element_type=jnp.float32)
    ffn_in_grad = row_grads + jnp.dot(logit_grad_b, router_weight.T, preferred_element_type=jnp.float32)
    middle_part, ffn_gain_grad = rms_backward(ffn_in_grad, unit_two, inverse_two, ffn_gain)
    middle_grad = cotangent + middle_part
    middle_grad_b = middle_grad.astype(jnp.bfloat16)
    output_weight_grad = jnp.dot(attn_mix.T, middle_grad_b, preferred_element_type=jnp.float32)
    attn_mix_grad = jnp.dot(middle_grad_b, output_weight.T, preferred_element_type=jnp.float32).astype(jnp.bfloat16)

    def backward_block(packed):
        queries, key_rows, value_block, lengths_row, log_total, mixed_block, grad_block = packed
        offsets, allowed = segment_info(lengths_row, TOK_DEV)
        cosine, sine_table = rope_tables(offsets)
        grad_queries, grad_keys, grad_values = attend_backward(queries, key_rows, value_block.reshape(head_shape), allowed, log_total, mixed_block.reshape(head_shape), grad_block.reshape(head_shape))
        return (unrotate(grad_queries, cosine, sine_table).reshape(TOK_DEV, D), unrotate(grad_keys, cosine, sine_table).reshape(TOK_DEV, D), grad_values.reshape(TOK_DEV, D))
    query_rot_grad, key_rot_grad, value_lin_grad = lax.map(backward_block, (queries_all, keys_all, value_b.reshape(block_shape), doc_lengths, totals_all, mixed_all, attn_mix_grad.reshape(block_shape)))
    query_lin_grad, query_gain_grad = rms_backward(query_rot_grad.reshape(TOKENS, D), query_unit, query_inverse, query_gain)
    key_lin_grad, key_gain_grad = rms_backward(key_rot_grad.reshape(TOKENS, D), key_unit, key_inverse, key_gain)
    query_grad_b = query_lin_grad.astype(jnp.bfloat16)
    key_grad_b = key_lin_grad.astype(jnp.bfloat16)
    value_grad_b = value_lin_grad.reshape(TOKENS, D).astype(jnp.bfloat16)
    query_weight_grad = jnp.dot(attn_in.T, query_grad_b, preferred_element_type=jnp.float32)
    key_weight_grad = jnp.dot(attn_in.T, key_grad_b, preferred_element_type=jnp.float32)
    value_weight_grad = jnp.dot(attn_in.T, value_grad_b, preferred_element_type=jnp.float32)
    attn_in_grad = jnp.dot(query_grad_b, query_weight.T, preferred_element_type=jnp.float32)
    attn_in_grad = attn_in_grad + jnp.dot(key_grad_b, key_weight.T, preferred_element_type=jnp.float32)
    attn_in_grad = attn_in_grad + jnp.dot(value_grad_b, value_weight.T, preferred_element_type=jnp.float32)
    input_part, attn_gain_grad = rms_backward(attn_in_grad, unit_one, inverse_one, attn_gain)
    tokens_grad = middle_grad + input_part
    return (block_output, tokens_grad, attn_gain_grad, query_weight_grad, key_weight_grad, value_weight_grad, query_gain_grad, key_gain_grad, output_weight_grad, ffn_gain_grad, router_weight_grad, gate_weight_grad, up_weight_grad, down_weight_grad)
```

```python
import jax
import jax.numpy as jnp
from jax import lax
from jax.sharding import PartitionSpec as P

HEADS = 16
HEAD_DIM = 128
TOP = 8
EXP_DEV = 2


epsilon = 1e-05
theta_base = 10000.0


def rms_unit(activation):
    inverse = lax.rsqrt(jnp.mean(activation * activation, axis=-1, keepdims=True) + epsilon)
    return (activation * inverse, inverse)


def rms_backward(grad_out, normed, inverse, gain):
    gain_grad = jnp.sum(grad_out * normed, axis=0)
    grad_normed = grad_out * gain
    centred = grad_normed - normed * jnp.mean(grad_normed * normed, axis=-1, keepdims=True)
    return (inverse * centred, gain_grad)


def block_tables(lengths, rows):
    ends = jnp.cumsum(lengths, axis=1)
    row_index = jnp.arange(rows, dtype=jnp.int32)
    passed = (row_index[None, :, None] >= ends[:, None, :]).astype(jnp.int32)
    start = jnp.sum(passed * lengths[:, None, :], axis=2)
    allowed = (row_index[None, None, :] <= row_index[None, :, None]) & (
        row_index[None, None, :] >= start[:, :, None]
    )
    offsets = (row_index[None, :] - start).reshape(-1)
    half_dim = HEAD_DIM // 2
    frequency = theta_base ** (-2.0 * jnp.arange(half_dim, dtype=jnp.float32) / HEAD_DIM)
    angles = offsets.astype(jnp.float32)[:, None] * frequency[None, :]
    return (allowed, jnp.cos(angles), jnp.sin(angles))


def rotate(rows, cosine, sine):
    half_dim = HEAD_DIM // 2
    first = rows[..., :half_dim]
    second = rows[..., half_dim:]
    cosine = cosine[:, None, :]
    sine = sine[:, None, :]
    return jnp.concatenate([first * cosine - second * sine, second * cosine + first * sine], axis=-1)


def softmax_rows(logits):
    row_max = jnp.max(logits, axis=-1, keepdims=True)
    shifted = jnp.exp(logits - row_max)
    return shifted / jnp.sum(shifted, axis=-1, keepdims=True)


def dot(a, b):
    return jnp.dot(a, b, preferred_element_type=jnp.float32)


def dot_t(a, b):
    return lax.dot_general(a, b, (((1,), (1,)), ((), ())), preferred_element_type=jnp.float32)


def t_dot(a, b):
    return lax.dot_general(a, b, (((0,), (0,)), ((), ())), preferred_element_type=jnp.float32)


def group_sum(values, axis_name):
    return jnp.sum(lax.all_gather(values, axis_name, axis=0), axis=0)


def local(
    tokens,
    doc_lengths,
    expert_ids,
    attn_gain,
    query_weight,
    key_weight,
    value_weight,
    query_gain,
    key_gain,
    output_weight,
    ffn_gain,
    router_weight,
    gate_weight,
    up_weight,
    down_weight,
    cotangent,
):
    bf16 = jnp.bfloat16
    f32 = jnp.float32
    rows, width = tokens.shape
    owners = lax.axis_size("expert")
    parts = lax.axis_size("wshard")
    w_index = lax.axis_index("wshard")
    experts = EXP_DEV * owners
    group = parts * rows
    cols = width // parts
    heads = HEADS // parts
    ff = gate_weight.shape[2]

    tokens_all = lax.all_gather(tokens, "wshard", axis=0, tiled=True)
    docs = doc_lengths.shape[1]
    lengths_row = jnp.zeros((1, cols), bf16).at[:, :docs].set(doc_lengths.astype(bf16))
    small = jnp.concatenate(
        [attn_gain[None, :], ffn_gain[None, :], lengths_row, router_weight.T], axis=0
    )
    small_all = lax.all_gather(small, "wshard", axis=0)
    attn_gain_all = small_all[:, 0, :].reshape(width).astype(f32)
    ffn_gain_all = small_all[:, 1, :].reshape(width).astype(f32)
    lengths_all = small_all[:, 2, :docs].astype(jnp.int32)
    router_t = small_all[:, 3:, :].transpose(1, 0, 2).reshape(experts, width)
    qkv_send = jnp.stack(
        [
            weight.reshape(cols, parts, cols)
            for weight in (query_weight, key_weight, value_weight)
        ],
        axis=2,
    )
    qkv_send = qkv_send.transpose(1, 0, 2, 3).reshape(parts * cols, 3 * cols)
    qkv_w = lax.all_to_all(qkv_send, "wshard", split_axis=0, concat_axis=0, tiled=True)

    gate_all = lax.all_gather(gate_weight, "wshard", axis=1, tiled=True)
    up_all = lax.all_gather(up_weight, "wshard", axis=1, tiled=True)
    down_all = lax.all_gather(down_weight, "wshard", axis=2, tiled=True)
    cot_all = lax.all_gather(cotangent.astype(bf16), "expert", axis=0, tiled=True)

    unit_all, _ = rms_unit(tokens_all.astype(f32))
    attn_in = (unit_all * attn_gain_all).astype(bf16)
    qkv = dot(attn_in, qkv_w)
    query_lin, key_lin, value_lin = (qkv[:, i * cols : (i + 1) * cols] for i in range(3))
    squares = jnp.stack(
        [jnp.sum(query_lin * query_lin, axis=1), jnp.sum(key_lin * key_lin, axis=1)], axis=0
    )
    squares = group_sum(squares, "wshard")
    inverses = lax.rsqrt(squares / width + epsilon)
    query_inverse = inverses[0][:, None]
    key_inverse = inverses[1][:, None]
    query_unit = query_lin * query_inverse
    key_unit = key_lin * key_inverse
    query_gain_f = query_gain.astype(f32)
    key_gain_f = key_gain.astype(f32)
    allowed, cosine, sine = block_tables(lengths_all, rows)
    wide = (group, heads, HEAD_DIM)
    blocked = (parts, rows, heads, HEAD_DIM)
    queries = rotate((query_unit * query_gain_f).reshape(wide), cosine, sine).astype(bf16)
    queries = queries.reshape(blocked)
    keys = rotate((key_unit * key_gain_f).reshape(wide), cosine, sine).astype(bf16)
    keys = keys.reshape(blocked)
    values = value_lin.astype(bf16).reshape(blocked)
    scale = HEAD_DIM ** (-0.5)
    scores = jnp.einsum("bqhd,bkhd->bhqk", queries, keys, preferred_element_type=f32) * scale
    scores = jnp.where(allowed[:, None, :, :], scores, -1e30)
    row_max = jnp.max(scores, axis=-1, keepdims=True)
    log_total = row_max + jnp.log(jnp.sum(jnp.exp(scores - row_max), axis=-1, keepdims=True))
    probs = jnp.exp(scores - log_total)
    probs_b = probs.astype(bf16)
    mixed = jnp.einsum("bhqk,bkhd->bqhd", probs_b, values, preferred_element_type=f32).astype(bf16)
    attn_mix = mixed.reshape(group, cols)
    attn_out = dot(attn_mix, output_weight).astype(bf16)
    attn_out = lax.psum_scatter(attn_out, "wshard", scatter_dimension=0, tiled=True)

    residual = tokens.astype(f32)
    middle = residual + attn_out.astype(f32)
    unit_two, inverse_two = rms_unit(middle)
    ffn_in = (unit_two * ffn_gain_all).astype(bf16)
    router_probs = softmax_rows(dot_t(ffn_in, router_t))
    expert_range = jnp.arange(experts, dtype=jnp.int32)
    named = jnp.any(expert_ids[:, :, None] == expert_range[None, None, :], axis=1)
    route_table = jnp.where(named, router_probs, 0.0)

    arrived = lax.all_gather(ffn_in, "expert", axis=0, tiled=True)
    weights = lax.all_to_all(
        route_table.reshape(rows, owners, EXP_DEV).transpose(1, 2, 0),
        "expert",
        split_axis=0,
        concat_axis=0,
        tiled=True,
    )
    weights = weights.transpose(1, 0, 2).reshape(EXP_DEV, owners * rows)
    gate_lin = jnp.einsum("rd,edf->erf", arrived, gate_all, preferred_element_type=f32)
    up_lin = jnp.einsum("rd,edf->erf", arrived, up_all, preferred_element_type=f32)
    hidden_back = jnp.einsum("rd,efd->erf", cot_all, down_all, preferred_element_type=f32)
    weight_col = weights[:, :, None]
    sigmoid_gate = jax.nn.sigmoid(gate_lin)
    swish = gate_lin * sigmoid_gate
    hidden = swish * up_lin
    route_back = jnp.sum(hidden * hidden_back, axis=2)
    hidden_w = (hidden * weight_col).astype(bf16)
    hidden_grad = hidden_back * weight_col
    gate_grad_b = (
        hidden_grad * up_lin * sigmoid_gate * (1.0 + gate_lin * (1.0 - sigmoid_gate))
    ).astype(bf16)
    up_grad_b = (hidden_grad * swish).astype(bf16)
    row_partial = jnp.einsum("erf,edf->rd", gate_grad_b, gate_all, preferred_element_type=f32)
    row_partial = row_partial + jnp.einsum(
        "erf,edf->rd", up_grad_b, up_all, preferred_element_type=f32
    )
    row_grads = lax.psum_scatter(
        row_partial.astype(bf16), "expert", scatter_dimension=0, tiled=True
    )
    route_back = lax.all_to_all(
        route_back.reshape(EXP_DEV, owners, rows).transpose(1, 0, 2),
        "expert",
        split_axis=0,
        concat_axis=0,
        tiled=True,
    )
    out_partial = jnp.einsum("erf,efd->rd", hidden_w, down_all, preferred_element_type=f32)
    moe_out = lax.psum_scatter(out_partial.astype(bf16), "expert", scatter_dimension=0, tiled=True)
    block_output = middle + moe_out.astype(f32)
    gate_part = jnp.einsum("rd,erf->edf", arrived, gate_grad_b, preferred_element_type=f32)
    up_part = jnp.einsum("rd,erf->edf", arrived, up_grad_b, preferred_element_type=f32)
    down_part = jnp.einsum("erf,rd->efd", hidden_w, cot_all, preferred_element_type=f32)
    gate_weight_grad = lax.psum_scatter(
        gate_part.astype(bf16), "wshard", scatter_dimension=1, tiled=True
    ).astype(f32)
    up_weight_grad = lax.psum_scatter(
        up_part.astype(bf16), "wshard", scatter_dimension=1, tiled=True
    ).astype(f32)
    down_weight_grad = lax.psum_scatter(
        down_part.astype(bf16), "wshard", scatter_dimension=2, tiled=True
    ).astype(f32)

    route_grad = route_back.reshape(experts, rows).T
    prob_grad = jnp.where(named, route_grad, 0.0)
    logit_grad = router_probs * (
        prob_grad - jnp.sum(router_probs * prob_grad, axis=1, keepdims=True)
    )
    logit_grad_b = logit_grad.astype(bf16)
    ffn_in_grad = row_grads.astype(f32) + dot(logit_grad_b, router_t)
    middle_part, ffn_gain_grad = rms_backward(ffn_in_grad, unit_two, inverse_two, ffn_gain_all)
    middle_grad = cotangent + middle_part
    router_grad = t_dot(logit_grad_b, ffn_in)

    mid_all = lax.all_gather(middle_grad.astype(bf16), "wshard", axis=0, tiled=True)
    output_part = t_dot(attn_mix, mid_all).astype(bf16)
    mix_grad = dot_t(mid_all, output_weight).astype(bf16).reshape(blocked)
    delta = jnp.sum(mix_grad.astype(f32) * mixed.astype(f32), axis=-1)
    prob_back = jnp.einsum("bqhd,bkhd->bhqk", mix_grad, values, preferred_element_type=f32)
    score_grad = (probs * (prob_back - delta.transpose(0, 2, 1)[:, :, :, None])).astype(bf16)
    grad_queries = jnp.einsum("bhqk,bkhd->bqhd", score_grad, keys, preferred_element_type=f32)
    grad_keys = jnp.einsum("bhqk,bqhd->bkhd", score_grad, queries, preferred_element_type=f32)
    grad_values = jnp.einsum("bhqk,bqhd->bkhd", probs_b, mix_grad, preferred_element_type=f32)
    grad_queries = rotate((grad_queries * scale).reshape(wide), cosine, -sine).reshape(group, cols)
    grad_keys = rotate((grad_keys * scale).reshape(wide), cosine, -sine).reshape(group, cols)
    query_gain_grad = jnp.sum(grad_queries * query_unit, axis=0)
    key_gain_grad = jnp.sum(grad_keys * key_unit, axis=0)
    grad_queries = grad_queries * query_gain_f
    grad_keys = grad_keys * key_gain_f
    means = jnp.stack(
        [jnp.sum(grad_queries * query_unit, axis=1), jnp.sum(grad_keys * key_unit, axis=1)], axis=0
    )
    means = group_sum(means, "wshard") / width
    query_grad_b = (query_inverse * (grad_queries - query_unit * means[0][:, None])).astype(bf16)
    key_grad_b = (key_inverse * (grad_keys - key_unit * means[1][:, None])).astype(bf16)
    value_grad_b = grad_values.reshape(group, cols).astype(bf16)
    qkv_grad = jnp.concatenate([query_grad_b, key_grad_b, value_grad_b], axis=1)
    attn_in_part = dot_t(qkv_grad, qkv_w).astype(bf16)
    attn_in_grad = lax.psum_scatter(attn_in_part, "wshard", scatter_dimension=0, tiled=True)
    qkv_part = t_dot(attn_in, qkv_grad).astype(bf16)

    unit_one, inverse_one = rms_unit(residual)
    input_part, attn_gain_grad = rms_backward(
        attn_in_grad.astype(f32), unit_one, inverse_one, attn_gain_all
    )
    tokens_grad = middle_grad + input_part

    qkv_sum = lax.psum_scatter(qkv_part, "expert", scatter_dimension=0, tiled=True)
    qkv_sum = lax.all_to_all(qkv_sum, "wshard", split_axis=0, concat_axis=0, tiled=True)
    final_rows = width // (owners * parts)
    qkv_sum = qkv_sum.reshape(parts, final_rows, 3, cols).transpose(2, 1, 0, 3)
    qkv_sum = qkv_sum.reshape(3, final_rows, width).astype(f32)
    output_sum = lax.psum_scatter(output_part, "expert", scatter_dimension=0, tiled=True)
    moves = []
    for e in range(owners):
        for w in range(parts):
            moves.append((e * parts + w, w * owners + e))
    output_sum = lax.ppermute(output_sum, ("expert", "wshard"), moves).astype(f32)

    own = jnp.zeros((2, parts, cols), f32)
    own = lax.dynamic_update_slice(
        own, jnp.stack([query_gain_grad, key_gain_grad])[:, None, :], (0, w_index, 0)
    ).reshape(2, width)
    table = jnp.concatenate([attn_gain_grad[None], ffn_gain_grad[None], own, router_grad], axis=0)
    count = table.shape[0]
    table = table.reshape(count, owners, parts * final_rows).transpose(1, 0, 2)
    table = jnp.sum(
        lax.all_to_all(table, "expert", split_axis=0, concat_axis=0, tiled=True), axis=0
    )
    table = table.reshape(count, parts, final_rows).transpose(1, 0, 2)
    table = jnp.sum(
        lax.all_to_all(table, "wshard", split_axis=0, concat_axis=0, tiled=True), axis=0
    )
    return (
        block_output,
        tokens_grad,
        table[0],
        qkv_sum[0],
        qkv_sum[1],
        qkv_sum[2],
        table[2],
        table[3],
        output_sum,
        table[1],
        table[4:].T,
        gate_weight_grad,
        up_weight_grad,
        down_weight_grad,
    )


def solution(mesh):
    in_specs = (
        P(("expert", "wshard"), None),
        P(("expert", "wshard"), None),
        P(("expert", "wshard"), None),
        P("wshard"),
        P("wshard", None),
        P("wshard", None),
        P("wshard", None),
        P("wshard"),
        P("wshard"),
        P("wshard", None),
        P("wshard"),
        P("wshard", None),
        P("expert", "wshard", None),
        P("expert", "wshard", None),
        P("expert", None, "wshard"),
        P(("expert", "wshard"), None),
    )
    out_specs = (
        P(("expert", "wshard"), None),
        P(("expert", "wshard"), None),
        P(("expert", "wshard")),
        P(("expert", "wshard"), None),
        P(("expert", "wshard"), None),
        P(("expert", "wshard"), None),
        P(("expert", "wshard")),
        P(("expert", "wshard")),
        P(("expert", "wshard"), None),
        P(("expert", "wshard")),
        P(("expert", "wshard"), None),
        P("expert", "wshard", None),
        P("expert", "wshard", None),
        P("expert", None, "wshard"),
    )
    return jax.shard_map(local, mesh=mesh, in_specs=in_specs, out_specs=out_specs, check_vma=False)
```

```python
import jax
import jax.numpy as jnp
from jax import lax
from jax.sharding import PartitionSpec as P


HEADS = 16
HEAD_DIM = 128
EXP_DEV = 2


epsilon = 1e-05
theta_base = 10000.0


def rms_unit(activation):
    inverse = lax.rsqrt(jnp.mean(activation * activation, axis=-1, keepdims=True) + epsilon)
    return (activation * inverse, inverse)


def rms_backward(grad_out, normed, inverse, gain):
    gain_grad = jnp.sum(grad_out * normed, axis=0)
    grad_normed = grad_out * gain
    centred = grad_normed - normed * jnp.mean(grad_normed * normed, axis=-1, keepdims=True)
    return (inverse * centred, gain_grad)


def block_tables(lengths, rows):
    ends = jnp.cumsum(lengths, axis=1)
    row_index = jnp.arange(rows, dtype=jnp.int32)
    passed = (row_index[None, :, None] >= ends[:, None, :]).astype(jnp.int32)
    start = jnp.sum(passed * lengths[:, None, :], axis=2)
    allowed = (row_index[None, None, :] <= row_index[None, :, None]) & (
        row_index[None, None, :] >= start[:, :, None]
    )
    offsets = (row_index[None, :] - start).reshape(-1)
    half_dim = HEAD_DIM // 2
    frequency = theta_base ** (-2.0 * jnp.arange(half_dim, dtype=jnp.float32) / HEAD_DIM)
    angles = offsets.astype(jnp.float32)[:, None] * frequency[None, :]
    return (allowed, jnp.cos(angles), jnp.sin(angles))


def rotate(rows, cosine, sine):
    half_dim = HEAD_DIM // 2
    first = rows[..., :half_dim]
    second = rows[..., half_dim:]
    cosine = cosine[None, :, :]
    sine = sine[None, :, :]
    return jnp.concatenate([first * cosine - second * sine, second * cosine + first * sine], axis=-1)


def softmax_rows(logits):
    row_max = jnp.max(logits, axis=-1, keepdims=True)
    shifted = jnp.exp(logits - row_max)
    return shifted / jnp.sum(shifted, axis=-1, keepdims=True)


def dot(a, b):
    return jnp.dot(a, b, preferred_element_type=jnp.float32)


def dot_t(a, b):
    return lax.dot_general(a, b, (((1,), (1,)), ((), ())), preferred_element_type=jnp.float32)


def t_dot(a, b):
    return lax.dot_general(a, b, (((0,), (0,)), ((), ())), preferred_element_type=jnp.float32)


def swap(values, mask, axis_name="wshard"):
    count = lax.axis_size(axis_name)
    return lax.ppermute(values, axis_name, [(i, i ^ mask) for i in range(count)])


def after(values, *others):
    return lax.optimization_barrier((values, *others))[0]


def bits_of(count):
    return [1 << k for k in range(count.bit_length() - 1)]


def gather_pieces(shard):
    pieces = {0: shard}
    for bit in reversed(bits_of(lax.axis_size("wshard"))):
        for mask in list(pieces):
            pieces[mask ^ bit] = swap(pieces[mask], bit)
    return [pieces[mask] for mask in sorted(pieces)]


def scatter_stage(blocks, bit):
    masks = sorted(blocks, reverse=True)
    arrived = {m ^ bit: swap(blocks[m].astype(jnp.bfloat16), bit) for m in masks if m & bit}
    return {m: blocks[m] + arrived[m].astype(jnp.float32) for m in arrived}


def scatter_near(blocks):
    return scatter_stage(dict(enumerate(blocks)), 1)


def scatter_far(blocks):
    for bit in bits_of(lax.axis_size("wshard"))[1:]:
        blocks = scatter_stage(blocks, bit)
    return blocks[0]


def scatter_pieces(blocks):
    return scatter_far(scatter_near(blocks))


def block_of(array, index, count, axis):
    size = array.shape[axis] // count
    return lax.dynamic_slice_in_dim(array, index * size, size, axis)


def mixed_order(array, w_index, count):
    return jnp.concatenate(
        [block_of(array, w_index ^ mask, count, array.ndim - 1) for mask in range(count)], axis=-1
    )


def group_sum(values, axis_name):
    return jnp.sum(lax.all_gather(values, axis_name, axis=0), axis=0)


def local(
    tokens,
    doc_lengths,
    expert_ids,
    attn_gain,
    query_weight,
    key_weight,
    value_weight,
    query_gain,
    key_gain,
    output_weight,
    ffn_gain,
    router_weight,
    gate_weight,
    up_weight,
    down_weight,
    cotangent,
):
    bf16 = jnp.bfloat16
    f32 = jnp.float32
    rows, width = tokens.shape
    owners = lax.axis_size("expert")
    parts = lax.axis_size("wshard")
    w_index = lax.axis_index("wshard")
    experts = EXP_DEV * owners
    group = parts * rows
    cols = width // parts
    heads = HEADS // parts
    final_rows = width // (owners * parts)
    ff = gate_weight.shape[2]

    e_index = lax.axis_index("expert")
    half = cols // 2
    unit = 2 * w_index + e_index % 2
    units = 2 * parts

    tokens_all = lax.all_gather(tokens, "wshard", axis=0, tiled=True)
    docs = doc_lengths.shape[1]
    lengths_row = jnp.zeros((1, cols), bf16).at[:, :docs].set(doc_lengths.astype(bf16))
    small = jnp.concatenate(
        [attn_gain[None, :], ffn_gain[None, :], lengths_row, router_weight.T], axis=0
    )
    small_all = lax.all_gather(small, "wshard", axis=0)
    attn_gain_all = small_all[:, 0, :].reshape(width).astype(f32)
    ffn_gain_all = small_all[:, 1, :].reshape(width).astype(f32)
    lengths_all = small_all[:, 2, :docs].astype(jnp.int32)
    router_t = small_all[:, 3:, :].transpose(1, 0, 2).reshape(experts, width)

    weights_in = after((query_weight, key_weight, value_weight), small_all)
    pieces = [None] * units
    for mask in reversed(range(parts)):
        piece = jnp.concatenate(
            [block_of(weight, w_index ^ mask, parts, 1) for weight in weights_in], axis=1
        )
        for side in range(2):
            pieces[2 * mask + side] = block_of(piece, side ^ (e_index % 2), 2, 0)
    for mask in reversed(range(1, parts)):
        pieces[2 * mask] = swap(pieces[2 * mask], mask)
        if mask == 1:
            pieces[3] = swap(pieces[3], 1)
    for mask in reversed(range(2, parts)):
        pieces[2 * mask + 1] = swap(pieces[2 * mask], 1, "expert")
    cot_b = mixed_order(cotangent, w_index, parts).astype(bf16)
    cot_all = lax.all_gather(cot_b, "expert", axis=0, tiled=True)
    down_in = after(down_weight, pieces[4])
    down_pieces = gather_pieces(down_in)

    unit_all, _ = rms_unit(tokens_all.astype(f32))
    attn_in = (unit_all * attn_gain_all).astype(bf16)
    attn_in_mixed = mixed_order(attn_in, unit, units)
    qkv = 0.0
    for at in [0, 1, 2, 3] + [2 * m for m in range(2, parts)] + [2 * m + 1 for m in range(2, parts)]:
        qkv = qkv + dot(attn_in_mixed[:, at * half : (at + 1) * half], pieces[at])
    query_lin, key_lin, value_lin = (qkv[:, i * cols : (i + 1) * cols] for i in range(3))
    squares = jnp.stack(
        [jnp.sum(query_lin * query_lin, axis=1), jnp.sum(key_lin * key_lin, axis=1)], axis=0
    )
    squares = group_sum(squares, "wshard")
    inverses = lax.rsqrt(squares / width + epsilon)
    query_inverse = inverses[0][:, None]
    key_inverse = inverses[1][:, None]
    query_unit = query_lin * query_inverse
    key_unit = key_lin * key_inverse
    query_gain_f = query_gain.astype(f32)
    key_gain_f = key_gain.astype(f32)
    allowed, cosine, sine = block_tables(lengths_all, rows)
    scale = HEAD_DIM ** (-0.5)

    def by_head(array):
        return jnp.stack(
            [array[:, h * HEAD_DIM : (h + 1) * HEAD_DIM] for h in range(heads)], axis=0
        )

    def by_row(array):
        return jnp.concatenate([array[h] for h in range(heads)], axis=1)

    blocked = (heads, parts, rows, HEAD_DIM)
    whole = (heads, group, HEAD_DIM)
    queries = rotate(by_head(query_unit * query_gain_f), cosine, sine).astype(bf16)
    queries = queries.reshape(blocked)
    keys = rotate(by_head(key_unit * key_gain_f), cosine, sine).astype(bf16).reshape(blocked)
    values = by_head(value_lin).astype(bf16).reshape(blocked)
    scores = jnp.einsum("hbqd,hbkd->hbqk", queries, keys, preferred_element_type=f32) * scale
    scores = jnp.where(allowed[None, :, :, :], scores, -1e30)
    row_max = jnp.max(scores, axis=-1, keepdims=True)
    log_total = row_max + jnp.log(jnp.sum(jnp.exp(scores - row_max), axis=-1, keepdims=True))
    probs = jnp.exp(scores - log_total)
    probs_b = probs.astype(bf16)
    mixed = jnp.einsum("hbqk,hbkd->hbqd", probs_b, values, preferred_element_type=f32).astype(bf16)
    attn_mix = by_row(mixed.reshape(whole))
    attn_out = dot(attn_mix, output_weight)
    attn_out = scatter_pieces(
        [block_of(attn_out, w_index ^ mask, parts, 0) for mask in range(parts)]
    )
    attn_out, cot_all, down_pieces, *pieces = lax.optimization_barrier(
        (attn_out, cot_all, down_pieces, *pieces)
    )
    qkv_w = jnp.concatenate([block_of(jnp.concatenate(pieces, axis=0), unit ^ k, units, 0) for k in range(units)], axis=0)
    down_all = jnp.concatenate(
        [piece.reshape(EXP_DEV * ff, cols) for piece in down_pieces], axis=1
    )
    residual = tokens.astype(f32)
    middle = residual + attn_out
    unit_two, inverse_two = rms_unit(middle)
    ffn_in = (unit_two * ffn_gain_all).astype(bf16)
    ffn_in_mixed = mixed_order(ffn_in, w_index, parts)
    gate_in, up_in, ffn_in_mixed, ffn_in = lax.optimization_barrier(
        (gate_weight, up_weight, ffn_in_mixed, ffn_in)
    )
    gate_pieces = gather_pieces(gate_in)
    up_pieces = gather_pieces(up_in)
    gate_up = jnp.concatenate(
        [
            jnp.concatenate([g[0], g[1], u[0], u[1]], axis=1)
            for g, u in zip(gate_pieces, up_pieces)
        ],
        axis=0,
    )

    router_probs = softmax_rows(dot_t(ffn_in, router_t))
    expert_range = jnp.arange(experts, dtype=jnp.int32)
    named = jnp.any(expert_ids[:, :, None] == expert_range[None, None, :], axis=1)
    route_table = jnp.where(named, router_probs, 0.0)

    arrived = lax.all_gather(ffn_in_mixed, "expert", axis=0, tiled=True)
    weights = lax.all_to_all(
        route_table.reshape(rows, owners, EXP_DEV).transpose(1, 2, 0),
        "expert",
        split_axis=0,
        concat_axis=0,
        tiled=True,
    )
    weights = weights.transpose(1, 0, 2).reshape(EXP_DEV, owners * rows)
    weight_cols = jnp.concatenate(
        [jnp.broadcast_to(w[:, None], (owners * rows, ff)) for w in weights], axis=1
    )
    wide = EXP_DEV * ff
    lin = dot(arrived, gate_up)
    gate_lin = lin[:, :wide]
    up_lin = lin[:, wide:]
    hidden_back = dot_t(cot_all, down_all)
    sigmoid_gate = jax.nn.sigmoid(gate_lin)
    swish = gate_lin * sigmoid_gate
    hidden = swish * up_lin
    route_back = jnp.sum((hidden * hidden_back).reshape(owners * rows, EXP_DEV, ff), axis=2).T
    hidden_w = (hidden * weight_cols).astype(bf16)
    hidden_grad = hidden_back * weight_cols
    gate_grad_b = (
        hidden_grad * up_lin * sigmoid_gate * (1.0 + gate_lin * (1.0 - sigmoid_gate))
    ).astype(bf16)
    up_grad_b = (hidden_grad * swish).astype(bf16)
    grads_b = jnp.concatenate([gate_grad_b, up_grad_b], axis=1)
    row_partial = dot_t(grads_b, gate_up).astype(bf16)
    row_grads = lax.psum_scatter(row_partial, "expert", scatter_dimension=0, tiled=True)
    route_back = lax.all_to_all(
        route_back.reshape(EXP_DEV, owners, rows).transpose(1, 0, 2),
        "expert",
        split_axis=0,
        concat_axis=0,
        tiled=True,
    )
    grads_b = after(grads_b, row_partial)
    part_of = lambda array, mask: array[:, mask * cols : (mask + 1) * cols]
    blocks = [None] * parts
    order = sorted(range(parts), key=lambda m: (m < parts // 2, -m))
    for mask in order[: parts // 2]:
        blocks[mask] = t_dot(part_of(arrived, mask), grads_b)
    grads_b = after(grads_b, *(blocks[mask] for mask in order[: parts // 2]))
    for mask in order[parts // 2 :]:
        blocks[mask] = t_dot(part_of(arrived, mask), grads_b)
    gate_up_sum = scatter_pieces(blocks)
    gate_up_sum = [gate_up_sum[:, k * ff : (k + 1) * ff] for k in range(2 * EXP_DEV)]
    gate_weight_grad = jnp.stack(gate_up_sum[:EXP_DEV])
    up_weight_grad = jnp.stack(gate_up_sum[EXP_DEV:])
    hidden_w, qkv_w, *_ = lax.optimization_barrier((hidden_w, qkv_w, *blocks))
    down_blocks = [t_dot(hidden_w, part_of(cot_all, mask)) for mask in range(parts)]
    down_blocks = scatter_near(down_blocks)
    out_partial = dot(hidden_w, down_all).astype(bf16)
    row_grads, out_partial = lax.optimization_barrier((row_grads, out_partial))
    moe_out = lax.psum_scatter(out_partial, "expert", scatter_dimension=0, tiled=True)

    route_grad = route_back.reshape(experts, rows).T
    prob_grad = jnp.where(named, route_grad, 0.0)
    logit_grad = router_probs * (
        prob_grad - jnp.sum(router_probs * prob_grad, axis=1, keepdims=True)
    )
    logit_grad_b = logit_grad.astype(bf16)
    ffn_in_grad = mixed_order(row_grads, w_index, parts).astype(f32) + dot(logit_grad_b, router_t)
    middle_part, ffn_gain_grad = rms_backward(ffn_in_grad, unit_two, inverse_two, ffn_gain_all)
    middle_grad = cotangent + middle_part
    router_grad = t_dot(logit_grad_b, ffn_in)

    mid_all = jnp.zeros((group, width), bf16)
    mid_pieces = gather_pieces(middle_grad.astype(bf16))
    down_blocks = after(down_blocks, *mid_pieces)
    down_weight_grad = scatter_far(down_blocks).reshape(EXP_DEV, ff, cols)
    for mask, piece in enumerate(mid_pieces):
        mid_all = lax.dynamic_update_slice(mid_all, piece, ((w_index ^ mask) * rows, 0))
    output_part = t_dot(attn_mix, mid_all).astype(bf16)
    output_sum = lax.all_to_all(
        output_part.reshape(owners, final_rows, width),
        "expert",
        split_axis=0,
        concat_axis=0,
        tiled=True,
    )
    output_sum = jnp.sum(output_sum.astype(f32), axis=0).astype(bf16)
    mix_grad = by_head(dot_t(mid_all, output_weight).astype(bf16)).reshape(blocked)
    delta = jnp.sum(mix_grad.astype(f32) * mixed.astype(f32), axis=-1, keepdims=True)
    prob_back = jnp.einsum("hbqd,hbkd->hbqk", mix_grad, values, preferred_element_type=f32)
    score_grad = (probs * (prob_back - delta)).astype(bf16)
    grad_queries = jnp.einsum("hbqk,hbkd->hbqd", score_grad, keys, preferred_element_type=f32)
    grad_keys = jnp.einsum("hbqk,hbqd->hbkd", score_grad, queries, preferred_element_type=f32)
    grad_values = jnp.einsum("hbqk,hbqd->hbkd", probs_b, mix_grad, preferred_element_type=f32)
    grad_queries = by_row(rotate((grad_queries * scale).reshape(whole), cosine, -sine))
    grad_keys = by_row(rotate((grad_keys * scale).reshape(whole), cosine, -sine))
    query_gain_grad = jnp.sum(grad_queries * query_unit, axis=0)
    key_gain_grad = jnp.sum(grad_keys * key_unit, axis=0)
    grad_queries = grad_queries * query_gain_f
    grad_keys = grad_keys * key_gain_f
    means = jnp.stack(
        [jnp.sum(grad_queries * query_unit, axis=1), jnp.sum(grad_keys * key_unit, axis=1)], axis=0
    )
    means = group_sum(means, "wshard") / width
    query_grad_b = (query_inverse * (grad_queries - query_unit * means[0][:, None])).astype(bf16)
    key_grad_b = (key_inverse * (grad_keys - key_unit * means[1][:, None])).astype(bf16)
    value_grad_b = by_row(grad_values.reshape(whole)).astype(bf16)
    qkv_grad = jnp.concatenate([query_grad_b, key_grad_b, value_grad_b], axis=1)
    attn_in_part = dot_t(qkv_grad, qkv_w)
    attn_in_grad = scatter_pieces(
        [block_of(attn_in_part, w_index ^ mask, parts, 0) for mask in range(parts)]
    )
    value_part = t_dot(attn_in, value_grad_b).astype(bf16).reshape(owners, parts * final_rows, cols)
    value_sum = lax.all_to_all(value_part, "expert", split_axis=0, concat_axis=0, tiled=True)
    value_sum = jnp.sum(value_sum.astype(f32), axis=0).astype(bf16)
    qk_part = t_dot(attn_in, qkv_grad[:, : 2 * cols]).astype(bf16)

    unit_one, inverse_one = rms_unit(residual)
    input_part, attn_gain_grad = rms_backward(
        attn_in_grad, unit_one, inverse_one, attn_gain_all
    )
    tokens_grad = middle_grad + input_part
    moe_out = after(moe_out, attn_in_part)
    block_output = middle + mixed_order(moe_out, w_index, parts).astype(f32)

    qk_sum = lax.psum_scatter(qk_part, "expert", scatter_dimension=0, tiled=True)
    qkv_sum = jnp.concatenate([qk_sum, value_sum], axis=1)
    qkv_sum = lax.all_to_all(qkv_sum, "wshard", split_axis=0, concat_axis=0, tiled=True)
    qkv_sum = qkv_sum.reshape(parts, final_rows, 3, cols).transpose(2, 1, 0, 3)
    qkv_sum = qkv_sum.reshape(3, final_rows, width).astype(f32)
    moves = []
    for e in range(owners):
        for w in range(parts):
            moves.append((e * parts + w, w * owners + e))
    output_sum = lax.ppermute(output_sum, ("expert", "wshard"), moves).astype(f32)

    own = jnp.zeros((2, parts, cols), f32)
    own = lax.dynamic_update_slice(
        own, jnp.stack([query_gain_grad, key_gain_grad])[:, None, :], (0, w_index, 0)
    ).reshape(2, width)
    table = jnp.concatenate([attn_gain_grad[None], ffn_gain_grad[None], own, router_grad], axis=0)
    count = table.shape[0]
    table = table.reshape(count, owners, parts * final_rows).transpose(1, 0, 2)
    table = lax.all_to_all(table, "expert", split_axis=0, concat_axis=0, tiled=True)
    table = jnp.sum(table, axis=0)
    table = table.reshape(count, parts, final_rows).transpose(1, 0, 2)
    table = jnp.sum(
        lax.all_to_all(table, "wshard", split_axis=0, concat_axis=0, tiled=True), axis=0
    )
    return (
        block_output,
        tokens_grad,
        table[0],
        qkv_sum[0],
        qkv_sum[1],
        qkv_sum[2],
        table[2],
        table[3],
        output_sum,
        table[1],
        table[4:].T,
        gate_weight_grad,
        up_weight_grad,
        down_weight_grad,
    )


def solution(mesh):
    in_specs = (
        P(("expert", "wshard"), None),
        P(("expert", "wshard"), None),
        P(("expert", "wshard"), None),
        P("wshard"),
        P("wshard", None),
        P("wshard", None),
        P("wshard", None),
        P("wshard"),
        P("wshard"),
        P("wshard", None),
        P("wshard"),
        P("wshard", None),
        P("expert", "wshard", None),
        P("expert", "wshard", None),
        P("expert", None, "wshard"),
        P(("expert", "wshard"), None),
    )
    out_specs = (
        P(("expert", "wshard"), None),
        P(("expert", "wshard"), None),
        P(("expert", "wshard")),
        P(("expert", "wshard"), None),
        P(("expert", "wshard"), None),
        P(("expert", "wshard"), None),
        P(("expert", "wshard")),
        P(("expert", "wshard")),
        P(("expert", "wshard"), None),
        P(("expert", "wshard")),
        P(("expert", "wshard"), None),
        P("expert", "wshard", None),
        P("expert", "wshard", None),
        P("expert", None, "wshard"),
    )

    return jax.shard_map(local, mesh=mesh, in_specs=in_specs, out_specs=out_specs, check_vma=False)
```

```python
import functools

import jax
import jax.numpy as jnp
from jax import lax
from jax.experimental import pallas as pl
from jax.experimental.pallas import tpu as pltpu
from jax.sharding import PartitionSpec as P


HEADS = 16
HEAD_DIM = 128
EXP_DEV = 2
OWNER = "expert"
SHARD = "wshard"


epsilon = 1e-05
theta_base = 10000.0


def rms_unit(activation):
    inverse = lax.rsqrt(jnp.mean(activation * activation, axis=-1, keepdims=True) + epsilon)
    return (activation * inverse, inverse)


def rms_backward(grad_out, normed, inverse, gain):
    gain_grad = jnp.sum(grad_out * normed, axis=0)
    grad_normed = grad_out * gain
    centred = grad_normed - normed * jnp.mean(grad_normed * normed, axis=-1, keepdims=True)
    return (inverse * centred, gain_grad)


def block_tables(lengths, rows):
    ends = jnp.cumsum(lengths, axis=1)
    row_index = jnp.arange(rows, dtype=jnp.int32)
    passed = (row_index[None, :, None] >= ends[:, None, :]).astype(jnp.int32)
    start = jnp.sum(passed * lengths[:, None, :], axis=2)
    allowed = (row_index[None, None, :] <= row_index[None, :, None]) & (
        row_index[None, None, :] >= start[:, :, None]
    )
    offsets = (row_index[None, :] - start).reshape(-1)
    half_dim = HEAD_DIM // 2
    frequency = theta_base ** (-2.0 * jnp.arange(half_dim, dtype=jnp.float32) / HEAD_DIM)
    angles = offsets.astype(jnp.float32)[:, None] * frequency[None, :]
    return (allowed, jnp.cos(angles), jnp.sin(angles))


def rotate(rows, cosine, sine):
    half_dim = HEAD_DIM // 2
    first = rows[..., :half_dim]
    second = rows[..., half_dim:]
    cosine = cosine[None, :, :]
    sine = sine[None, :, :]
    return jnp.concatenate([first * cosine - second * sine, second * cosine + first * sine], axis=-1)


def softmax_rows(logits):
    row_max = jnp.max(logits, axis=-1, keepdims=True)
    shifted = jnp.exp(logits - row_max)
    return shifted / jnp.sum(shifted, axis=-1, keepdims=True)


def dot(a, b):
    return jnp.dot(a, b, preferred_element_type=jnp.float32)


def dot_t(a, b):
    return lax.dot_general(a, b, (((1,), (1,)), ((), ())), preferred_element_type=jnp.float32)


def t_dot(a, b):
    return lax.dot_general(a, b, (((0,), (0,)), ((), ())), preferred_element_type=jnp.float32)


def swap(values, mask, axis_name=SHARD):
    count = lax.axis_size(axis_name)
    return lax.ppermute(values, axis_name, [(i, i ^ mask) for i in range(count)])


def after(values, *others):
    return lax.optimization_barrier((values, *others))[0]


def bits_of(count):
    return [1 << k for k in range(count.bit_length() - 1)]


def gather_far(shard):
    pieces = {0: shard}
    for bit in reversed(bits_of(lax.axis_size(SHARD))[1:]):
        for mask in list(pieces):
            pieces[mask ^ bit] = swap(pieces[mask], bit)
    return pieces


def gather_near(pieces):
    pieces = dict(pieces)
    for mask in list(pieces):
        pieces[mask ^ 1] = swap(pieces[mask], 1)
    return [pieces[mask] for mask in sorted(pieces)]


def gather_pieces(shard):
    return gather_near(gather_far(shard))


def scatter_stage(blocks, bit):
    masks = sorted(blocks, reverse=True)
    arrived = {m ^ bit: swap(blocks[m].astype(jnp.bfloat16), bit) for m in masks if m & bit}
    return {m: blocks[m] + arrived[m].astype(jnp.float32) for m in arrived}


def scatter_near(blocks):
    return scatter_stage(dict(enumerate(blocks)), 1)


def scatter_far(blocks):
    for bit in bits_of(lax.axis_size(SHARD))[1:]:
        blocks = scatter_stage(blocks, bit)
    return blocks[0]


def scatter_pieces(blocks):
    return scatter_far(scatter_near(blocks))


def block_of(array, index, count, axis):
    size = array.shape[axis] // count
    return lax.dynamic_slice_in_dim(array, index * size, size, axis)


def mixed_order(array, w_index, count):
    return jnp.concatenate(
        [block_of(array, w_index ^ mask, count, array.ndim - 1) for mask in range(count)], axis=-1
    )


def pair_dot(a, b, a_axis, b_axis):
    dims = (((a_axis,), (b_axis,)), ((0, 1), (0, 1)))
    return lax.dot_general(a, b, dims, preferred_element_type=jnp.float32)


def group_sum(values, axis_name):
    return jnp.sum(lax.all_gather(values, axis_name, axis=0), axis=0)


def expert_hidden_kernel(parts, x_ref, cot_ref, weight_ref, *refs):
    gates, ups, downs = refs[:parts], refs[parts : 2 * parts], refs[2 * parts : 3 * parts]
    hidden_ref, gate_grad_ref, up_grad_ref, route_ref = refs[3 * parts :]
    cols = gates[0].shape[0]
    f32 = jnp.float32
    gate_lin = up_lin = back = 0.0
    for m in range(parts):
        x = x_ref[:, m * cols : (m + 1) * cols]
        gate_lin = gate_lin + jnp.dot(x, gates[m][...], preferred_element_type=f32)
        up_lin = up_lin + jnp.dot(x, ups[m][...], preferred_element_type=f32)
        back = back + dot_t(cot_ref[:, m * cols : (m + 1) * cols], downs[m][...])
    weight = weight_ref[...]
    sigmoid = jax.nn.sigmoid(gate_lin)
    swish = gate_lin * sigmoid
    hidden = swish * up_lin
    product = hidden * back
    route = product[:, :128]
    for k in range(1, product.shape[1] // 128):
        route = route + product[:, k * 128 : (k + 1) * 128]
    hidden_ref[...] = (hidden * weight).astype(jnp.bfloat16)
    grad = back * weight
    gate_grad_ref[...] = (grad * up_lin * sigmoid * (1.0 + gate_lin * (1.0 - sigmoid))).astype(
        jnp.bfloat16
    )
    up_grad_ref[...] = (grad * swish).astype(jnp.bfloat16)

    @pl.when(pl.program_id(2) == 0)
    def _():
        route_ref[...] = route

    @pl.when(pl.program_id(2) > 0)
    def _():
        route_ref[...] += route


def row_tile_of(rows):
    return min(rows, 1024)


def expert_hidden(x, cot, weights, gates, ups, downs, tile=256):
    rows, width = x.shape
    parts = len(gates)
    count, cols, ff = gates[0].shape
    row_tile = row_tile_of(rows)
    steps = ff // tile
    row_spec = pl.BlockSpec((row_tile, width), lambda r, e, f: (r, 0))
    in_piece = pl.BlockSpec((None, cols, tile), lambda r, e, f: (e, 0, f))
    out_piece = pl.BlockSpec((None, tile, cols), lambda r, e, f: (e, f, 0))
    wide_spec = pl.BlockSpec((row_tile, tile), lambda r, e, f: (r, e * steps + f))
    wide = jax.ShapeDtypeStruct((rows, count * ff), jnp.bfloat16)
    return pl.pallas_call(
functools.partial(expert_hidden_kernel, parts),
grid=(rows // row_tile, count, steps),
in_specs=[row_spec, row_spec, pl.BlockSpec((None, row_tile, 1), lambda r, e, f: (e, r, 0))]
+ [in_piece] * (2 * parts)
+ [out_piece] * parts,
out_specs=[wide_spec] * 3
+ [pl.BlockSpec((None, row_tile, 128), lambda r, e, f: (e, r, 0))],
out_shape=[wide] * 3 + [jax.ShapeDtypeStruct((count, rows, 128), jnp.float32)],
compiler_params=pltpu.CompilerParams(vmem_limit_bytes=60 * 1024 * 1024),
    )(x, cot, weights, *gates, *ups, *downs)


def back_rows_kernel(parts, gate_grad_ref, up_grad_ref, *refs):
    gates, ups = refs[:parts], refs[parts : 2 * parts]
    out_ref, sum_ref = refs[2 * parts :]
    cols = gates[0].shape[0]
    step = pl.program_id(1) * pl.num_programs(2) + pl.program_id(2)
    last = pl.num_programs(1) * pl.num_programs(2) - 1
    for m in range(parts):
        at = slice(m * cols, (m + 1) * cols)
        part = dot_t(gate_grad_ref[...], gates[m][...]) + dot_t(up_grad_ref[...], ups[m][...])

        @pl.when(step == 0)
        def _():
            sum_ref[:, at] = part

        @pl.when((step > 0) & (step < last))
        def _():
            sum_ref[:, at] += part

        @pl.when(step == last)
        def _():
            out_ref[:, at] = (sum_ref[:, at] + part).astype(jnp.bfloat16)


def back_rows(gate_grad, up_grad, gates, ups, tile=512):
    rows = gate_grad.shape[0]
    parts = len(gates)
    count, cols, ff = gates[0].shape
    row_tile = row_tile_of(rows)
    steps = ff // tile
    wide_spec = pl.BlockSpec((row_tile, tile), lambda r, e, f: (r, e * steps + f))
    piece = pl.BlockSpec((None, cols, tile), lambda r, e, f: (e, 0, f))
    return pl.pallas_call(
functools.partial(back_rows_kernel, parts),
grid=(rows // row_tile, count, steps),
in_specs=[wide_spec] * 2 + [piece] * (2 * parts),
out_specs=pl.BlockSpec((row_tile, parts * cols), lambda r, e, f: (r, 0)),
out_shape=jax.ShapeDtypeStruct((rows, parts * cols), jnp.bfloat16),
scratch_shapes=[pltpu.VMEM((row_tile, parts * cols), jnp.float32)],
compiler_params=pltpu.CompilerParams(vmem_limit_bytes=60 * 1024 * 1024),
    )(gate_grad, up_grad, *gates, *ups)


def local(
    tokens,
    doc_lengths,
    expert_ids,
    attn_gain,
    query_weight,
    key_weight,
    value_weight,
    query_gain,
    key_gain,
    output_weight,
    ffn_gain,
    router_weight,
    gate_weight,
    up_weight,
    down_weight,
    cotangent,
):
    bf16 = jnp.bfloat16
    f32 = jnp.float32
    rows, width = tokens.shape
    owners = lax.axis_size(OWNER)
    parts = lax.axis_size(SHARD)
    w_index = lax.axis_index(SHARD)
    experts = EXP_DEV * owners
    group = parts * rows
    cols = width // parts
    heads = HEADS // parts
    final_rows = width // (owners * parts)
    ff = gate_weight.shape[2]

    e_index = lax.axis_index(OWNER)
    half = cols // 2
    unit = 2 * w_index + e_index % 2
    units = 2 * parts

    tokens_all = lax.all_gather(tokens, SHARD, axis=0, tiled=True)
    docs = doc_lengths.shape[1]
    lengths_row = jnp.zeros((1, cols), bf16).at[:, :docs].set(doc_lengths.astype(bf16))
    small = jnp.concatenate(
        [attn_gain[None, :], ffn_gain[None, :], lengths_row, router_weight.T], axis=0
    )
    small_all = lax.all_gather(small, SHARD, axis=0)
    attn_gain_all = small_all[:, 0, :].reshape(width).astype(f32)
    ffn_gain_all = small_all[:, 1, :].reshape(width).astype(f32)
    lengths_all = small_all[:, 2, :docs].astype(jnp.int32)
    router_t = small_all[:, 3:, :].transpose(1, 0, 2).reshape(experts, width)

    weights_in = after((query_weight, key_weight, value_weight), small_all)
    pieces = [None] * units
    for mask in reversed(range(parts)):
        piece = jnp.concatenate(
            [block_of(weight, w_index ^ mask, parts, 1) for weight in weights_in], axis=1
        )
        for side in range(2):
            pieces[2 * mask + side] = block_of(piece, side ^ (e_index % 2), 2, 0)
    for mask in reversed(range(1, parts)):
        pieces[2 * mask] = swap(pieces[2 * mask], mask)
        if mask == 1:
            pieces[3] = swap(pieces[3], 1)
    for mask in reversed(range(2, parts)):
        pieces[2 * mask + 1] = swap(pieces[2 * mask], 1, OWNER)
    cot_b = mixed_order(cotangent, w_index, parts).astype(bf16)
    cot_all = lax.all_gather(cot_b, OWNER, axis=0, tiled=True)
    down_in = after(down_weight, pieces[4])
    down_pieces = gather_far(down_in)

    unit_all, _ = rms_unit(tokens_all.astype(f32))
    attn_in = (unit_all * attn_gain_all).astype(bf16)
    attn_in_mixed = mixed_order(attn_in, unit, units)
    qkv = 0.0
    for at in [0, 1, 2, 3] + [2 * m for m in range(2, parts)] + [2 * m + 1 for m in range(2, parts)]:
        qkv = qkv + dot(attn_in_mixed[:, at * half : (at + 1) * half], pieces[at])
    query_lin, key_lin, value_lin = (qkv[:, i * cols : (i + 1) * cols] for i in range(3))
    squares = jnp.stack(
        [jnp.sum(query_lin * query_lin, axis=1), jnp.sum(key_lin * key_lin, axis=1)], axis=0
    )
    squares = group_sum(squares, SHARD)
    inverses = lax.rsqrt(squares / width + epsilon)
    query_inverse = inverses[0][:, None]
    key_inverse = inverses[1][:, None]
    query_unit = query_lin * query_inverse
    key_unit = key_lin * key_inverse
    query_gain_f = query_gain.astype(f32)
    key_gain_f = key_gain.astype(f32)
    allowed, cosine, sine = block_tables(lengths_all, rows)
    scale = HEAD_DIM ** (-0.5)

    def by_head(array):
        return jnp.stack(
            [array[:, h * HEAD_DIM : (h + 1) * HEAD_DIM] for h in range(heads)], axis=0
        )

    def by_row(array):
        return jnp.concatenate([array[h] for h in range(heads)], axis=1)

    blocked = (heads, parts, rows, HEAD_DIM)
    whole = (heads, group, HEAD_DIM)
    queries = rotate(by_head(query_unit * query_gain_f), cosine, sine).astype(bf16)
    queries = queries.reshape(blocked)
    keys = rotate(by_head(key_unit * key_gain_f), cosine, sine).astype(bf16).reshape(blocked)
    values = by_head(value_lin).astype(bf16).reshape(blocked)
    scores = pair_dot(queries, keys, 3, 3) * scale
    scores = jnp.where(allowed[None, :, :, :], scores, -1e30)
    row_max = jnp.max(scores, axis=-1, keepdims=True)
    log_total = row_max + jnp.log(jnp.sum(jnp.exp(scores - row_max), axis=-1, keepdims=True))
    probs = jnp.exp(scores - log_total)
    probs_b = probs.astype(bf16)
    mixed = pair_dot(probs_b, values, 3, 2).astype(bf16)
    attn_mix = by_row(mixed.reshape(whole))
    attn_out = dot(attn_mix, output_weight)
    attn_out = scatter_pieces(
        [block_of(attn_out, w_index ^ mask, parts, 0) for mask in range(parts)]
    )
    attn_out, cot_all, down_pieces, *pieces = lax.optimization_barrier(
        (attn_out, cot_all, down_pieces, *pieces)
    )
    down_pieces = gather_near(down_pieces)
    qkv_w = jnp.concatenate(pieces, axis=0)
    qkv_w = jnp.concatenate([block_of(qkv_w, unit ^ k, units, 0) for k in range(units)], axis=0)

    residual = tokens.astype(f32)
    middle = residual + attn_out
    unit_two, inverse_two = rms_unit(middle)
    ffn_in = (unit_two * ffn_gain_all).astype(bf16)
    ffn_in_mixed = mixed_order(ffn_in, w_index, parts)
    gate_in, up_in, ffn_in_mixed, ffn_in = lax.optimization_barrier(
        (gate_weight, up_weight, ffn_in_mixed, ffn_in)
    )
    gate_pieces = gather_pieces(gate_in)
    up_pieces = gather_pieces(up_in)
    router_probs = softmax_rows(dot_t(ffn_in, router_t))
    expert_range = jnp.arange(experts, dtype=jnp.int32)
    named = jnp.any(expert_ids[:, :, None] == expert_range[None, None, :], axis=1)
    route_table = jnp.where(named, router_probs, 0.0)

    arrived = lax.all_gather(ffn_in_mixed, OWNER, axis=0, tiled=True)
    weights = lax.all_to_all(
        route_table.reshape(rows, owners, EXP_DEV).transpose(1, 2, 0),
        OWNER,
        split_axis=0,
        concat_axis=0,
        tiled=True,
    )
    weights = weights.transpose(1, 0, 2).reshape(EXP_DEV, owners * rows, 1)
    hidden_w, gate_grad_b, up_grad_b, route_part = expert_hidden(
        arrived, cot_all, weights, gate_pieces, up_pieces, down_pieces
    )
    row_partial = back_rows(gate_grad_b, up_grad_b, gate_pieces, up_pieces)
    row_grads = lax.psum_scatter(row_partial, OWNER, scatter_dimension=0, tiled=True)
    route_back = jnp.sum(route_part, axis=2)
    route_back = lax.all_to_all(
        route_back.reshape(EXP_DEV, owners, rows).transpose(1, 0, 2),
        OWNER,
        split_axis=0,
        concat_axis=0,
        tiled=True,
    )
    part_of = lambda array, mask: array[:, mask * cols : (mask + 1) * cols]
    order = sorted(range(parts), key=lambda m: (m < parts // 2, -m))

    def ordered_blocks(make):
        blocks = [None] * parts
        for mask in order:
            blocks[mask] = make(mask)
        return blocks

    gate_blocks = ordered_blocks(lambda m: t_dot(part_of(arrived, m), gate_grad_b))
    gate_near = scatter_near(gate_blocks)
    up_blocks = ordered_blocks(lambda m: t_dot(part_of(arrived, m), up_grad_b))
    up_near = scatter_near(up_blocks)
    hidden_w, qkv_w, *_ = lax.optimization_barrier((hidden_w, qkv_w, *gate_blocks, *up_blocks))
    down_blocks = ordered_blocks(lambda m: t_dot(hidden_w, part_of(cot_all, m)))
    down_near = scatter_near(down_blocks)
    gate_sum = scatter_far(gate_near)
    gate_weight_grad = jnp.stack([gate_sum[:, e * ff : (e + 1) * ff] for e in range(EXP_DEV)])
    down_all = jnp.concatenate(
        [piece.reshape(EXP_DEV * ff, cols) for piece in down_pieces], axis=1
    )
    out_partial = dot(hidden_w, down_all).astype(bf16)
    row_grads, out_partial = lax.optimization_barrier((row_grads, out_partial))
    moe_out = lax.psum_scatter(out_partial, OWNER, scatter_dimension=0, tiled=True)

    route_grad = route_back.reshape(experts, rows).T
    prob_grad = jnp.where(named, route_grad, 0.0)
    logit_grad = router_probs * (
        prob_grad - jnp.sum(router_probs * prob_grad, axis=1, keepdims=True)
    )
    logit_grad_b = logit_grad.astype(bf16)
    ffn_in_grad = mixed_order(row_grads, w_index, parts).astype(f32) + dot(logit_grad_b, router_t)
    middle_part, ffn_gain_grad = rms_backward(ffn_in_grad, unit_two, inverse_two, ffn_gain_all)
    middle_grad = cotangent + middle_part
    router_grad = t_dot(logit_grad_b, ffn_in)

    mid_all = jnp.zeros((group, width), bf16)
    mid_pieces = gather_pieces(middle_grad.astype(bf16))
    up_sum = scatter_far(after(up_near, *mid_pieces))
    up_weight_grad = jnp.stack([up_sum[:, e * ff : (e + 1) * ff] for e in range(EXP_DEV)])
    for mask, piece in enumerate(mid_pieces):
        mid_all = lax.dynamic_update_slice(mid_all, piece, ((w_index ^ mask) * rows, 0))
    output_part = t_dot(attn_mix, mid_all).astype(bf16)
    output_sum = lax.all_to_all(
        output_part.reshape(owners, final_rows, width),
        OWNER,
        split_axis=0,
        concat_axis=0,
        tiled=True,
    )
    output_sum = jnp.sum(output_sum.astype(f32), axis=0).astype(bf16)
    mix_grad = by_head(dot_t(mid_all, output_weight).astype(bf16)).reshape(blocked)
    delta = jnp.sum(mix_grad.astype(f32) * mixed.astype(f32), axis=-1, keepdims=True)
    prob_back = pair_dot(mix_grad, values, 3, 3)
    score_grad = (probs * (prob_back - delta)).astype(bf16)
    grad_queries = pair_dot(score_grad, keys, 3, 2)
    grad_keys = pair_dot(score_grad, queries, 2, 2)
    grad_values = pair_dot(probs_b, mix_grad, 2, 2)
    grad_queries = by_row(rotate((grad_queries * scale).reshape(whole), cosine, -sine))
    grad_keys = by_row(rotate((grad_keys * scale).reshape(whole), cosine, -sine))
    query_gain_grad = jnp.sum(grad_queries * query_unit, axis=0)
    key_gain_grad = jnp.sum(grad_keys * key_unit, axis=0)
    grad_queries = grad_queries * query_gain_f
    grad_keys = grad_keys * key_gain_f
    means = jnp.stack(
        [jnp.sum(grad_queries * query_unit, axis=1), jnp.sum(grad_keys * key_unit, axis=1)], axis=0
    )
    means = group_sum(means, SHARD) / width
    query_grad_b = (query_inverse * (grad_queries - query_unit * means[0][:, None])).astype(bf16)
    key_grad_b = (key_inverse * (grad_keys - key_unit * means[1][:, None])).astype(bf16)
    value_grad_b = by_row(grad_values.reshape(whole)).astype(bf16)
    qkv_grad = jnp.concatenate([query_grad_b, key_grad_b, value_grad_b], axis=1)
    attn_in_part = dot_t(qkv_grad, qkv_w)
    attn_in_grad = scatter_pieces(
        [block_of(attn_in_part, w_index ^ mask, parts, 0) for mask in range(parts)]
    )
    value_part = t_dot(attn_in, value_grad_b).astype(bf16).reshape(owners, parts * final_rows, cols)
    down_weight_grad = scatter_far(after(down_near, attn_in_part)).reshape(EXP_DEV, ff, cols)
    value_sum = lax.all_to_all(value_part, OWNER, split_axis=0, concat_axis=0, tiled=True)
    value_sum = jnp.sum(value_sum.astype(f32), axis=0).astype(bf16)
    qk_part = t_dot(attn_in, qkv_grad[:, : 2 * cols]).astype(bf16)

    unit_one, inverse_one = rms_unit(residual)
    input_part, attn_gain_grad = rms_backward(
        attn_in_grad, unit_one, inverse_one, attn_gain_all
    )
    tokens_grad = middle_grad + input_part
    moe_out = after(moe_out, attn_in_part)
    block_output = middle + mixed_order(moe_out, w_index, parts).astype(f32)

    qk_sum = lax.psum_scatter(qk_part, OWNER, scatter_dimension=0, tiled=True)
    qkv_sum = jnp.concatenate([qk_sum, value_sum], axis=1)
    qkv_sum = lax.all_to_all(qkv_sum, SHARD, split_axis=0, concat_axis=0, tiled=True)
    qkv_sum = qkv_sum.reshape(parts, final_rows, 3, cols).transpose(2, 1, 0, 3)
    qkv_sum = qkv_sum.reshape(3, final_rows, width).astype(f32)
    moves = []
    for e in range(owners):
        for w in range(parts):
            moves.append((e * parts + w, w * owners + e))
    output_sum = lax.ppermute(output_sum, (OWNER, SHARD), moves).astype(f32)

    own = jnp.zeros((2, parts, cols), f32)
    own = lax.dynamic_update_slice(
        own, jnp.stack([query_gain_grad, key_gain_grad])[:, None, :], (0, w_index, 0)
    ).reshape(2, width)
    table = jnp.concatenate([attn_gain_grad[None], ffn_gain_grad[None], own, router_grad], axis=0)
    count = table.shape[0]
    table = table.reshape(count, owners, parts * final_rows).transpose(1, 0, 2)
    table = lax.all_to_all(table, OWNER, split_axis=0, concat_axis=0, tiled=True)
    table = jnp.sum(table, axis=0)
    table = table.reshape(count, parts, final_rows).transpose(1, 0, 2)
    table = jnp.sum(
        lax.all_to_all(table, SHARD, split_axis=0, concat_axis=0, tiled=True), axis=0
    )
    return (
        block_output,
        tokens_grad,
        table[0],
        qkv_sum[0],
        qkv_sum[1],
        qkv_sum[2],
        table[2],
        table[3],
        output_sum,
        table[1],
        table[4:].T,
        gate_weight_grad,
        up_weight_grad,
        down_weight_grad,
    )


def solution(mesh):
    rows = P((OWNER, SHARD), None)
    line = P((OWNER, SHARD))
    part = P(SHARD)
    wide = P(SHARD, None)
    into = P(OWNER, SHARD, None)
    back = P(OWNER, None, SHARD)
    in_specs = (rows,) * 3 + (part, wide, wide, wide, part, part, wide, part, wide)
    in_specs = in_specs + (into, into, back, rows)
    out_specs = (rows, rows, line, rows, rows, rows, line, line, rows, line, rows)
    out_specs = out_specs + (into, into, back)

    return jax.shard_map(local, mesh=mesh, in_specs=in_specs, out_specs=out_specs, check_vma=False)
```

```python
import functools

import jax
import jax.numpy as jnp
from jax import lax
from jax.experimental import pallas as pl
from jax.experimental.pallas import tpu as pltpu
from jax.sharding import PartitionSpec as P


HEADS = 16
HEAD_DIM = 128
EXP_DEV = 2
OWNER = "expert"
SHARD = "wshard"


epsilon = 1e-05
theta_base = 10000.0


def rms_unit(activation):
    inverse = lax.rsqrt(jnp.mean(activation * activation, axis=-1, keepdims=True) + epsilon)
    return (activation * inverse, inverse)


def rms_backward(grad_out, normed, inverse, gain):
    gain_grad = jnp.sum(grad_out * normed, axis=0)
    grad_normed = grad_out * gain
    centred = grad_normed - normed * jnp.mean(grad_normed * normed, axis=-1, keepdims=True)
    return (inverse * centred, gain_grad)


def block_tables(lengths, rows):
    ends = jnp.cumsum(lengths, axis=1)
    row_index = jnp.arange(rows, dtype=jnp.int32)
    passed = (row_index[None, :, None] >= ends[:, None, :]).astype(jnp.int32)
    start = jnp.sum(passed * lengths[:, None, :], axis=2)
    allowed = (row_index[None, None, :] <= row_index[None, :, None]) & (
        row_index[None, None, :] >= start[:, :, None]
    )
    offsets = (row_index[None, :] - start).reshape(-1)
    half_dim = HEAD_DIM // 2
    frequency = theta_base ** (-2.0 * jnp.arange(half_dim, dtype=jnp.float32) / HEAD_DIM)
    angles = offsets.astype(jnp.float32)[:, None] * frequency[None, :]
    return (allowed, jnp.cos(angles), jnp.sin(angles))


def rotate(rows, cosine, sine):
    half_dim = HEAD_DIM // 2
    first = rows[..., :half_dim]
    second = rows[..., half_dim:]
    cosine = cosine[None, :, :]
    sine = sine[None, :, :]
    return jnp.concatenate([first * cosine - second * sine, second * cosine + first * sine], axis=-1)


def softmax_rows(logits):
    row_max = jnp.max(logits, axis=-1, keepdims=True)
    shifted = jnp.exp(logits - row_max)
    return shifted / jnp.sum(shifted, axis=-1, keepdims=True)


def dot(a, b):
    return jnp.dot(a, b, preferred_element_type=jnp.float32)


def dot_t(a, b):
    return lax.dot_general(a, b, (((1,), (1,)), ((), ())), preferred_element_type=jnp.float32)


def t_dot(a, b):
    return lax.dot_general(a, b, (((0,), (0,)), ((), ())), preferred_element_type=jnp.float32)


def swap(values, mask, axis_name=SHARD):
    count = lax.axis_size(axis_name)
    return lax.ppermute(values, axis_name, [(i, i ^ mask) for i in range(count)])


def after(values, *others):
    return lax.optimization_barrier((values, *others))[0]


def bits_of(count):
    return [1 << k for k in range(count.bit_length() - 1)]


def gather_far(shard):
    pieces = {0: shard}
    for bit in reversed(bits_of(lax.axis_size(SHARD))[1:]):
        for mask in list(pieces):
            pieces[mask ^ bit] = swap(pieces[mask], bit)
    return pieces


def gather_near(pieces):
    pieces = dict(pieces)
    for mask in list(pieces):
        pieces[mask ^ 1] = swap(pieces[mask], 1)
    return [pieces[mask] for mask in sorted(pieces)]


def gather_pieces(shard):
    return gather_near(gather_far(shard))


def scatter_stage(blocks, bit):
    masks = sorted(blocks, reverse=True)
    arrived = {m ^ bit: swap(blocks[m].astype(jnp.bfloat16), bit) for m in masks if m & bit}
    return {m: blocks[m] + arrived[m].astype(jnp.float32) for m in arrived}


def scatter_near(blocks):
    return scatter_stage(dict(enumerate(blocks)), 1)


def scatter_far(blocks):
    for bit in bits_of(lax.axis_size(SHARD))[1:]:
        blocks = scatter_stage(blocks, bit)
    return blocks[0]


def scatter_pieces(blocks):
    return scatter_far(scatter_near(blocks))


def block_of(array, index, count, axis):
    size = array.shape[axis] // count
    return lax.dynamic_slice_in_dim(array, index * size, size, axis)


def mixed_order(array, w_index, count):
    return jnp.concatenate(
        [block_of(array, w_index ^ mask, count, array.ndim - 1) for mask in range(count)], axis=-1
    )


def pair_dot(a, b, a_axis, b_axis):
    dims = (((a_axis,), (b_axis,)), ((0, 1), (0, 1)))
    return lax.dot_general(a, b, dims, preferred_element_type=jnp.float32)


def group_sum(values):
    count = lax.axis_size(SHARD)
    blocks = values.reshape(values.shape[0], count, -1)
    total = blocks
    for mask in reversed(range(1, count)):
        arrived = swap(blocks, mask)
        total = total + jnp.stack([arrived[:, m ^ mask] for m in range(count)], axis=1)
    return total.reshape(values.shape)


def owner_scatter(values):
    owners = lax.axis_size(OWNER)
    index = lax.axis_index(OWNER)
    if owners > 8:
        return lax.psum_scatter(values, OWNER, scatter_dimension=0, tiled=True)[0]
    pairs = values.reshape(owners // 2, 2, *values.shape[1:])
    away = lax.dynamic_index_in_dim(pairs, 1 - index % 2, 1, keepdims=False)
    kept = lax.dynamic_index_in_dim(pairs, index % 2, 1, keepdims=False)
    arrived = swap(away, 1, OWNER)
    near = (kept.astype(jnp.float32) + arrived.astype(jnp.float32)).astype(jnp.bfloat16)
    total = 0.0
    for mask in reversed(range(owners // 2)):
        part = lax.dynamic_index_in_dim(near, (index // 2) ^ mask, 0, keepdims=False)
        if mask:
            part = swap(part, 2 * mask, OWNER)
        total = total + part.astype(jnp.float32)
    return total.astype(jnp.bfloat16)


def place_kernel(heads_ref, values_ref, query_ref, key_ref, value_ref):
    parts, _, cols = values_ref.shape
    for p in range(parts):
        at = slice(p * cols, (p + 1) * cols)
        query_ref[:, at] = heads_ref[p, :, :cols].astype(jnp.float32)
        key_ref[:, at] = heads_ref[p, :, cols:].astype(jnp.float32)
        value_ref[:, at] = values_ref[p].astype(jnp.float32)


def place(heads, values):
    parts, rows, cols = values.shape
    shape = jax.ShapeDtypeStruct((rows, parts * cols), jnp.float32)
    return pl.pallas_call(place_kernel, out_shape=[shape] * 3)(heads, values)


def expert_hidden_kernel(parts, x_ref, cot_ref, weight_ref, *refs):
    gates, ups, downs = refs[:parts], refs[parts : 2 * parts], refs[2 * parts : 3 * parts]
    hidden_ref, gate_grad_ref, up_grad_ref, route_ref = refs[3 * parts :]
    cols = gates[0].shape[0]
    f32 = jnp.float32
    gate_lin = up_lin = back = 0.0
    for m in range(parts):
        x = x_ref[:, m * cols : (m + 1) * cols]
        gate_lin = gate_lin + jnp.dot(x, gates[m][...], preferred_element_type=f32)
        up_lin = up_lin + jnp.dot(x, ups[m][...], preferred_element_type=f32)
        back = back + dot_t(cot_ref[:, m * cols : (m + 1) * cols], downs[m][...])
    weight = weight_ref[...]
    sigmoid = jax.nn.sigmoid(gate_lin)
    swish = gate_lin * sigmoid
    hidden = swish * up_lin
    product = hidden * back
    route = product[:, :128]
    for k in range(1, product.shape[1] // 128):
        route = route + product[:, k * 128 : (k + 1) * 128]
    hidden_ref[...] = (hidden * weight).astype(jnp.bfloat16)
    grad = back * weight
    gate_grad_ref[...] = (grad * up_lin * sigmoid * (1.0 + gate_lin * (1.0 - sigmoid))).astype(
        jnp.bfloat16
    )
    up_grad_ref[...] = (grad * swish).astype(jnp.bfloat16)

    @pl.when(pl.program_id(2) == 0)
    def _():
        route_ref[...] = route

    @pl.when(pl.program_id(2) > 0)
    def _():
        route_ref[...] += route


def row_tile_of(rows):
    return min(rows, 1024)


def expert_hidden(x, cot, weights, gates, ups, downs, tile=256):
    rows, width = x.shape
    parts = len(gates)
    count, cols, ff = gates[0].shape
    row_tile = row_tile_of(rows)
    steps = ff // tile
    row_spec = pl.BlockSpec((row_tile, width), lambda r, e, f: (r, 0))
    in_piece = pl.BlockSpec((None, cols, tile), lambda r, e, f: (e, 0, f))
    out_piece = pl.BlockSpec((None, tile, cols), lambda r, e, f: (e, f, 0))
    wide_spec = pl.BlockSpec((row_tile, tile), lambda r, e, f: (r, e * steps + f))
    wide = jax.ShapeDtypeStruct((rows, count * ff), jnp.bfloat16)
    return pl.pallas_call(
functools.partial(expert_hidden_kernel, parts),
grid=(rows // row_tile, count, steps),
in_specs=[row_spec, row_spec, pl.BlockSpec((None, row_tile, 1), lambda r, e, f: (e, r, 0))]
+ [in_piece] * (2 * parts)
+ [out_piece] * parts,
out_specs=[wide_spec] * 3
+ [pl.BlockSpec((None, row_tile, 128), lambda r, e, f: (e, r, 0))],
out_shape=[wide] * 3 + [jax.ShapeDtypeStruct((count, rows, 128), jnp.float32)],
compiler_params=pltpu.CompilerParams(vmem_limit_bytes=60 * 1024 * 1024),
    )(x, cot, weights, *gates, *ups, *downs)


def back_rows_kernel(parts, gate_grad_ref, up_grad_ref, *refs):
    gates, ups = refs[:parts], refs[parts : 2 * parts]
    out_ref, sum_ref = refs[2 * parts :]
    cols = gates[0].shape[0]
    step = pl.program_id(1) * pl.num_programs(2) + pl.program_id(2)
    last = pl.num_programs(1) * pl.num_programs(2) - 1
    for m in range(parts):
        at = slice(m * cols, (m + 1) * cols)
        part = dot_t(gate_grad_ref[...], gates[m][...]) + dot_t(up_grad_ref[...], ups[m][...])

        @pl.when(step == 0)
        def _():
            sum_ref[:, at] = part

        @pl.when((step > 0) & (step < last))
        def _():
            sum_ref[:, at] += part

        @pl.when(step == last)
        def _():
            out_ref[:, at] = (sum_ref[:, at] + part).astype(jnp.bfloat16)


def back_rows(gate_grad, up_grad, gates, ups, tile=512):
    rows = gate_grad.shape[0]
    parts = len(gates)
    count, cols, ff = gates[0].shape
    row_tile = row_tile_of(rows)
    steps = ff // tile
    wide_spec = pl.BlockSpec((row_tile, tile), lambda r, e, f: (r, e * steps + f))
    piece = pl.BlockSpec((None, cols, tile), lambda r, e, f: (e, 0, f))
    return pl.pallas_call(
functools.partial(back_rows_kernel, parts),
grid=(rows // row_tile, count, steps),
in_specs=[wide_spec] * 2 + [piece] * (2 * parts),
out_specs=pl.BlockSpec((row_tile, parts * cols), lambda r, e, f: (r, 0)),
out_shape=jax.ShapeDtypeStruct((rows, parts * cols), jnp.bfloat16),
scratch_shapes=[pltpu.VMEM((row_tile, parts * cols), jnp.float32)],
compiler_params=pltpu.CompilerParams(vmem_limit_bytes=60 * 1024 * 1024),
    )(gate_grad, up_grad, *gates, *ups)


def local(
    tokens,
    doc_lengths,
    expert_ids,
    attn_gain,
    query_weight,
    key_weight,
    value_weight,
    query_gain,
    key_gain,
    output_weight,
    ffn_gain,
    router_weight,
    gate_weight,
    up_weight,
    down_weight,
    cotangent,
):
    bf16 = jnp.bfloat16
    f32 = jnp.float32
    rows, width = tokens.shape
    owners = lax.axis_size(OWNER)
    parts = lax.axis_size(SHARD)
    w_index = lax.axis_index(SHARD)
    experts = EXP_DEV * owners
    group = parts * rows
    cols = width // parts
    heads = HEADS // parts
    final_rows = width // (owners * parts)
    ff = gate_weight.shape[2]

    e_index = lax.axis_index(OWNER)
    half = cols // 2
    unit = 2 * w_index + e_index % 2
    units = 2 * parts

    cot_b = mixed_order(cotangent, w_index, parts).astype(bf16)
    cot_all = lax.all_gather(cot_b, OWNER, axis=0, tiled=True)
    docs = doc_lengths.shape[1]
    lengths_row = jnp.zeros((1, cols), bf16).at[:, :docs].set(doc_lengths.astype(bf16))
    small = jnp.concatenate(
        [attn_gain[None, :], ffn_gain[None, :], lengths_row, router_weight.T], axis=0
    )
    small_all = lax.all_gather(small, SHARD, axis=0)
    attn_gain_all = small_all[:, 0, :].reshape(width).astype(f32)
    ffn_gain_all = small_all[:, 1, :].reshape(width).astype(f32)
    lengths_all = small_all[:, 2, :docs].astype(jnp.int32)
    lengths_all = jnp.concatenate([block_of(lengths_all, w_index ^ m, parts, 0) for m in range(parts)])
    router_t = small_all[:, 3:, :].transpose(1, 0, 2).reshape(experts, width)

    *weights_in, tokens_in, _ = lax.optimization_barrier(
        (query_weight, key_weight, value_weight, tokens, small_all)
    )
    tokens_far = gather_far(tokens_in)
    tokens_all = jnp.concatenate(gather_near(tokens_far), axis=0)
    pieces = [None] * units
    for mask in reversed(range(parts)):
        piece = jnp.concatenate(
            [block_of(weight, w_index ^ mask, parts, 1) for weight in weights_in], axis=1
        )
        for side in range(2):
            pieces[2 * mask + side] = block_of(piece, side ^ (e_index % 2), 2, 0)
    for mask in reversed(range(1, parts)):
        pieces[2 * mask] = swap(pieces[2 * mask], mask)
        if mask == 1:
            pieces[3] = swap(pieces[3], 1)
    for mask in reversed(range(2, parts)):
        pieces[2 * mask + 1] = swap(pieces[2 * mask], 1, OWNER)
    down_in = after(down_weight, pieces[4])
    down_pieces = gather_far(down_in)

    unit_all, _ = rms_unit(tokens_all.astype(f32))
    attn_in = (unit_all * attn_gain_all).astype(bf16)
    attn_in_mixed = mixed_order(attn_in, unit, units)
    qkv = 0.0
    for at in [0, 1, 2, 3] + [2 * m for m in range(2, parts)] + [2 * m + 1 for m in range(2, parts)]:
        qkv = qkv + dot(attn_in_mixed[:, at * half : (at + 1) * half], pieces[at])
    query_lin, key_lin, value_lin = (qkv[:, i * cols : (i + 1) * cols] for i in range(3))
    squares = jnp.stack(
        [jnp.sum(query_lin * query_lin, axis=1), jnp.sum(key_lin * key_lin, axis=1)], axis=0
    )
    squares = group_sum(squares)
    inverses = lax.rsqrt(squares / width + epsilon)
    query_inverse = inverses[0][:, None]
    key_inverse = inverses[1][:, None]
    query_unit = query_lin * query_inverse
    key_unit = key_lin * key_inverse
    query_gain_f = query_gain.astype(f32)
    key_gain_f = key_gain.astype(f32)
    allowed, cosine, sine = block_tables(lengths_all, rows)
    scale = HEAD_DIM ** (-0.5)

    def by_head(array):
        return jnp.stack(
            [array[:, h * HEAD_DIM : (h + 1) * HEAD_DIM] for h in range(heads)], axis=0
        )

    def by_row(array):
        return jnp.concatenate([array[h] for h in range(heads)], axis=1)

    blocked = (heads, parts, rows, HEAD_DIM)
    whole = (heads, group, HEAD_DIM)
    queries = rotate(by_head(query_unit * query_gain_f), cosine, sine).astype(bf16)
    queries = queries.reshape(blocked)
    keys = rotate(by_head(key_unit * key_gain_f), cosine, sine).astype(bf16).reshape(blocked)
    values = by_head(value_lin).astype(bf16).reshape(blocked)
    scores = pair_dot(queries, keys, 3, 3) * scale
    scores = jnp.where(allowed[None, :, :, :], scores, -1e30)
    row_max = jnp.max(scores, axis=-1, keepdims=True)
    log_total = row_max + jnp.log(jnp.sum(jnp.exp(scores - row_max), axis=-1, keepdims=True))
    probs = jnp.exp(scores - log_total)
    probs_b = probs.astype(bf16)
    mixed = pair_dot(probs_b, values, 3, 2).astype(bf16)
    attn_mix = by_row(mixed.reshape(whole))
    attn_out = dot(attn_mix, output_weight)
    attn_out = scatter_pieces([attn_out[mask * rows : (mask + 1) * rows] for mask in range(parts)])
    attn_out, cot_all, down_pieces, *pieces = lax.optimization_barrier(
        (attn_out, cot_all, down_pieces, *pieces)
    )
    down_pieces = gather_near(down_pieces)
    qkv_w = jnp.concatenate(pieces, axis=0)
    qkv_w = jnp.concatenate([block_of(qkv_w, unit ^ k, units, 0) for k in range(units)], axis=0)

    residual = tokens.astype(f32)
    middle = residual + attn_out
    unit_two, inverse_two = rms_unit(middle)
    ffn_in = (unit_two * ffn_gain_all).astype(bf16)
    ffn_in_mixed = mixed_order(ffn_in, w_index, parts)
    gate_in, up_in, ffn_in_mixed, ffn_in = lax.optimization_barrier(
        (gate_weight, up_weight, ffn_in_mixed, ffn_in)
    )
    gate_pieces = gather_pieces(gate_in)
    up_pieces = gather_pieces(up_in)
    router_probs = softmax_rows(dot_t(ffn_in, router_t))
    expert_range = jnp.arange(experts, dtype=jnp.int32)
    named = jnp.any(expert_ids[:, :, None] == expert_range[None, None, :], axis=1)
    route_table = jnp.where(named, router_probs, 0.0)

    arrived = lax.all_gather(ffn_in_mixed, OWNER, axis=0, tiled=True)
    weights = lax.all_to_all(
        route_table.reshape(rows, owners, EXP_DEV).transpose(1, 2, 0),
        OWNER,
        split_axis=0,
        concat_axis=0,
        tiled=True,
    )
    weights = weights.transpose(1, 0, 2).reshape(EXP_DEV, owners * rows, 1)
    hidden_w, gate_grad_b, up_grad_b, route_part = expert_hidden(
        arrived, cot_all, weights, gate_pieces, up_pieces, down_pieces
    )
    row_partial = back_rows(gate_grad_b, up_grad_b, gate_pieces, up_pieces)
    row_grads = lax.psum_scatter(row_partial, OWNER, scatter_dimension=0, tiled=True)
    route_back = jnp.sum(route_part, axis=2)
    route_back = lax.all_to_all(
        route_back.reshape(EXP_DEV, owners, rows).transpose(1, 0, 2),
        OWNER,
        split_axis=0,
        concat_axis=0,
        tiled=True,
    )
    part_of = lambda array, mask: array[:, mask * cols : (mask + 1) * cols]
    order = sorted(range(parts), key=lambda m: (m < parts // 2, -m))

    def ordered_blocks(make):
        blocks = [None] * parts
        for mask in order:
            blocks[mask] = make(mask)
        return blocks

    gate_blocks = ordered_blocks(lambda m: t_dot(part_of(arrived, m), gate_grad_b))
    gate_near = scatter_near(gate_blocks)
    up_blocks = ordered_blocks(lambda m: t_dot(part_of(arrived, m), up_grad_b))
    up_near = scatter_near(up_blocks)
    hidden_w, qkv_w, *_ = lax.optimization_barrier((hidden_w, qkv_w, *gate_blocks, *up_blocks))
    down_blocks = ordered_blocks(lambda m: t_dot(hidden_w, part_of(cot_all, m)))
    down_near = scatter_near(down_blocks)
    gate_sum = scatter_far(gate_near)
    gate_weight_grad = jnp.stack([gate_sum[:, e * ff : (e + 1) * ff] for e in range(EXP_DEV)])
    down_all = jnp.concatenate(
        [piece.reshape(EXP_DEV * ff, cols) for piece in down_pieces], axis=1
    )
    out_partial = dot(hidden_w, down_all).astype(bf16)
    moe_out = owner_scatter(out_partial.reshape(owners, rows, width))
    row_grads, route_back = lax.optimization_barrier((row_grads, route_back))

    route_grad = route_back.reshape(experts, rows).T
    prob_grad = jnp.where(named, route_grad, 0.0)
    logit_grad = router_probs * (
        prob_grad - jnp.sum(router_probs * prob_grad, axis=1, keepdims=True)
    )
    logit_grad_b = logit_grad.astype(bf16)
    ffn_in_grad = mixed_order(row_grads, w_index, parts).astype(f32) + dot(logit_grad_b, router_t)
    middle_part, ffn_gain_grad = rms_backward(ffn_in_grad, unit_two, inverse_two, ffn_gain_all)
    middle_grad = cotangent + middle_part
    router_grad = t_dot(logit_grad_b, ffn_in)

    mid_pieces = gather_pieces(middle_grad.astype(bf16))
    mid_all = jnp.concatenate(mid_pieces, axis=0)
    output_part = t_dot(attn_mix, mid_all).astype(bf16)
    output_sum = owner_scatter(output_part.reshape(owners, final_rows, width))
    mix_grad = by_head(dot_t(mid_all, output_weight).astype(bf16)).reshape(blocked)
    delta = jnp.sum(mix_grad.astype(f32) * mixed.astype(f32), axis=-1, keepdims=True)
    prob_back = pair_dot(mix_grad, values, 3, 3)
    score_grad = (probs * (prob_back - delta)).astype(bf16)
    grad_queries = pair_dot(score_grad, keys, 3, 2)
    grad_keys = pair_dot(score_grad, queries, 2, 2)
    grad_values = pair_dot(probs_b, mix_grad, 2, 2)
    grad_queries = by_row(rotate((grad_queries * scale).reshape(whole), cosine, -sine))
    grad_keys = by_row(rotate((grad_keys * scale).reshape(whole), cosine, -sine))
    query_gain_grad = jnp.sum(grad_queries * query_unit, axis=0)
    key_gain_grad = jnp.sum(grad_keys * key_unit, axis=0)
    grad_queries = grad_queries * query_gain_f
    grad_keys = grad_keys * key_gain_f
    means = jnp.stack(
        [jnp.sum(grad_queries * query_unit, axis=1), jnp.sum(grad_keys * key_unit, axis=1)], axis=0
    )
    means = group_sum(means) / width
    up_sum = scatter_far(after(up_near, means))
    up_weight_grad = jnp.stack([up_sum[:, e * ff : (e + 1) * ff] for e in range(EXP_DEV)])
    query_grad_b = (query_inverse * (grad_queries - query_unit * means[0][:, None])).astype(bf16)
    key_grad_b = (key_inverse * (grad_keys - key_unit * means[1][:, None])).astype(bf16)
    value_grad_b = by_row(grad_values.reshape(whole)).astype(bf16)
    qkv_grad = jnp.concatenate([query_grad_b, key_grad_b, value_grad_b], axis=1)
    attn_in_part = dot_t(qkv_grad, qkv_w)
    attn_in_grad = scatter_pieces(
        [attn_in_part[mask * rows : (mask + 1) * rows] for mask in range(parts)]
    )
    value_part = t_dot(attn_in, value_grad_b).astype(bf16).reshape(owners, parts * final_rows, cols)
    down_weight_grad = scatter_far(after(down_near, attn_in_part)).reshape(EXP_DEV, ff, cols)
    value_sum = owner_scatter(value_part).reshape(parts, final_rows, cols)
    value_sum = lax.all_to_all(value_sum, SHARD, split_axis=0, concat_axis=0, tiled=True)
    qk_part = t_dot(attn_in, qkv_grad[:, : 2 * cols])
    qk_part = qk_part.astype(bf16)

    unit_one, inverse_one = rms_unit(residual)
    input_part, attn_gain_grad = rms_backward(
        attn_in_grad, unit_one, inverse_one, attn_gain_all
    )
    tokens_grad = middle_grad + input_part
    moe_out = after(moe_out, attn_in_part)
    block_output = middle + mixed_order(moe_out, w_index, parts).astype(f32)

    qk_sum = lax.psum_scatter(qk_part, OWNER, scatter_dimension=0, tiled=True)
    qk_sum = qk_sum.reshape(parts, final_rows, 2 * cols)
    qk_sum = lax.all_to_all(qk_sum, SHARD, split_axis=0, concat_axis=0, tiled=True)
    qkv_sum = place(qk_sum, value_sum)
    moves = []
    for e in range(owners):
        for w in range(parts):
            moves.append((e * parts + w, w * owners + e))
    output_sum = lax.ppermute(output_sum, (OWNER, SHARD), moves).astype(f32)

    own = jnp.zeros((2, parts, cols), f32)
    own = lax.dynamic_update_slice(
        own, jnp.stack([query_gain_grad, key_gain_grad])[:, None, :], (0, w_index, 0)
    ).reshape(2, width)
    table = jnp.concatenate([attn_gain_grad[None], ffn_gain_grad[None], own, router_grad], axis=0)
    count = table.shape[0]
    table = table.reshape(count, owners, parts * final_rows).transpose(1, 0, 2)
    table = lax.all_to_all(table, OWNER, split_axis=0, concat_axis=0, tiled=True)
    table = jnp.sum(table, axis=0)
    table = table.reshape(count, parts, final_rows).transpose(1, 0, 2)
    table = jnp.sum(
        lax.all_to_all(table, SHARD, split_axis=0, concat_axis=0, tiled=True), axis=0
    )
    return (
        block_output,
        tokens_grad,
        table[0],
        qkv_sum[0],
        qkv_sum[1],
        qkv_sum[2],
        table[2],
        table[3],
        output_sum,
        table[1],
        table[4:].T,
        gate_weight_grad,
        up_weight_grad,
        down_weight_grad,
    )


def solution(mesh):
    rows = P((OWNER, SHARD), None)
    line = P((OWNER, SHARD))
    part = P(SHARD)
    wide = P(SHARD, None)
    into = P(OWNER, SHARD, None)
    back = P(OWNER, None, SHARD)
    in_specs = (rows,) * 3 + (part, wide, wide, wide, part, part, wide, part, wide)
    in_specs = in_specs + (into, into, back, rows)
    out_specs = (rows, rows, line, rows, rows, rows, line, line, rows, line, rows)
    out_specs = out_specs + (into, into, back)

    return jax.shard_map(local, mesh=mesh, in_specs=in_specs, out_specs=out_specs, check_vma=False)
```

```python
import functools

import jax
import jax.numpy as jnp
from jax import lax
from jax.experimental import pallas as pl
from jax.experimental.pallas import tpu as pltpu
from jax.sharding import PartitionSpec as P


HEADS = 16
HEAD_DIM = 128
EXP_DEV = 2
OWNER = "expert"
SHARD = "wshard"


epsilon = 1e-05
theta_base = 10000.0


def rms_unit(activation):
    inverse = lax.rsqrt(jnp.mean(activation * activation, axis=-1, keepdims=True) + epsilon)
    return (activation * inverse, inverse)


def rms_backward(grad_out, normed, inverse, gain):
    gain_grad = jnp.sum(grad_out * normed, axis=0)
    grad_normed = grad_out * gain
    centred = grad_normed - normed * jnp.mean(grad_normed * normed, axis=-1, keepdims=True)
    return (inverse * centred, gain_grad)


def block_tables(lengths, rows):
    ends = jnp.cumsum(lengths, axis=1)
    row_index = jnp.arange(rows, dtype=jnp.int32)
    passed = (row_index[None, :, None] >= ends[:, None, :]).astype(jnp.int32)
    start = jnp.sum(passed * lengths[:, None, :], axis=2)
    allowed = (row_index[None, None, :] <= row_index[None, :, None]) & (
        row_index[None, None, :] >= start[:, :, None]
    )
    offsets = (row_index[None, :] - start).reshape(-1)
    half_dim = HEAD_DIM // 2
    frequency = theta_base ** (-2.0 * jnp.arange(half_dim, dtype=jnp.float32) / HEAD_DIM)
    angles = offsets.astype(jnp.float32)[:, None] * frequency[None, :]
    return (allowed, jnp.cos(angles), jnp.sin(angles))


def rotate(rows, cosine, sine):
    half_dim = HEAD_DIM // 2
    first = rows[..., :half_dim]
    second = rows[..., half_dim:]
    cosine = cosine[None, :, :]
    sine = sine[None, :, :]
    return jnp.concatenate([first * cosine - second * sine, second * cosine + first * sine], axis=-1)


def softmax_rows(logits):
    row_max = jnp.max(logits, axis=-1, keepdims=True)
    shifted = jnp.exp(logits - row_max)
    return shifted / jnp.sum(shifted, axis=-1, keepdims=True)


def dot(a, b):
    return jnp.dot(a, b, preferred_element_type=jnp.float32)


def dot_t(a, b):
    return lax.dot_general(a, b, (((1,), (1,)), ((), ())), preferred_element_type=jnp.float32)


def t_dot(a, b):
    return lax.dot_general(a, b, (((0,), (0,)), ((), ())), preferred_element_type=jnp.float32)


def swap(values, mask, axis_name=SHARD):
    count = lax.axis_size(axis_name)
    return lax.ppermute(values, axis_name, [(i, i ^ mask) for i in range(count)])


def after(values, *others):
    return lax.optimization_barrier((values, *others))[0]


def bits_of(count):
    return [1 << k for k in range(count.bit_length() - 1)]


def gather_far(shard):
    pieces = {0: shard}
    for bit in reversed(bits_of(lax.axis_size(SHARD))[1:]):
        for mask in list(pieces):
            pieces[mask ^ bit] = swap(pieces[mask], bit)
    return pieces


def gather_near(pieces):
    pieces = dict(pieces)
    for mask in list(pieces):
        pieces[mask ^ 1] = swap(pieces[mask], 1)
    return [pieces[mask] for mask in sorted(pieces)]


def gather_pieces(shard):
    return gather_near(gather_far(shard))


def scatter_stage(blocks, bit):
    masks = sorted(blocks, reverse=True)
    arrived = {m ^ bit: swap(blocks[m].astype(jnp.bfloat16), bit) for m in masks if m & bit}
    return {m: blocks[m] + arrived[m].astype(jnp.float32) for m in arrived}


def scatter_near(blocks):
    return scatter_stage(dict(enumerate(blocks)), 1)


def scatter_far(blocks):
    for bit in bits_of(lax.axis_size(SHARD))[1:]:
        blocks = scatter_stage(blocks, bit)
    return blocks[0]


def scatter_pieces(blocks):
    return scatter_far(scatter_near(blocks))


def block_of(array, index, count, axis):
    size = array.shape[axis] // count
    return lax.dynamic_slice_in_dim(array, index * size, size, axis)


def mixed_order(array, w_index, count):
    return jnp.concatenate(
        [block_of(array, w_index ^ mask, count, array.ndim - 1) for mask in range(count)], axis=-1
    )


def pair_dot(a, b, a_axis, b_axis):
    dims = (((a_axis,), (b_axis,)), ((0, 1), (0, 1)))
    return lax.dot_general(a, b, dims, preferred_element_type=jnp.float32)


def group_sum(values):
    count = lax.axis_size(SHARD)
    blocks = values.reshape(values.shape[0], count, -1)
    total = blocks
    for mask in reversed(range(1, count)):
        arrived = swap(blocks, mask)
        total = total + jnp.stack([arrived[:, m ^ mask] for m in range(count)], axis=1)
    return total.reshape(values.shape)


def owner_scatter(values):
    owners = lax.axis_size(OWNER)
    index = lax.axis_index(OWNER)
    if owners > 8:
        return lax.psum_scatter(values, OWNER, scatter_dimension=0, tiled=True)[0]
    pairs = values.reshape(owners // 2, 2, *values.shape[1:])
    away = lax.dynamic_index_in_dim(pairs, 1 - index % 2, 1, keepdims=False)
    kept = lax.dynamic_index_in_dim(pairs, index % 2, 1, keepdims=False)
    arrived = swap(away, 1, OWNER)
    near = (kept.astype(jnp.float32) + arrived.astype(jnp.float32)).astype(jnp.bfloat16)
    total = 0.0
    for mask in reversed(range(owners // 2)):
        part = lax.dynamic_index_in_dim(near, (index // 2) ^ mask, 0, keepdims=False)
        if mask:
            part = swap(part, 2 * mask, OWNER)
        total = total + part.astype(jnp.float32)
    return total.astype(jnp.bfloat16)


def place_kernel(values_ref, out_ref):
    parts, _, cols = values_ref.shape
    for p in range(parts):
        out_ref[:, p * cols : (p + 1) * cols] = values_ref[p].astype(jnp.float32)


def place(values):
    parts, rows, cols = values.shape
    shape = jax.ShapeDtypeStruct((rows, parts * cols), jnp.float32)
    return pl.pallas_call(place_kernel, out_shape=shape)(values)


def expert_hidden_kernel(parts, x_ref, cot_ref, weight_ref, *refs):
    gates, ups, downs = refs[:parts], refs[parts : 2 * parts], refs[2 * parts : 3 * parts]
    hidden_ref, gate_grad_ref, up_grad_ref, route_ref = refs[3 * parts :]
    cols = gates[0].shape[0]
    f32 = jnp.float32
    gate_lin = up_lin = back = 0.0
    for m in range(parts):
        x = x_ref[:, m * cols : (m + 1) * cols]
        gate_lin = gate_lin + jnp.dot(x, gates[m][...], preferred_element_type=f32)
        up_lin = up_lin + jnp.dot(x, ups[m][...], preferred_element_type=f32)
        back = back + dot_t(cot_ref[:, m * cols : (m + 1) * cols], downs[m][...])
    weight = weight_ref[...]
    sigmoid = jax.nn.sigmoid(gate_lin)
    swish = gate_lin * sigmoid
    hidden = swish * up_lin
    product = hidden * back
    route = product[:, :128]
    for k in range(1, product.shape[1] // 128):
        route = route + product[:, k * 128 : (k + 1) * 128]
    hidden_ref[...] = (hidden * weight).astype(jnp.bfloat16)
    grad = back * weight
    gate_grad_ref[...] = (grad * up_lin * sigmoid * (1.0 + gate_lin * (1.0 - sigmoid))).astype(
        jnp.bfloat16
    )
    up_grad_ref[...] = (grad * swish).astype(jnp.bfloat16)

    @pl.when(pl.program_id(2) == 0)
    def _():
        route_ref[...] = route

    @pl.when(pl.program_id(2) > 0)
    def _():
        route_ref[...] += route


def row_tile_of(rows):
    return min(rows, 1024)


def expert_hidden(x, cot, weights, gates, ups, downs, tile=256):
    rows, width = x.shape
    parts = len(gates)
    count, cols, ff = gates[0].shape
    row_tile = row_tile_of(rows)
    steps = ff // tile
    row_spec = pl.BlockSpec((row_tile, width), lambda r, e, f: (r, 0))
    in_piece = pl.BlockSpec((None, cols, tile), lambda r, e, f: (e, 0, f))
    out_piece = pl.BlockSpec((None, tile, cols), lambda r, e, f: (e, f, 0))
    wide_spec = pl.BlockSpec((row_tile, tile), lambda r, e, f: (r, e * steps + f))
    wide = jax.ShapeDtypeStruct((rows, count * ff), jnp.bfloat16)
    return pl.pallas_call(
functools.partial(expert_hidden_kernel, parts),
grid=(rows // row_tile, count, steps),
in_specs=[row_spec, row_spec, pl.BlockSpec((None, row_tile, 1), lambda r, e, f: (e, r, 0))]
+ [in_piece] * (2 * parts)
+ [out_piece] * parts,
out_specs=[wide_spec] * 3
+ [pl.BlockSpec((None, row_tile, 128), lambda r, e, f: (e, r, 0))],
out_shape=[wide] * 3 + [jax.ShapeDtypeStruct((count, rows, 128), jnp.float32)],
compiler_params=pltpu.CompilerParams(vmem_limit_bytes=60 * 1024 * 1024),
    )(x, cot, weights, *gates, *ups, *downs)


def back_rows_kernel(parts, gate_grad_ref, up_grad_ref, *refs):
    gates, ups = refs[:parts], refs[parts : 2 * parts]
    out_ref, sum_ref = refs[2 * parts :]
    cols = gates[0].shape[0]
    step = pl.program_id(1) * pl.num_programs(2) + pl.program_id(2)
    last = pl.num_programs(1) * pl.num_programs(2) - 1
    for m in range(parts):
        at = slice(m * cols, (m + 1) * cols)
        part = dot_t(gate_grad_ref[...], gates[m][...]) + dot_t(up_grad_ref[...], ups[m][...])

        @pl.when(step == 0)
        def _():
            sum_ref[:, at] = part

        @pl.when((step > 0) & (step < last))
        def _():
            sum_ref[:, at] += part

        @pl.when(step == last)
        def _():
            out_ref[:, at] = (sum_ref[:, at] + part).astype(jnp.bfloat16)


def back_rows(gate_grad, up_grad, gates, ups, tile=512):
    rows = gate_grad.shape[0]
    parts = len(gates)
    count, cols, ff = gates[0].shape
    row_tile = row_tile_of(rows)
    steps = ff // tile
    wide_spec = pl.BlockSpec((row_tile, tile), lambda r, e, f: (r, e * steps + f))
    piece = pl.BlockSpec((None, cols, tile), lambda r, e, f: (e, 0, f))
    return pl.pallas_call(
functools.partial(back_rows_kernel, parts),
grid=(rows // row_tile, count, steps),
in_specs=[wide_spec] * 2 + [piece] * (2 * parts),
out_specs=pl.BlockSpec((row_tile, parts * cols), lambda r, e, f: (r, 0)),
out_shape=jax.ShapeDtypeStruct((rows, parts * cols), jnp.bfloat16),
scratch_shapes=[pltpu.VMEM((row_tile, parts * cols), jnp.float32)],
compiler_params=pltpu.CompilerParams(vmem_limit_bytes=60 * 1024 * 1024),
    )(gate_grad, up_grad, *gates, *ups)


def local(
    tokens,
    doc_lengths,
    expert_ids,
    attn_gain,
    query_weight,
    key_weight,
    value_weight,
    query_gain,
    key_gain,
    output_weight,
    ffn_gain,
    router_weight,
    gate_weight,
    up_weight,
    down_weight,
    cotangent,
):
    bf16 = jnp.bfloat16
    f32 = jnp.float32
    rows, width = tokens.shape
    owners = lax.axis_size(OWNER)
    parts = lax.axis_size(SHARD)
    w_index = lax.axis_index(SHARD)
    experts = EXP_DEV * owners
    group = parts * rows
    cols = width // parts
    heads = HEADS // parts
    final_rows = width // (owners * parts)
    ff = gate_weight.shape[2]

    e_index = lax.axis_index(OWNER)
    half = cols // 2
    unit = 2 * w_index + e_index % 2
    units = 2 * parts

    docs = doc_lengths.shape[1]
    lengths_row = jnp.zeros((1, cols), bf16).at[:, :docs].set(doc_lengths.astype(bf16))
    small = jnp.concatenate(
        [attn_gain[None, :], ffn_gain[None, :], lengths_row, router_weight.T], axis=0
    )
    small_all = lax.all_gather(small, SHARD, axis=0)
    attn_gain_all = small_all[:, 0, :].reshape(width).astype(f32)
    ffn_gain_all = small_all[:, 1, :].reshape(width).astype(f32)
    lengths_all = small_all[:, 2, :docs].astype(jnp.int32)
    lengths_all = jnp.concatenate([block_of(lengths_all, w_index ^ m, parts, 0) for m in range(parts)])
    router_t = small_all[:, 3:, :].transpose(1, 0, 2).reshape(experts, width)

    *weights_in, tokens_in, _ = lax.optimization_barrier(
        (query_weight, key_weight, value_weight, tokens, small_all)
    )
    tokens_far = gather_far(tokens_in)
    tokens_all = jnp.concatenate(gather_near(tokens_far), axis=0)
    pieces = [None] * units
    for mask in reversed(range(parts)):
        piece = jnp.concatenate(
            [block_of(weight, w_index ^ mask, parts, 1) for weight in weights_in], axis=1
        )
        for side in range(2):
            pieces[2 * mask + side] = block_of(piece, side ^ (e_index % 2), 2, 0)
    for mask in reversed(range(1, parts)):
        pieces[2 * mask] = swap(pieces[2 * mask], mask)
        if mask == 1:
            pieces[3] = swap(pieces[3], 1)
    for mask in reversed(range(2, parts)):
        pieces[2 * mask + 1] = swap(pieces[2 * mask], 1, OWNER)
    cot_b = mixed_order(cotangent, w_index, parts).astype(bf16)
    cot_b = after(cot_b, *pieces[5:])
    cot_all = lax.all_gather(cot_b, OWNER, axis=0, tiled=True)
    down_in = after(down_weight, pieces[4])
    down_pieces = gather_far(down_in)

    unit_all, _ = rms_unit(tokens_all.astype(f32))
    attn_in = (unit_all * attn_gain_all).astype(bf16)
    attn_in_mixed = mixed_order(attn_in, unit, units)
    qkv = 0.0
    for at in [0, 1, 2, 3] + [2 * m for m in range(2, parts)] + [2 * m + 1 for m in range(2, parts)]:
        qkv = qkv + dot(attn_in_mixed[:, at * half : (at + 1) * half], pieces[at])
    query_lin, key_lin, value_lin = (qkv[:, i * cols : (i + 1) * cols] for i in range(3))
    squares = jnp.stack(
        [jnp.sum(query_lin * query_lin, axis=1), jnp.sum(key_lin * key_lin, axis=1)], axis=0
    )
    squares = group_sum(squares)
    inverses = lax.rsqrt(squares / width + epsilon)
    query_inverse = inverses[0][:, None]
    key_inverse = inverses[1][:, None]
    query_unit = query_lin * query_inverse
    key_unit = key_lin * key_inverse
    query_gain_f = query_gain.astype(f32)
    key_gain_f = key_gain.astype(f32)
    allowed, cosine, sine = block_tables(lengths_all, rows)
    scale = HEAD_DIM ** (-0.5)

    def by_head(array):
        return jnp.stack(
            [array[:, h * HEAD_DIM : (h + 1) * HEAD_DIM] for h in range(heads)], axis=0
        )

    def by_row(array):
        return jnp.concatenate([array[h] for h in range(heads)], axis=1)

    blocked = (heads, parts, rows, HEAD_DIM)
    whole = (heads, group, HEAD_DIM)
    queries = rotate(by_head(query_unit * query_gain_f), cosine, sine).astype(bf16)
    queries = queries.reshape(blocked)
    keys = rotate(by_head(key_unit * key_gain_f), cosine, sine).astype(bf16).reshape(blocked)
    values = by_head(value_lin).astype(bf16).reshape(blocked)
    scores = pair_dot(queries, keys, 3, 3)
    scores = scores * scale
    scores = jnp.where(allowed[None, :, :, :], scores, -1e30)
    row_max = jnp.max(scores, axis=-1, keepdims=True)
    log_total = row_max + jnp.log(jnp.sum(jnp.exp(scores - row_max), axis=-1, keepdims=True))
    probs = jnp.exp(scores - log_total)
    probs_b = probs.astype(bf16)
    mixed = pair_dot(probs_b, values, 3, 2).astype(bf16)
    attn_mix = by_row(mixed.reshape(whole))
    attn_out = dot(attn_mix, output_weight)
    attn_out = scatter_pieces([attn_out[mask * rows : (mask + 1) * rows] for mask in range(parts)])
    attn_out, down_pieces, *pieces = lax.optimization_barrier((attn_out, down_pieces, *pieces))
    down_pieces = gather_near(down_pieces)
    qkv_w = jnp.concatenate(pieces, axis=0)
    qkv_w = jnp.concatenate(
        [block_of(qkv_w, unit ^ k, units, 0) for k in range(units)], axis=0
    )

    residual = tokens.astype(f32)
    middle = residual + attn_out
    unit_two, inverse_two = rms_unit(middle)
    ffn_in = (unit_two * ffn_gain_all).astype(bf16)
    ffn_in_mixed = mixed_order(ffn_in, w_index, parts)
    gate_in, up_in, ffn_in_mixed, ffn_in = lax.optimization_barrier(
        (gate_weight, up_weight, ffn_in_mixed, ffn_in)
    )
    gate_far = gather_far(gate_in)
    gate_pieces = gather_near(gate_far)
    up_pieces = gather_pieces(up_in)
    router_probs = softmax_rows(dot_t(ffn_in, router_t))
    expert_range = jnp.arange(experts, dtype=jnp.int32)
    named = jnp.any(expert_ids[:, :, None] == expert_range[None, None, :], axis=1)
    route_table = jnp.where(named, router_probs, 0.0)

    arrived = lax.all_gather(ffn_in_mixed, OWNER, axis=0, tiled=True)
    weights = lax.all_to_all(
        route_table.reshape(rows, owners, EXP_DEV).transpose(1, 2, 0),
        OWNER,
        split_axis=0,
        concat_axis=0,
        tiled=True,
    )
    weights = weights.transpose(1, 0, 2).reshape(EXP_DEV, owners * rows, 1)
    hidden_w, gate_grad_b, up_grad_b, route_part = expert_hidden(
        arrived, cot_all, weights, gate_pieces, up_pieces, down_pieces
    )
    row_grads = []
    for at in (0, parts // 2):
        chosen = slice(at, at + parts // 2)
        row_partial = back_rows(gate_grad_b, up_grad_b, gate_pieces[chosen], up_pieces[chosen])
        row_grads.append(owner_scatter(row_partial.reshape(owners, rows, width // 2)))
    row_grads = jnp.concatenate(row_grads, axis=1)
    gate_grad_b, up_grad_b, _ = lax.optimization_barrier((gate_grad_b, up_grad_b, row_partial))
    route_back = jnp.sum(route_part, axis=2)
    route_back = lax.all_to_all(
        route_back.reshape(EXP_DEV, owners, rows).transpose(1, 0, 2),
        OWNER,
        split_axis=0,
        concat_axis=0,
        tiled=True,
    )
    part_of = lambda array, mask: array[:, mask * cols : (mask + 1) * cols]
    order = sorted(range(parts), key=lambda m: (m < parts // 2, -m))

    def ordered_blocks(make):
        blocks = [None] * parts
        for mask in order:
            blocks[mask] = make(mask)
        return blocks

    gate_blocks = ordered_blocks(lambda m: t_dot(part_of(arrived, m), gate_grad_b))
    gate_near = scatter_near(gate_blocks)
    up_blocks = ordered_blocks(lambda m: t_dot(part_of(arrived, m), up_grad_b))
    up_near = scatter_near(up_blocks)
    hidden_w, qkv_w, *_ = lax.optimization_barrier((hidden_w, qkv_w, *gate_blocks, *up_blocks))
    down_blocks = ordered_blocks(lambda m: t_dot(hidden_w, part_of(cot_all, m)))
    down_near = scatter_near(down_blocks)
    gate_sum = scatter_far(gate_near)
    gate_weight_grad = jnp.stack([gate_sum[:, e * ff : (e + 1) * ff] for e in range(EXP_DEV)])
    down_all = jnp.concatenate(
        [piece.reshape(EXP_DEV * ff, cols) for piece in down_pieces], axis=1
    )
    out_partial = dot(hidden_w, down_all).astype(bf16)
    moe_out = lax.psum_scatter(out_partial, OWNER, scatter_dimension=0, tiled=True)
    row_grads, route_back = lax.optimization_barrier((row_grads, route_back))

    route_grad = route_back.reshape(experts, rows).T
    prob_grad = jnp.where(named, route_grad, 0.0)
    logit_grad = router_probs * (
        prob_grad - jnp.sum(router_probs * prob_grad, axis=1, keepdims=True)
    )
    logit_grad_b = logit_grad.astype(bf16)
    ffn_in_grad = mixed_order(row_grads, w_index, parts).astype(f32) + dot(logit_grad_b, router_t)
    middle_part, ffn_gain_grad = rms_backward(ffn_in_grad, unit_two, inverse_two, ffn_gain_all)
    middle_grad = cotangent + middle_part
    router_grad = t_dot(logit_grad_b, ffn_in)

    mid_pieces = gather_pieces(middle_grad.astype(bf16))
    mid_all = jnp.concatenate(mid_pieces, axis=0)
    output_part = t_dot(attn_mix, mid_all).astype(bf16)
    output_sum = owner_scatter(output_part.reshape(owners, final_rows, width))
    mix_grad = by_head(dot_t(mid_all, output_weight).astype(bf16)).reshape(blocked)
    delta = jnp.sum(mix_grad.astype(f32) * mixed.astype(f32), axis=-1, keepdims=True)
    prob_back = pair_dot(mix_grad, values, 3, 3)
    score_grad = (probs * (prob_back - delta)).astype(bf16)
    grad_queries = pair_dot(score_grad, keys, 3, 2)
    grad_keys = pair_dot(score_grad, queries, 2, 2)
    grad_values = pair_dot(probs_b, mix_grad, 2, 2)
    grad_queries = by_row(rotate((grad_queries * scale).reshape(whole), cosine, -sine))
    grad_keys = by_row(rotate((grad_keys * scale).reshape(whole), cosine, -sine))
    query_gain_grad = jnp.sum(grad_queries * query_unit, axis=0)
    key_gain_grad = jnp.sum(grad_keys * key_unit, axis=0)
    grad_queries = grad_queries * query_gain_f
    grad_keys = grad_keys * key_gain_f
    means = jnp.stack(
        [jnp.sum(grad_queries * query_unit, axis=1), jnp.sum(grad_keys * key_unit, axis=1)], axis=0
    )
    means = group_sum(means) / width
    up_sum = scatter_far(up_near)
    up_weight_grad = jnp.stack([up_sum[:, e * ff : (e + 1) * ff] for e in range(EXP_DEV)])
    query_grad_b = (query_inverse * (grad_queries - query_unit * means[0][:, None])).astype(bf16)
    key_grad_b = (key_inverse * (grad_keys - key_unit * means[1][:, None])).astype(bf16)
    value_grad_b = by_row(grad_values.reshape(whole)).astype(bf16)
    qkv_grad = jnp.concatenate([query_grad_b, key_grad_b, value_grad_b], axis=1)
    attn_in_part = dot_t(qkv_grad, qkv_w)
    attn_in_grad = scatter_pieces(
        [attn_in_part[mask * rows : (mask + 1) * rows] for mask in range(parts)]
    )
    placed = []
    for grad in (value_grad_b, query_grad_b, key_grad_b):
        part = t_dot(attn_in, grad)
        part = part.astype(bf16).reshape(owners, parts * final_rows, cols)
        total = owner_scatter(part).reshape(parts, final_rows, cols)
        total = lax.all_to_all(total, SHARD, split_axis=0, concat_axis=0, tiled=True)
        placed.append(place(total))
    down_weight_grad = scatter_far(after(down_near, attn_in_part)).reshape(EXP_DEV, ff, cols)

    unit_one, inverse_one = rms_unit(residual)
    input_part, attn_gain_grad = rms_backward(
        attn_in_grad, unit_one, inverse_one, attn_gain_all
    )
    tokens_grad = middle_grad + input_part
    moe_out = after(moe_out, attn_in_part)
    block_output = middle + mixed_order(moe_out, w_index, parts).astype(f32)

    moves = []
    for e in range(owners):
        for w in range(parts):
            moves.append((e * parts + w, w * owners + e))
    output_sum = lax.ppermute(output_sum, (OWNER, SHARD), moves).astype(f32)

    own = jnp.zeros((2, parts, cols), f32)
    own = lax.dynamic_update_slice(
        own, jnp.stack([query_gain_grad, key_gain_grad])[:, None, :], (0, w_index, 0)
    ).reshape(2, width)
    table = jnp.concatenate([attn_gain_grad[None], ffn_gain_grad[None], own, router_grad], axis=0)
    count = table.shape[0]
    table = table.reshape(count, owners, parts * final_rows).transpose(1, 0, 2)
    table = lax.all_to_all(table, OWNER, split_axis=0, concat_axis=0, tiled=True)
    table = jnp.sum(table, axis=0)
    table = table.reshape(count, parts, final_rows).transpose(1, 0, 2)
    table = jnp.sum(
        lax.all_to_all(table, SHARD, split_axis=0, concat_axis=0, tiled=True), axis=0
    )
    return (
        block_output,
        tokens_grad,
        table[0],
        placed[1],
        placed[2],
        placed[0],
        table[2],
        table[3],
        output_sum,
        table[1],
        table[4:].T,
        gate_weight_grad,
        up_weight_grad,
        down_weight_grad,
    )


def solution(mesh):
    rows = P((OWNER, SHARD), None)
    line = P((OWNER, SHARD))
    part = P(SHARD)
    wide = P(SHARD, None)
    into = P(OWNER, SHARD, None)
    back = P(OWNER, None, SHARD)
    in_specs = (rows,) * 3 + (part, wide, wide, wide, part, part, wide, part, wide)
    in_specs = in_specs + (into, into, back, rows)
    out_specs = (rows, rows, line, rows, rows, rows, line, line, rows, line, rows)
    out_specs = out_specs + (into, into, back)

    return jax.shard_map(local, mesh=mesh, in_specs=in_specs, out_specs=out_specs, check_vma=False)
```

```python
import functools

import jax
import jax.numpy as jnp
from jax import lax
from jax.experimental import pallas as pl
from jax.experimental.pallas import tpu as pltpu
from jax.sharding import PartitionSpec as P


HEADS = 16
HEAD_DIM = 128
EXP_DEV = 2
OWNER = "expert"
SHARD = "wshard"


epsilon = 1e-05
theta_base = 10000.0


def rms_unit(activation):
    inverse = lax.rsqrt(jnp.mean(activation * activation, axis=-1, keepdims=True) + epsilon)
    return (activation * inverse, inverse)


def rms_backward(grad_out, normed, inverse, gain):
    gain_grad = jnp.sum(grad_out * normed, axis=0)
    grad_normed = grad_out * gain
    centred = grad_normed - normed * jnp.mean(grad_normed * normed, axis=-1, keepdims=True)
    return (inverse * centred, gain_grad)


def block_tables(lengths, rows):
    ends = jnp.cumsum(lengths, axis=1)
    row_index = jnp.arange(rows, dtype=jnp.int32)
    passed = (row_index[None, :, None] >= ends[:, None, :]).astype(jnp.int32)
    start = jnp.sum(passed * lengths[:, None, :], axis=2)
    allowed = (row_index[None, None, :] <= row_index[None, :, None]) & (
        row_index[None, None, :] >= start[:, :, None]
    )
    offsets = (row_index[None, :] - start).reshape(-1)
    half_dim = HEAD_DIM // 2
    frequency = theta_base ** (-2.0 * jnp.arange(half_dim, dtype=jnp.float32) / HEAD_DIM)
    angles = offsets.astype(jnp.float32)[:, None] * frequency[None, :]
    return (allowed, jnp.cos(angles), jnp.sin(angles))


def rotate(rows, cosine, sine):
    half_dim = HEAD_DIM // 2
    first = rows[..., :half_dim]
    second = rows[..., half_dim:]
    cosine = cosine[None, :, :]
    sine = sine[None, :, :]
    return jnp.concatenate([first * cosine - second * sine, second * cosine + first * sine], axis=-1)


def softmax_rows(logits):
    row_max = jnp.max(logits, axis=-1, keepdims=True)
    shifted = jnp.exp(logits - row_max)
    return shifted / jnp.sum(shifted, axis=-1, keepdims=True)


def dot(a, b):
    return jnp.dot(a, b, preferred_element_type=jnp.float32)


def dot_t(a, b):
    return lax.dot_general(a, b, (((1,), (1,)), ((), ())), preferred_element_type=jnp.float32)


def t_dot(a, b):
    return lax.dot_general(a, b, (((0,), (0,)), ((), ())), preferred_element_type=jnp.float32)


def swap(values, mask, axis_name=SHARD):
    count = lax.axis_size(axis_name)
    return lax.ppermute(values, axis_name, [(i, i ^ mask) for i in range(count)])


def after(values, *others):
    return lax.optimization_barrier((values, *others))[0]


def bits_of(count):
    return [1 << k for k in range(count.bit_length() - 1)]


def gather_far(shard):
    pieces = {0: shard}
    for bit in reversed(bits_of(lax.axis_size(SHARD))[1:]):
        for mask in list(pieces):
            pieces[mask ^ bit] = swap(pieces[mask], bit)
    return pieces


def gather_near(pieces):
    pieces = dict(pieces)
    for mask in list(pieces):
        pieces[mask ^ 1] = swap(pieces[mask], 1)
    return [pieces[mask] for mask in sorted(pieces)]


def gather_pieces(shard):
    return gather_near(gather_far(shard))


def scatter_stage(blocks, bit):
    masks = sorted(blocks, reverse=True)
    arrived = {m ^ bit: swap(blocks[m].astype(jnp.bfloat16), bit) for m in masks if m & bit}
    return {m: blocks[m] + arrived[m].astype(jnp.float32) for m in arrived}


def scatter_near(blocks):
    return scatter_stage(dict(enumerate(blocks)), 1)


def scatter_far(blocks):
    for bit in bits_of(lax.axis_size(SHARD))[1:]:
        blocks = scatter_stage(blocks, bit)
    return blocks[0]


def scatter_pieces(blocks):
    return scatter_far(scatter_near(blocks))


def block_of(array, index, count, axis):
    size = array.shape[axis] // count
    return lax.dynamic_slice_in_dim(array, index * size, size, axis)


def mixed_order(array, w_index, count):
    return jnp.concatenate(
        [block_of(array, w_index ^ mask, count, array.ndim - 1) for mask in range(count)], axis=-1
    )


def pair_dot(a, b, a_axis, b_axis):
    dims = (((a_axis,), (b_axis,)), ((0, 1), (0, 1)))
    return lax.dot_general(a, b, dims, preferred_element_type=jnp.float32)


def group_sum(values):
    count = lax.axis_size(SHARD)
    blocks = values.reshape(values.shape[0], count, -1)
    total = blocks
    for mask in reversed(range(1, count)):
        arrived = swap(blocks, mask)
        total = total + jnp.stack([arrived[:, m ^ mask] for m in range(count)], axis=1)
    return total.reshape(values.shape)


def owner_scatter(values):
    owners = lax.axis_size(OWNER)
    index = lax.axis_index(OWNER)
    if owners > 8:
        return lax.psum_scatter(values, OWNER, scatter_dimension=0, tiled=True)[0]
    pairs = values.reshape(owners // 2, 2, *values.shape[1:])
    away = lax.dynamic_index_in_dim(pairs, 1 - index % 2, 1, keepdims=False)
    kept = lax.dynamic_index_in_dim(pairs, index % 2, 1, keepdims=False)
    arrived = swap(away, 1, OWNER)
    near = (kept.astype(jnp.float32) + arrived.astype(jnp.float32)).astype(jnp.bfloat16)
    total = 0.0
    for mask in reversed(range(owners // 2)):
        part = lax.dynamic_index_in_dim(near, (index // 2) ^ mask, 0, keepdims=False)
        if mask:
            part = swap(part, 2 * mask, OWNER)
        total = total + part.astype(jnp.float32)
    return total.astype(jnp.bfloat16)


def place_kernel(heads_ref, values_ref, query_ref, key_ref, value_ref):
    parts, _, cols = values_ref.shape
    for p in range(parts):
        at = slice(p * cols, (p + 1) * cols)
        query_ref[:, at] = heads_ref[p, :, :cols].astype(jnp.float32)
        key_ref[:, at] = heads_ref[p, :, cols:].astype(jnp.float32)
        value_ref[:, at] = values_ref[p].astype(jnp.float32)


def place(heads, values):
    parts, rows, cols = values.shape
    shape = jax.ShapeDtypeStruct((rows, parts * cols), jnp.float32)
    return pl.pallas_call(place_kernel, out_shape=[shape] * 3)(heads, values)


def expert_hidden_kernel(parts, x_ref, cot_ref, weight_ref, *refs):
    gates, ups, downs = refs[:parts], refs[parts : 2 * parts], refs[2 * parts : 3 * parts]
    hidden_ref, gate_grad_ref, up_grad_ref, route_ref = refs[3 * parts :]
    cols = gates[0].shape[0]
    f32 = jnp.float32
    gate_lin = up_lin = back = 0.0
    for m in range(parts):
        x = x_ref[:, m * cols : (m + 1) * cols]
        gate_lin = gate_lin + jnp.dot(x, gates[m][...], preferred_element_type=f32)
        up_lin = up_lin + jnp.dot(x, ups[m][...], preferred_element_type=f32)
        back = back + dot_t(cot_ref[:, m * cols : (m + 1) * cols], downs[m][...])
    weight = weight_ref[...]
    sigmoid = jax.nn.sigmoid(gate_lin)
    swish = gate_lin * sigmoid
    hidden = swish * up_lin
    product = hidden * back
    route = product[:, :128]
    for k in range(1, product.shape[1] // 128):
        route = route + product[:, k * 128 : (k + 1) * 128]
    hidden_ref[...] = (hidden * weight).astype(jnp.bfloat16)
    grad = back * weight
    gate_grad_ref[...] = (grad * up_lin * sigmoid * (1.0 + gate_lin * (1.0 - sigmoid))).astype(
        jnp.bfloat16
    )
    up_grad_ref[...] = (grad * swish).astype(jnp.bfloat16)

    @pl.when(pl.program_id(2) == 0)
    def _():
        route_ref[...] = route

    @pl.when(pl.program_id(2) > 0)
    def _():
        route_ref[...] += route


def row_tile_of(rows):
    return min(rows, 1024)


def expert_hidden(x, cot, weights, gates, ups, downs, tile=256):
    rows, width = x.shape
    parts = len(gates)
    count, cols, ff = gates[0].shape
    row_tile = row_tile_of(rows)
    steps = ff // tile
    row_spec = pl.BlockSpec((row_tile, width), lambda r, e, f: (r, 0))
    in_piece = pl.BlockSpec((None, cols, tile), lambda r, e, f: (e, 0, f))
    out_piece = pl.BlockSpec((None, tile, cols), lambda r, e, f: (e, f, 0))
    wide_spec = pl.BlockSpec((row_tile, tile), lambda r, e, f: (r, e * steps + f))
    wide = jax.ShapeDtypeStruct((rows, count * ff), jnp.bfloat16)
    return pl.pallas_call(
functools.partial(expert_hidden_kernel, parts),
grid=(rows // row_tile, count, steps),
in_specs=[row_spec, row_spec, pl.BlockSpec((None, row_tile, 1), lambda r, e, f: (e, r, 0))]
+ [in_piece] * (2 * parts)
+ [out_piece] * parts,
out_specs=[wide_spec] * 3
+ [pl.BlockSpec((None, row_tile, 128), lambda r, e, f: (e, r, 0))],
out_shape=[wide] * 3 + [jax.ShapeDtypeStruct((count, rows, 128), jnp.float32)],
compiler_params=pltpu.CompilerParams(vmem_limit_bytes=60 * 1024 * 1024),
    )(x, cot, weights, *gates, *ups, *downs)


def back_rows_kernel(parts, gate_grad_ref, up_grad_ref, *refs):
    gates, ups = refs[:parts], refs[parts : 2 * parts]
    out_ref, sum_ref = refs[2 * parts :]
    cols = gates[0].shape[0]
    step = pl.program_id(1) * pl.num_programs(2) + pl.program_id(2)
    last = pl.num_programs(1) * pl.num_programs(2) - 1
    for m in range(parts):
        at = slice(m * cols, (m + 1) * cols)
        part = dot_t(gate_grad_ref[...], gates[m][...]) + dot_t(up_grad_ref[...], ups[m][...])

        @pl.when(step == 0)
        def _():
            sum_ref[:, at] = part

        @pl.when((step > 0) & (step < last))
        def _():
            sum_ref[:, at] += part

        @pl.when(step == last)
        def _():
            out_ref[:, at] = (sum_ref[:, at] + part).astype(jnp.bfloat16)


def back_rows(gate_grad, up_grad, gates, ups, tile=512):
    rows = gate_grad.shape[0]
    parts = len(gates)
    count, cols, ff = gates[0].shape
    row_tile = row_tile_of(rows)
    steps = ff // tile
    wide_spec = pl.BlockSpec((row_tile, tile), lambda r, e, f: (r, e * steps + f))
    piece = pl.BlockSpec((None, cols, tile), lambda r, e, f: (e, 0, f))
    return pl.pallas_call(
functools.partial(back_rows_kernel, parts),
grid=(rows // row_tile, count, steps),
in_specs=[wide_spec] * 2 + [piece] * (2 * parts),
out_specs=pl.BlockSpec((row_tile, parts * cols), lambda r, e, f: (r, 0)),
out_shape=jax.ShapeDtypeStruct((rows, parts * cols), jnp.bfloat16),
scratch_shapes=[pltpu.VMEM((row_tile, parts * cols), jnp.float32)],
compiler_params=pltpu.CompilerParams(vmem_limit_bytes=60 * 1024 * 1024),
    )(gate_grad, up_grad, *gates, *ups)


def local(
    tokens,
    doc_lengths,
    expert_ids,
    attn_gain,
    query_weight,
    key_weight,
    value_weight,
    query_gain,
    key_gain,
    output_weight,
    ffn_gain,
    router_weight,
    gate_weight,
    up_weight,
    down_weight,
    cotangent,
):
    bf16 = jnp.bfloat16
    f32 = jnp.float32
    rows, width = tokens.shape
    owners = lax.axis_size(OWNER)
    parts = lax.axis_size(SHARD)
    w_index = lax.axis_index(SHARD)
    experts = EXP_DEV * owners
    group = parts * rows
    cols = width // parts
    heads = HEADS // parts
    final_rows = width // (owners * parts)
    ff = gate_weight.shape[2]

    e_index = lax.axis_index(OWNER)
    half = cols // 2
    unit = 2 * w_index + e_index % 2
    units = 2 * parts

    docs = doc_lengths.shape[1]
    lengths_row = jnp.zeros((1, cols), bf16).at[:, :docs].set(doc_lengths.astype(bf16))
    small = jnp.concatenate(
        [attn_gain[None, :], ffn_gain[None, :], lengths_row, router_weight.T], axis=0
    )
    small_all = lax.all_gather(small, SHARD, axis=0)
    attn_gain_all = small_all[:, 0, :].reshape(width).astype(f32)
    ffn_gain_all = small_all[:, 1, :].reshape(width).astype(f32)
    lengths_all = small_all[:, 2, :docs].astype(jnp.int32)
    lengths_all = jnp.concatenate([block_of(lengths_all, w_index ^ m, parts, 0) for m in range(parts)])
    router_t = small_all[:, 3:, :].transpose(1, 0, 2).reshape(experts, width)

    *weights_in, tokens_in, _ = lax.optimization_barrier(
        (query_weight, key_weight, value_weight, tokens, small_all)
    )
    tokens_far = gather_far(tokens_in)
    tokens_all = jnp.concatenate(gather_near(tokens_far), axis=0)
    pieces = [None] * units
    for mask in reversed(range(parts)):
        piece = jnp.concatenate(
            [block_of(weight, w_index ^ mask, parts, 1) for weight in weights_in], axis=1
        )
        for side in range(2):
            pieces[2 * mask + side] = block_of(piece, side ^ (e_index % 2), 2, 0)
    for mask in reversed(range(1, parts)):
        pieces[2 * mask] = swap(pieces[2 * mask], mask)
        if mask == 1:
            pieces[3] = swap(pieces[3], 1)
    for mask in reversed(range(2, parts)):
        pieces[2 * mask + 1] = swap(pieces[2 * mask], 1, OWNER)
    cot_b = mixed_order(cotangent, w_index, parts).astype(bf16)
    cot_all = lax.all_gather(cot_b, OWNER, axis=0, tiled=True)
    down_first = after(down_weight[:1], pieces[4])
    down_first = gather_far(down_first)
    down_second = after(down_weight[1:], pieces[4])
    down_second = gather_far(down_second)

    unit_all, _ = rms_unit(tokens_all.astype(f32))
    attn_in = (unit_all * attn_gain_all).astype(bf16)
    attn_in_mixed = mixed_order(attn_in, unit, units)
    qkv = 0.0
    for at in [0, 1, 2, 3] + [2 * m for m in range(2, parts)] + [2 * m + 1 for m in range(2, parts)]:
        qkv = qkv + dot(attn_in_mixed[:, at * half : (at + 1) * half], pieces[at])
    query_lin, key_lin, value_lin = (qkv[:, i * cols : (i + 1) * cols] for i in range(3))
    squares = jnp.stack(
        [jnp.sum(query_lin * query_lin, axis=1), jnp.sum(key_lin * key_lin, axis=1)], axis=0
    )
    squares = group_sum(squares)
    inverses = lax.rsqrt(squares / width + epsilon)
    query_inverse = inverses[0][:, None]
    key_inverse = inverses[1][:, None]
    query_unit = query_lin * query_inverse
    key_unit = key_lin * key_inverse
    query_gain_f = query_gain.astype(f32)
    key_gain_f = key_gain.astype(f32)
    allowed, cosine, sine = block_tables(lengths_all, rows)
    scale = HEAD_DIM ** (-0.5)

    def by_head(array):
        return jnp.stack(
            [array[:, h * HEAD_DIM : (h + 1) * HEAD_DIM] for h in range(heads)], axis=0
        )

    def by_row(array):
        return jnp.concatenate([array[h] for h in range(heads)], axis=1)

    blocked = (heads, parts, rows, HEAD_DIM)
    whole = (heads, group, HEAD_DIM)
    queries = rotate(by_head(query_unit * query_gain_f), cosine, sine).astype(bf16)
    queries = queries.reshape(blocked)
    keys = rotate(by_head(key_unit * key_gain_f), cosine, sine).astype(bf16).reshape(blocked)
    values = by_head(value_lin).astype(bf16).reshape(blocked)
    scores = pair_dot(queries, keys, 3, 3) * scale
    scores = jnp.where(allowed[None, :, :, :], scores, -1e30)
    row_max = jnp.max(scores, axis=-1, keepdims=True)
    log_total = row_max + jnp.log(jnp.sum(jnp.exp(scores - row_max), axis=-1, keepdims=True))
    probs = jnp.exp(scores - log_total)
    probs_b = probs.astype(bf16)
    mixed = pair_dot(probs_b, values, 3, 2).astype(bf16)
    attn_mix = by_row(mixed.reshape(whole))
    attn_out = dot(attn_mix, output_weight)
    attn_out = scatter_pieces([attn_out[mask * rows : (mask + 1) * rows] for mask in range(parts)])
    attn_out, *pieces = lax.optimization_barrier((attn_out, *pieces))
    qkv_w = jnp.concatenate(pieces, axis=0)
    qkv_w = jnp.concatenate(
        [block_of(qkv_w, unit ^ k, units, 0) for k in range(units)], axis=0
    )

    residual = tokens.astype(f32)
    middle = residual + attn_out
    unit_two, inverse_two = rms_unit(middle)
    ffn_in = (unit_two * ffn_gain_all).astype(bf16)
    ffn_in_mixed = mixed_order(ffn_in, w_index, parts)
    gate_in, up_in, ffn_in_mixed, ffn_in = lax.optimization_barrier(
        (gate_weight, up_weight, ffn_in_mixed, ffn_in)
    )
    gate_far = gather_far(gate_in)
    up_far = gather_far(up_in)
    router_probs = softmax_rows(dot_t(ffn_in, router_t))
    expert_range = jnp.arange(experts, dtype=jnp.int32)
    named = jnp.any(expert_ids[:, :, None] == expert_range[None, None, :], axis=1)
    route_table = jnp.where(named, router_probs, 0.0)

    arrived = lax.all_gather(ffn_in_mixed, OWNER, axis=0, tiled=True)
    weights = lax.all_to_all(
        route_table.reshape(rows, owners, EXP_DEV).transpose(1, 2, 0),
        OWNER,
        split_axis=0,
        concat_axis=0,
        tiled=True,
    )
    weights = weights.transpose(1, 0, 2).reshape(EXP_DEV, owners * rows, 1)
    gate_pieces = gather_near(gate_far)
    up_pieces = gather_near(
        {m: after(p, weights, gate_pieces[-1]) if m else p for m, p in up_far.items()}
    )
    down_far = {m: jnp.concatenate([down_first[m], down_second[m]]) for m in down_first if m}
    down_pieces = gather_near({0: down_weight, **down_far})
    hidden_w, gate_grad_b, up_grad_b, route_part = expert_hidden(
        arrived, cot_all, weights, gate_pieces, up_pieces, down_pieces
    )
    row_partial = back_rows(gate_grad_b, up_grad_b, gate_pieces, up_pieces)
    row_grads = lax.psum_scatter(row_partial, OWNER, scatter_dimension=0, tiled=True)
    route_back = jnp.sum(route_part, axis=2)
    route_back = lax.all_to_all(
        route_back.reshape(EXP_DEV, owners, rows).transpose(1, 0, 2),
        OWNER,
        split_axis=0,
        concat_axis=0,
        tiled=True,
    )
    part_of = lambda array, mask: array[:, mask * cols : (mask + 1) * cols]
    order = sorted(range(parts), key=lambda m: (m < parts // 2, -m))

    def ordered_blocks(make):
        blocks = [None] * parts
        for mask in order:
            blocks[mask] = make(mask)
        return blocks

    gate_blocks = ordered_blocks(lambda m: t_dot(part_of(arrived, m), gate_grad_b))
    gate_near = scatter_near(gate_blocks)
    up_blocks = ordered_blocks(lambda m: t_dot(part_of(arrived, m), up_grad_b))
    up_near = scatter_near(up_blocks)
    hidden_w, qkv_w, *_ = lax.optimization_barrier((hidden_w, qkv_w, *gate_blocks, *up_blocks))
    down_blocks = ordered_blocks(lambda m: t_dot(hidden_w, part_of(cot_all, m)))
    down_near = scatter_near(down_blocks)
    gate_sum = scatter_far(gate_near)
    gate_weight_grad = jnp.stack([gate_sum[:, e * ff : (e + 1) * ff] for e in range(EXP_DEV)])
    down_all = jnp.concatenate(
        [piece.reshape(EXP_DEV * ff, cols) for piece in down_pieces], axis=1
    )
    out_partial = dot(hidden_w, down_all).astype(bf16)
    moe_out = owner_scatter(out_partial.reshape(owners, rows, width))
    row_grads, route_back = lax.optimization_barrier((row_grads, route_back))

    route_grad = route_back.reshape(experts, rows).T
    prob_grad = jnp.where(named, route_grad, 0.0)
    logit_grad = router_probs * (
        prob_grad - jnp.sum(router_probs * prob_grad, axis=1, keepdims=True)
    )
    logit_grad_b = logit_grad.astype(bf16)
    ffn_in_grad = mixed_order(row_grads, w_index, parts).astype(f32) + dot(logit_grad_b, router_t)
    middle_part, ffn_gain_grad = rms_backward(ffn_in_grad, unit_two, inverse_two, ffn_gain_all)
    middle_grad = cotangent + middle_part
    router_grad = t_dot(logit_grad_b, ffn_in)

    mid_pieces = gather_pieces(middle_grad.astype(bf16))
    mid_all = jnp.concatenate(mid_pieces, axis=0)
    output_part = t_dot(attn_mix, mid_all).astype(bf16)
    output_sum = owner_scatter(output_part.reshape(owners, final_rows, width))
    mix_grad = by_head(dot_t(mid_all, output_weight).astype(bf16)).reshape(blocked)
    delta = jnp.sum(mix_grad.astype(f32) * mixed.astype(f32), axis=-1, keepdims=True)
    prob_back = pair_dot(mix_grad, values, 3, 3)
    score_grad = (probs * (prob_back - delta)).astype(bf16)
    grad_queries = pair_dot(score_grad, keys, 3, 2)
    grad_keys = pair_dot(score_grad, queries, 2, 2)
    grad_values = pair_dot(probs_b, mix_grad, 2, 2)
    grad_queries = by_row(rotate((grad_queries * scale).reshape(whole), cosine, -sine))
    grad_keys = by_row(rotate((grad_keys * scale).reshape(whole), cosine, -sine))
    query_gain_grad = jnp.sum(grad_queries * query_unit, axis=0)
    key_gain_grad = jnp.sum(grad_keys * key_unit, axis=0)
    grad_queries = grad_queries * query_gain_f
    grad_keys = grad_keys * key_gain_f
    means = jnp.stack(
        [jnp.sum(grad_queries * query_unit, axis=1), jnp.sum(grad_keys * key_unit, axis=1)], axis=0
    )
    means = group_sum(means) / width
    up_sum = scatter_far(after(up_near, means))
    up_weight_grad = jnp.stack([up_sum[:, e * ff : (e + 1) * ff] for e in range(EXP_DEV)])
    query_grad_b = (query_inverse * (grad_queries - query_unit * means[0][:, None])).astype(bf16)
    key_grad_b = (key_inverse * (grad_keys - key_unit * means[1][:, None])).astype(bf16)
    value_grad_b = by_row(grad_values.reshape(whole)).astype(bf16)
    qkv_grad = jnp.concatenate([query_grad_b, key_grad_b, value_grad_b], axis=1)
    attn_in_part = dot_t(qkv_grad, qkv_w)
    attn_in_grad = scatter_pieces(
        [attn_in_part[mask * rows : (mask + 1) * rows] for mask in range(parts)]
    )
    value_part = t_dot(attn_in, value_grad_b).astype(bf16).reshape(owners, parts * final_rows, cols)
    down_weight_grad = scatter_far(after(down_near, attn_in_part)).reshape(EXP_DEV, ff, cols)
    value_sum = owner_scatter(value_part).reshape(parts, final_rows, cols)
    value_sum = lax.all_to_all(value_sum, SHARD, split_axis=0, concat_axis=0, tiled=True)
    qk_part = t_dot(attn_in, qkv_grad[:, : 2 * cols])
    qk_part = qk_part.astype(bf16)

    unit_one, inverse_one = rms_unit(residual)
    input_part, attn_gain_grad = rms_backward(
        attn_in_grad, unit_one, inverse_one, attn_gain_all
    )
    tokens_grad = middle_grad + input_part
    moe_out = after(moe_out, attn_in_part)
    block_output = middle + mixed_order(moe_out, w_index, parts).astype(f32)

    qk_sum = lax.psum_scatter(qk_part, OWNER, scatter_dimension=0, tiled=True)
    qk_sum = qk_sum.reshape(parts, final_rows, 2 * cols)
    qk_sum = lax.all_to_all(qk_sum, SHARD, split_axis=0, concat_axis=0, tiled=True)
    qkv_sum = place(qk_sum, value_sum)
    moves = []
    for e in range(owners):
        for w in range(parts):
            moves.append((e * parts + w, w * owners + e))
    output_sum = lax.ppermute(output_sum, (OWNER, SHARD), moves).astype(f32)

    own = jnp.zeros((2, parts, cols), f32)
    own = lax.dynamic_update_slice(
        own, jnp.stack([query_gain_grad, key_gain_grad])[:, None, :], (0, w_index, 0)
    ).reshape(2, width)
    table = jnp.concatenate([attn_gain_grad[None], ffn_gain_grad[None], own, router_grad], axis=0)
    count = table.shape[0]
    table = table.reshape(count, owners, parts * final_rows).transpose(1, 0, 2)
    table = lax.all_to_all(table, OWNER, split_axis=0, concat_axis=0, tiled=True)
    table = jnp.sum(table, axis=0)
    table = table.reshape(count, parts, final_rows).transpose(1, 0, 2)
    table = jnp.sum(
        lax.all_to_all(table, SHARD, split_axis=0, concat_axis=0, tiled=True), axis=0
    )
    return (
        block_output,
        tokens_grad,
        table[0],
        qkv_sum[0],
        qkv_sum[1],
        qkv_sum[2],
        table[2],
        table[3],
        output_sum,
        table[1],
        table[4:].T,
        gate_weight_grad,
        up_weight_grad,
        down_weight_grad,
    )


def solution(mesh):
    rows = P((OWNER, SHARD), None)
    line = P((OWNER, SHARD))
    part = P(SHARD)
    wide = P(SHARD, None)
    into = P(OWNER, SHARD, None)
    back = P(OWNER, None, SHARD)
    in_specs = (rows,) * 3 + (part, wide, wide, wide, part, part, wide, part, wide)
    in_specs = in_specs + (into, into, back, rows)
    out_specs = (rows, rows, line, rows, rows, rows, line, line, rows, line, rows)
    out_specs = out_specs + (into, into, back)

    return jax.shard_map(local, mesh=mesh, in_specs=in_specs, out_specs=out_specs, check_vma=False)
```

```python
import functools

import jax
import jax.numpy as jnp
from jax import lax
from jax.experimental import pallas as pl
from jax.experimental.pallas import tpu as pltpu
from jax.sharding import PartitionSpec as P


HEADS = 16
HEAD_DIM = 128
EXP_DEV = 2
OWNER = "expert"
SHARD = "wshard"


epsilon = 1e-05
theta_base = 10000.0


def rms_unit(activation):
    inverse = lax.rsqrt(jnp.mean(activation * activation, axis=-1, keepdims=True) + epsilon)
    return (activation * inverse, inverse)


def rms_backward(grad_out, normed, inverse, gain):
    gain_grad = jnp.sum(grad_out * normed, axis=0)
    grad_normed = grad_out * gain
    centred = grad_normed - normed * jnp.mean(grad_normed * normed, axis=-1, keepdims=True)
    return (inverse * centred, gain_grad)


def block_tables(lengths, rows):
    ends = jnp.cumsum(lengths, axis=1)
    row_index = jnp.arange(rows, dtype=jnp.int32)
    passed = (row_index[None, :, None] >= ends[:, None, :]).astype(jnp.int32)
    start = jnp.sum(passed * lengths[:, None, :], axis=2)
    allowed = (row_index[None, None, :] <= row_index[None, :, None]) & (
        row_index[None, None, :] >= start[:, :, None]
    )
    offsets = (row_index[None, :] - start).reshape(-1)
    half_dim = HEAD_DIM // 2
    frequency = theta_base ** (-2.0 * jnp.arange(half_dim, dtype=jnp.float32) / HEAD_DIM)
    angles = offsets.astype(jnp.float32)[:, None] * frequency[None, :]
    return (allowed, jnp.cos(angles), jnp.sin(angles))


def rotate(rows, cosine, sine):
    half_dim = HEAD_DIM // 2
    first = rows[..., :half_dim]
    second = rows[..., half_dim:]
    cosine = cosine[None, :, :]
    sine = sine[None, :, :]
    return jnp.concatenate([first * cosine - second * sine, second * cosine + first * sine], axis=-1)


def softmax_rows(logits):
    row_max = jnp.max(logits, axis=-1, keepdims=True)
    shifted = jnp.exp(logits - row_max)
    return shifted / jnp.sum(shifted, axis=-1, keepdims=True)


def dot(a, b):
    return jnp.dot(a, b, preferred_element_type=jnp.float32)


def dot_t(a, b):
    return lax.dot_general(a, b, (((1,), (1,)), ((), ())), preferred_element_type=jnp.float32)


def t_dot(a, b):
    return lax.dot_general(a, b, (((0,), (0,)), ((), ())), preferred_element_type=jnp.float32)


def swap(values, mask, axis_name=SHARD):
    count = lax.axis_size(axis_name)
    return lax.ppermute(values, axis_name, [(i, i ^ mask) for i in range(count)])


def after(values, *others):
    return lax.optimization_barrier((values, *others))[0]


def bits_of(count):
    return [1 << k for k in range(count.bit_length() - 1)]


def gather_far(shard):
    pieces = {0: shard}
    for bit in reversed(bits_of(lax.axis_size(SHARD))[1:]):
        for mask in list(pieces):
            pieces[mask ^ bit] = swap(pieces[mask], bit)
    return pieces


def gather_near(pieces):
    pieces = dict(pieces)
    for mask in list(pieces):
        pieces[mask ^ 1] = swap(pieces[mask], 1)
    return [pieces[mask] for mask in sorted(pieces)]


def gather_pieces(shard):
    return gather_near(gather_far(shard))


def scatter_stage(blocks, bit):
    masks = sorted(blocks, reverse=True)
    arrived = {m ^ bit: swap(blocks[m].astype(jnp.bfloat16), bit) for m in masks if m & bit}
    return {m: blocks[m] + arrived[m].astype(jnp.float32) for m in arrived}


def scatter_near(blocks):
    return scatter_stage(dict(enumerate(blocks)), 1)


def scatter_far(blocks):
    for bit in bits_of(lax.axis_size(SHARD))[1:]:
        blocks = scatter_stage(blocks, bit)
    return blocks[0]


def scatter_pieces(blocks):
    return scatter_far(scatter_near(blocks))


def block_of(array, index, count, axis):
    size = array.shape[axis] // count
    return lax.dynamic_slice_in_dim(array, index * size, size, axis)


def mixed_order(array, w_index, count):
    return jnp.concatenate(
        [block_of(array, w_index ^ mask, count, array.ndim - 1) for mask in range(count)], axis=-1
    )


def pair_dot(a, b, a_axis, b_axis):
    dims = (((a_axis,), (b_axis,)), ((0, 1), (0, 1)))
    return lax.dot_general(a, b, dims, preferred_element_type=jnp.float32)


def group_sum(values):
    count = lax.axis_size(SHARD)
    blocks = values.reshape(values.shape[0], count, -1)
    total = blocks
    for mask in reversed(range(1, count)):
        arrived = swap(blocks, mask)
        total = total + jnp.stack([arrived[:, m ^ mask] for m in range(count)], axis=1)
    return total.reshape(values.shape)


def owner_scatter(values):
    owners = lax.axis_size(OWNER)
    index = lax.axis_index(OWNER)
    if owners > 8:
        return lax.psum_scatter(values, OWNER, scatter_dimension=0, tiled=True)[0]
    pairs = values.reshape(owners // 2, 2, *values.shape[1:])
    away = lax.dynamic_index_in_dim(pairs, 1 - index % 2, 1, keepdims=False)
    kept = lax.dynamic_index_in_dim(pairs, index % 2, 1, keepdims=False)
    arrived = swap(away, 1, OWNER)
    near = (kept.astype(jnp.float32) + arrived.astype(jnp.float32)).astype(jnp.bfloat16)
    total = 0.0
    for mask in reversed(range(owners // 2)):
        part = lax.dynamic_index_in_dim(near, (index // 2) ^ mask, 0, keepdims=False)
        if mask:
            part = swap(part, 2 * mask, OWNER)
        total = total + part.astype(jnp.float32)
    return total.astype(jnp.bfloat16)


def place_kernel(heads_ref, values_ref, query_ref, key_ref, value_ref):
    parts, _, cols = values_ref.shape
    for p in range(parts):
        at = slice(p * cols, (p + 1) * cols)
        query_ref[:, at] = heads_ref[p, :, :cols].astype(jnp.float32)
        key_ref[:, at] = heads_ref[p, :, cols:].astype(jnp.float32)
        value_ref[:, at] = values_ref[p].astype(jnp.float32)


def place(heads, values):
    parts, rows, cols = values.shape
    shape = jax.ShapeDtypeStruct((rows, parts * cols), jnp.float32)
    return pl.pallas_call(place_kernel, out_shape=[shape] * 3)(heads, values)


def expert_hidden_kernel(parts, x_ref, cot_ref, weight_ref, *refs):
    gates, ups, downs = refs[:parts], refs[parts : 2 * parts], refs[2 * parts : 3 * parts]
    hidden_ref, gate_grad_ref, up_grad_ref, route_ref = refs[3 * parts :]
    cols = gates[0].shape[0]
    f32 = jnp.float32
    gate_lin = up_lin = back = 0.0
    for m in range(parts):
        x = x_ref[:, m * cols : (m + 1) * cols]
        gate_lin = gate_lin + jnp.dot(x, gates[m][...], preferred_element_type=f32)
        up_lin = up_lin + jnp.dot(x, ups[m][...], preferred_element_type=f32)
        back = back + dot_t(cot_ref[:, m * cols : (m + 1) * cols], downs[m][...])
    weight = weight_ref[...]
    sigmoid = jax.nn.sigmoid(gate_lin)
    swish = gate_lin * sigmoid
    hidden = swish * up_lin
    product = hidden * back
    route = product[:, :128]
    for k in range(1, product.shape[1] // 128):
        route = route + product[:, k * 128 : (k + 1) * 128]
    hidden_ref[...] = (hidden * weight).astype(jnp.bfloat16)
    grad = back * weight
    gate_grad_ref[...] = (grad * up_lin * sigmoid * (1.0 + gate_lin * (1.0 - sigmoid))).astype(
        jnp.bfloat16
    )
    up_grad_ref[...] = (grad * swish).astype(jnp.bfloat16)

    @pl.when(pl.program_id(2) == 0)
    def _():
        route_ref[...] = route

    @pl.when(pl.program_id(2) > 0)
    def _():
        route_ref[...] += route


def row_tile_of(rows):
    return min(rows, 1024)


def expert_hidden(x, cot, weights, gates, ups, downs, tile=256):
    rows, width = x.shape
    parts = len(gates)
    count, cols, ff = gates[0].shape
    row_tile = row_tile_of(rows)
    steps = ff // tile
    row_spec = pl.BlockSpec((row_tile, width), lambda r, e, f: (r, 0))
    in_piece = pl.BlockSpec((None, cols, tile), lambda r, e, f: (e, 0, f))
    out_piece = pl.BlockSpec((None, tile, cols), lambda r, e, f: (e, f, 0))
    wide_spec = pl.BlockSpec((row_tile, tile), lambda r, e, f: (r, e * steps + f))
    wide = jax.ShapeDtypeStruct((rows, count * ff), jnp.bfloat16)
    return pl.pallas_call(
functools.partial(expert_hidden_kernel, parts),
grid=(rows // row_tile, count, steps),
in_specs=[row_spec, row_spec, pl.BlockSpec((None, row_tile, 1), lambda r, e, f: (e, r, 0))]
+ [in_piece] * (2 * parts)
+ [out_piece] * parts,
out_specs=[wide_spec] * 3
+ [pl.BlockSpec((None, row_tile, 128), lambda r, e, f: (e, r, 0))],
out_shape=[wide] * 3 + [jax.ShapeDtypeStruct((count, rows, 128), jnp.float32)],
compiler_params=pltpu.CompilerParams(vmem_limit_bytes=60 * 1024 * 1024),
    )(x, cot, weights, *gates, *ups, *downs)


def back_rows_kernel(parts, gate_grad_ref, up_grad_ref, *refs):
    gates, ups = refs[:parts], refs[parts : 2 * parts]
    out_ref, sum_ref = refs[2 * parts :]
    cols = gates[0].shape[0]
    step = pl.program_id(1) * pl.num_programs(2) + pl.program_id(2)
    last = pl.num_programs(1) * pl.num_programs(2) - 1
    for m in range(parts):
        at = slice(m * cols, (m + 1) * cols)
        part = dot_t(gate_grad_ref[...], gates[m][...]) + dot_t(up_grad_ref[...], ups[m][...])

        @pl.when(step == 0)
        def _():
            sum_ref[:, at] = part

        @pl.when((step > 0) & (step < last))
        def _():
            sum_ref[:, at] += part

        @pl.when(step == last)
        def _():
            out_ref[:, at] = (sum_ref[:, at] + part).astype(jnp.bfloat16)


def back_rows(gate_grad, up_grad, gates, ups, tile=512):
    rows = gate_grad.shape[0]
    parts = len(gates)
    count, cols, ff = gates[0].shape
    row_tile = row_tile_of(rows)
    steps = ff // tile
    wide_spec = pl.BlockSpec((row_tile, tile), lambda r, e, f: (r, e * steps + f))
    piece = pl.BlockSpec((None, cols, tile), lambda r, e, f: (e, 0, f))
    return pl.pallas_call(
functools.partial(back_rows_kernel, parts),
grid=(rows // row_tile, count, steps),
in_specs=[wide_spec] * 2 + [piece] * (2 * parts),
out_specs=pl.BlockSpec((row_tile, parts * cols), lambda r, e, f: (r, 0)),
out_shape=jax.ShapeDtypeStruct((rows, parts * cols), jnp.bfloat16),
scratch_shapes=[pltpu.VMEM((row_tile, parts * cols), jnp.float32)],
compiler_params=pltpu.CompilerParams(vmem_limit_bytes=60 * 1024 * 1024),
    )(gate_grad, up_grad, *gates, *ups)


def local(
    tokens,
    doc_lengths,
    expert_ids,
    attn_gain,
    query_weight,
    key_weight,
    value_weight,
    query_gain,
    key_gain,
    output_weight,
    ffn_gain,
    router_weight,
    gate_weight,
    up_weight,
    down_weight,
    cotangent,
):
    bf16 = jnp.bfloat16
    f32 = jnp.float32
    rows, width = tokens.shape
    owners = lax.axis_size(OWNER)
    parts = lax.axis_size(SHARD)
    w_index = lax.axis_index(SHARD)
    experts = EXP_DEV * owners
    group = parts * rows
    cols = width // parts
    heads = HEADS // parts
    final_rows = width // (owners * parts)
    ff = gate_weight.shape[2]

    e_index = lax.axis_index(OWNER)
    half = cols // 2
    unit = 2 * w_index + e_index % 2
    units = 2 * parts

    docs = doc_lengths.shape[1]
    lengths_row = jnp.zeros((1, cols), bf16).at[:, :docs].set(doc_lengths.astype(bf16))
    small = jnp.concatenate(
        [attn_gain[None, :], ffn_gain[None, :], lengths_row, router_weight.T], axis=0
    )
    small_all = lax.all_gather(small, SHARD, axis=0)
    attn_gain_all = small_all[:, 0, :].reshape(width).astype(f32)
    ffn_gain_all = small_all[:, 1, :].reshape(width).astype(f32)
    lengths_all = small_all[:, 2, :docs].astype(jnp.int32)
    lengths_all = jnp.concatenate([block_of(lengths_all, w_index ^ m, parts, 0) for m in range(parts)])
    router_t = small_all[:, 3:, :].transpose(1, 0, 2).reshape(experts, width)

    *weights_in, tokens_in, _ = lax.optimization_barrier(
        (query_weight, key_weight, value_weight, tokens, small_all)
    )
    tokens_far = gather_far(tokens_in)
    tokens_all = jnp.concatenate(gather_near(tokens_far), axis=0)
    pieces = [None] * units
    for mask in reversed(range(parts)):
        piece = jnp.concatenate(
            [block_of(weight, w_index ^ mask, parts, 1) for weight in weights_in], axis=1
        )
        for side in range(2):
            pieces[2 * mask + side] = block_of(piece, side ^ (e_index % 2), 2, 0)
    for mask in reversed(range(1, parts)):
        pieces[2 * mask] = swap(pieces[2 * mask], mask)
        if mask == 1:
            pieces[3] = swap(pieces[3], 1)
    for mask in reversed(range(2, parts)):
        pieces[2 * mask + 1] = swap(pieces[2 * mask], 1, OWNER)
    cot_b = mixed_order(cotangent, w_index, parts).astype(bf16)
    cot_all = lax.all_gather(cot_b, OWNER, axis=0, tiled=True)
    down_in = after(down_weight, pieces[4])
    down_far = gather_far(down_in)

    unit_all, _ = rms_unit(tokens_all.astype(f32))
    attn_in = (unit_all * attn_gain_all).astype(bf16)
    attn_in_mixed = mixed_order(attn_in, unit, units)
    qkv = 0.0
    for at in [0, 1, 2, 3] + [2 * m for m in range(2, parts)] + [2 * m + 1 for m in range(2, parts)]:
        qkv = qkv + dot(attn_in_mixed[:, at * half : (at + 1) * half], pieces[at])
    query_lin, key_lin, value_lin = (qkv[:, i * cols : (i + 1) * cols] for i in range(3))
    squares = jnp.stack(
        [jnp.sum(query_lin * query_lin, axis=1), jnp.sum(key_lin * key_lin, axis=1)], axis=0
    )
    squares = group_sum(squares)
    inverses = lax.rsqrt(squares / width + epsilon)
    query_inverse = inverses[0][:, None]
    key_inverse = inverses[1][:, None]
    query_unit = query_lin * query_inverse
    key_unit = key_lin * key_inverse
    query_gain_f = query_gain.astype(f32)
    key_gain_f = key_gain.astype(f32)
    allowed, cosine, sine = block_tables(lengths_all, rows)
    scale = HEAD_DIM ** (-0.5)

    def by_head(array):
        return jnp.stack(
            [array[:, h * HEAD_DIM : (h + 1) * HEAD_DIM] for h in range(heads)], axis=0
        )

    def by_row(array):
        return jnp.concatenate([array[h] for h in range(heads)], axis=1)

    blocked = (heads, parts, rows, HEAD_DIM)
    whole = (heads, group, HEAD_DIM)
    queries = rotate(by_head(query_unit * query_gain_f), cosine, sine).astype(bf16)
    queries = queries.reshape(blocked)
    keys = rotate(by_head(key_unit * key_gain_f), cosine, sine).astype(bf16).reshape(blocked)
    values = by_head(value_lin).astype(bf16).reshape(blocked)
    scores = pair_dot(queries, keys, 3, 3) * scale
    scores = jnp.where(allowed[None, :, :, :], scores, -1e30)
    row_max = jnp.max(scores, axis=-1, keepdims=True)
    log_total = row_max + jnp.log(jnp.sum(jnp.exp(scores - row_max), axis=-1, keepdims=True))
    probs = jnp.exp(scores - log_total)
    probs_b = probs.astype(bf16)
    mixed = pair_dot(probs_b, values, 3, 2).astype(bf16)
    attn_mix = by_row(mixed.reshape(whole))
    attn_out = dot(attn_mix, output_weight)
    attn_out = scatter_pieces([attn_out[mask * rows : (mask + 1) * rows] for mask in range(parts)])
    attn_out, *pieces = lax.optimization_barrier((attn_out, *pieces))
    qkv_w = jnp.concatenate(pieces, axis=0)
    qkv_w = jnp.concatenate(
        [block_of(qkv_w, unit ^ k, units, 0) for k in range(units)], axis=0
    )

    residual = tokens.astype(f32)
    middle = residual + attn_out
    unit_two, inverse_two = rms_unit(middle)
    ffn_in = (unit_two * ffn_gain_all).astype(bf16)
    ffn_in_mixed = mixed_order(ffn_in, w_index, parts)
    gate_in, up_in, ffn_in_mixed, ffn_in = lax.optimization_barrier(
        (gate_weight, up_weight, ffn_in_mixed, ffn_in)
    )
    gate_far = gather_far(gate_in)
    up_far = gather_far(up_in)
    router_probs = softmax_rows(dot_t(ffn_in, router_t))
    expert_range = jnp.arange(experts, dtype=jnp.int32)
    named = jnp.any(expert_ids[:, :, None] == expert_range[None, None, :], axis=1)
    route_table = jnp.where(named, router_probs, 0.0)

    arrived = lax.all_gather(ffn_in_mixed, OWNER, axis=0, tiled=True)
    weights = lax.all_to_all(
        route_table.reshape(rows, owners, EXP_DEV).transpose(1, 2, 0),
        OWNER,
        split_axis=0,
        concat_axis=0,
        tiled=True,
    )
    weights = weights.transpose(1, 0, 2).reshape(EXP_DEV, owners * rows, 1)
    gate_pieces = gather_near(gate_far)
    up_pieces = gather_near(
        {m: after(p, weights, gate_pieces[-1]) if m else p for m, p in up_far.items()}
    )
    down_pieces = gather_near({m: after(p, attn_out) if m else p for m, p in down_far.items()})
    hidden_w, gate_grad_b, up_grad_b, route_part = expert_hidden(
        arrived, cot_all, weights, gate_pieces, up_pieces, down_pieces
    )
    row_partial = back_rows(gate_grad_b, up_grad_b, gate_pieces, up_pieces)
    row_grads = lax.psum_scatter(row_partial, OWNER, scatter_dimension=0, tiled=True)
    route_back = jnp.sum(route_part, axis=2)
    route_back = lax.all_to_all(
        route_back.reshape(EXP_DEV, owners, rows).transpose(1, 0, 2),
        OWNER,
        split_axis=0,
        concat_axis=0,
        tiled=True,
    )
    part_of = lambda array, mask: array[:, mask * cols : (mask + 1) * cols]
    order = sorted(range(parts), key=lambda m: (m < parts // 2, -m))

    def ordered_blocks(make):
        blocks = [None] * parts
        for mask in order:
            blocks[mask] = make(mask)
        return blocks

    gate_blocks = ordered_blocks(lambda m: t_dot(part_of(arrived, m), gate_grad_b))
    gate_near = scatter_near(gate_blocks)
    up_blocks = ordered_blocks(lambda m: t_dot(part_of(arrived, m), up_grad_b))
    up_near = scatter_near(up_blocks)
    hidden_w, qkv_w, *_ = lax.optimization_barrier((hidden_w, qkv_w, *gate_blocks, *up_blocks))
    down_blocks = ordered_blocks(lambda m: t_dot(hidden_w, part_of(cot_all, m)))
    down_near = scatter_near(down_blocks)
    gate_sum = scatter_far(gate_near)
    gate_weight_grad = jnp.stack([gate_sum[:, e * ff : (e + 1) * ff] for e in range(EXP_DEV)])
    down_all = jnp.concatenate(
        [piece.reshape(EXP_DEV * ff, cols) for piece in down_pieces], axis=1
    )
    out_partial = dot(hidden_w, down_all)
    out_partial = out_partial.astype(bf16)
    row_grads, route_back = lax.optimization_barrier((row_grads, route_back))
    moe_out = lax.psum_scatter(out_partial, OWNER, scatter_dimension=0, tiled=True)

    route_grad = route_back.reshape(experts, rows).T
    prob_grad = jnp.where(named, route_grad, 0.0)
    logit_grad = router_probs * (
        prob_grad - jnp.sum(router_probs * prob_grad, axis=1, keepdims=True)
    )
    logit_grad_b = logit_grad.astype(bf16)
    ffn_in_grad = mixed_order(row_grads, w_index, parts).astype(f32) + dot(logit_grad_b, router_t)
    middle_part, ffn_gain_grad = rms_backward(ffn_in_grad, unit_two, inverse_two, ffn_gain_all)
    middle_grad = cotangent + middle_part
    router_grad = t_dot(logit_grad_b, ffn_in)

    mid_pieces = gather_pieces(middle_grad.astype(bf16))
    mid_all = jnp.concatenate(mid_pieces, axis=0)
    output_part = t_dot(attn_mix, mid_all).astype(bf16)
    output_sum = owner_scatter(output_part.reshape(owners, final_rows, width))
    mix_grad = by_head(dot_t(mid_all, output_weight).astype(bf16)).reshape(blocked)
    delta = jnp.sum(mix_grad.astype(f32) * mixed.astype(f32), axis=-1, keepdims=True)
    prob_back = pair_dot(mix_grad, values, 3, 3)
    score_grad = (probs * (prob_back - delta)).astype(bf16)
    grad_queries = pair_dot(score_grad, keys, 3, 2)
    grad_keys = pair_dot(score_grad, queries, 2, 2)
    grad_values = pair_dot(probs_b, mix_grad, 2, 2)
    grad_queries = by_row(rotate((grad_queries * scale).reshape(whole), cosine, -sine))
    grad_keys = by_row(rotate((grad_keys * scale).reshape(whole), cosine, -sine))
    query_gain_grad = jnp.sum(grad_queries * query_unit, axis=0)
    key_gain_grad = jnp.sum(grad_keys * key_unit, axis=0)
    grad_queries = grad_queries * query_gain_f
    grad_keys = grad_keys * key_gain_f
    means = jnp.stack(
        [jnp.sum(grad_queries * query_unit, axis=1), jnp.sum(grad_keys * key_unit, axis=1)], axis=0
    )
    means = group_sum(means) / width
    up_sum = scatter_far(after(up_near, means))
    up_weight_grad = jnp.stack([up_sum[:, e * ff : (e + 1) * ff] for e in range(EXP_DEV)])
    query_grad_b = (query_inverse * (grad_queries - query_unit * means[0][:, None])).astype(bf16)
    key_grad_b = (key_inverse * (grad_keys - key_unit * means[1][:, None])).astype(bf16)
    value_grad_b = by_row(grad_values.reshape(whole)).astype(bf16)
    qkv_grad = jnp.concatenate([query_grad_b, key_grad_b, value_grad_b], axis=1)
    attn_in_part = dot_t(qkv_grad, qkv_w)
    attn_in_grad = scatter_pieces(
        [attn_in_part[mask * rows : (mask + 1) * rows] for mask in range(parts)]
    )
    value_part = t_dot(attn_in, value_grad_b).astype(bf16).reshape(owners, parts * final_rows, cols)
    down_weight_grad = scatter_far(after(down_near, attn_in_part)).reshape(EXP_DEV, ff, cols)
    value_sum = owner_scatter(value_part).reshape(parts, final_rows, cols)
    value_sum = lax.all_to_all(value_sum, SHARD, split_axis=0, concat_axis=0, tiled=True)
    qk_part = t_dot(attn_in, qkv_grad[:, : 2 * cols])
    qk_part = qk_part.astype(bf16)

    unit_one, inverse_one = rms_unit(residual)
    input_part, attn_gain_grad = rms_backward(
        attn_in_grad, unit_one, inverse_one, attn_gain_all
    )
    tokens_grad = middle_grad + input_part
    moe_out = after(moe_out, attn_in_part)
    block_output = middle + mixed_order(moe_out, w_index, parts).astype(f32)

    qk_sum = lax.psum_scatter(qk_part, OWNER, scatter_dimension=0, tiled=True)
    qk_sum = qk_sum.reshape(parts, final_rows, 2 * cols)
    qk_sum = lax.all_to_all(qk_sum, SHARD, split_axis=0, concat_axis=0, tiled=True)
    qkv_sum = place(qk_sum, value_sum)
    moves = []
    for e in range(owners):
        for w in range(parts):
            moves.append((e * parts + w, w * owners + e))
    output_sum = lax.ppermute(output_sum, (OWNER, SHARD), moves).astype(f32)

    own = jnp.zeros((2, parts, cols), f32)
    own = lax.dynamic_update_slice(
        own, jnp.stack([query_gain_grad, key_gain_grad])[:, None, :], (0, w_index, 0)
    ).reshape(2, width)
    table = jnp.concatenate([attn_gain_grad[None], ffn_gain_grad[None], own, router_grad], axis=0)
    count = table.shape[0]
    table = table.reshape(count, owners, parts * final_rows).transpose(1, 0, 2)
    table = lax.all_to_all(table, OWNER, split_axis=0, concat_axis=0, tiled=True)
    table = jnp.sum(table, axis=0)
    table = table.reshape(count, parts, final_rows).transpose(1, 0, 2)
    table = jnp.sum(
        lax.all_to_all(table, SHARD, split_axis=0, concat_axis=0, tiled=True), axis=0
    )
    return (
        block_output,
        tokens_grad,
        table[0],
        qkv_sum[0],
        qkv_sum[1],
        qkv_sum[2],
        table[2],
        table[3],
        output_sum,
        table[1],
        table[4:].T,
        gate_weight_grad,
        up_weight_grad,
        down_weight_grad,
    )


def solution(mesh):
    rows = P((OWNER, SHARD), None)
    line = P((OWNER, SHARD))
    part = P(SHARD)
    wide = P(SHARD, None)
    into = P(OWNER, SHARD, None)
    back = P(OWNER, None, SHARD)
    in_specs = (rows,) * 3 + (part, wide, wide, wide, part, part, wide, part, wide)
    in_specs = in_specs + (into, into, back, rows)
    out_specs = (rows, rows, line, rows, rows, rows, line, line, rows, line, rows)
    out_specs = out_specs + (into, into, back)

    return jax.shard_map(local, mesh=mesh, in_specs=in_specs, out_specs=out_specs, check_vma=False)
```

```python
import functools

import jax
import jax.numpy as jnp
from jax import lax
from jax.experimental import pallas as pl
from jax.experimental.pallas import tpu as pltpu
from jax.sharding import PartitionSpec as P


HEADS = 16
HEAD_DIM = 128
EXP_DEV = 2
OWNER = "expert"
SHARD = "wshard"


epsilon = 1e-05
theta_base = 10000.0


def rms_unit(activation):
    inverse = lax.rsqrt(jnp.mean(activation * activation, axis=-1, keepdims=True) + epsilon)
    return (activation * inverse, inverse)


def rms_backward(grad_out, normed, inverse, gain):
    gain_grad = jnp.sum(grad_out * normed, axis=0)
    grad_normed = grad_out * gain
    centred = grad_normed - normed * jnp.mean(grad_normed * normed, axis=-1, keepdims=True)
    return (inverse * centred, gain_grad)


def block_tables(lengths, rows):
    ends = jnp.cumsum(lengths, axis=1)
    row_index = jnp.arange(rows, dtype=jnp.int32)
    passed = (row_index[None, :, None] >= ends[:, None, :]).astype(jnp.int32)
    start = jnp.sum(passed * lengths[:, None, :], axis=2)
    allowed = (row_index[None, None, :] <= row_index[None, :, None]) & (
        row_index[None, None, :] >= start[:, :, None]
    )
    offsets = (row_index[None, :] - start).reshape(-1)
    half_dim = HEAD_DIM // 2
    frequency = theta_base ** (-2.0 * jnp.arange(half_dim, dtype=jnp.float32) / HEAD_DIM)
    angles = offsets.astype(jnp.float32)[:, None] * frequency[None, :]
    return (allowed, jnp.cos(angles), jnp.sin(angles))


def rotate(rows, cosine, sine):
    half_dim = HEAD_DIM // 2
    first = rows[..., :half_dim]
    second = rows[..., half_dim:]
    cosine = cosine[None, :, :]
    sine = sine[None, :, :]
    return jnp.concatenate([first * cosine - second * sine, second * cosine + first * sine], axis=-1)


def softmax_rows(logits):
    row_max = jnp.max(logits, axis=-1, keepdims=True)
    shifted = jnp.exp(logits - row_max)
    return shifted / jnp.sum(shifted, axis=-1, keepdims=True)


def dot(a, b):
    return jnp.dot(a, b, preferred_element_type=jnp.float32)


def dot_t(a, b):
    return lax.dot_general(a, b, (((1,), (1,)), ((), ())), preferred_element_type=jnp.float32)


def t_dot(a, b):
    return lax.dot_general(a, b, (((0,), (0,)), ((), ())), preferred_element_type=jnp.float32)


def swap(values, mask, axis_name=SHARD):
    count = lax.axis_size(axis_name)
    return lax.ppermute(values, axis_name, [(i, i ^ mask) for i in range(count)])


def after(values, *others):
    return lax.optimization_barrier((values, *others))[0]


def bits_of(count):
    return [1 << k for k in range(count.bit_length() - 1)]


def gather_far(shard):
    pieces = {0: shard}
    for bit in reversed(bits_of(lax.axis_size(SHARD))[1:]):
        for mask in list(pieces):
            pieces[mask ^ bit] = swap(pieces[mask], bit)
    return pieces


def gather_near(pieces):
    pieces = dict(pieces)
    for mask in list(pieces):
        pieces[mask ^ 1] = swap(pieces[mask], 1)
    return [pieces[mask] for mask in sorted(pieces)]


def gather_pieces(shard):
    return gather_near(gather_far(shard))


def scatter_stage(blocks, bit):
    masks = sorted(blocks, reverse=True)
    arrived = {m ^ bit: swap(blocks[m].astype(jnp.bfloat16), bit) for m in masks if m & bit}
    return {m: blocks[m] + arrived[m].astype(jnp.float32) for m in arrived}


def scatter_near(blocks):
    return scatter_stage(dict(enumerate(blocks)), 1)


def scatter_far(blocks):
    for bit in bits_of(lax.axis_size(SHARD))[1:]:
        blocks = scatter_stage(blocks, bit)
    return blocks[0]


def scatter_pieces(blocks):
    return scatter_far(scatter_near(blocks))


def block_of(array, index, count, axis):
    size = array.shape[axis] // count
    return lax.dynamic_slice_in_dim(array, index * size, size, axis)


def mixed_order(array, w_index, count):
    return jnp.concatenate(
        [block_of(array, w_index ^ mask, count, array.ndim - 1) for mask in range(count)], axis=-1
    )


def pair_dot(a, b, a_axis, b_axis):
    dims = (((a_axis,), (b_axis,)), ((0, 1), (0, 1)))
    return lax.dot_general(a, b, dims, preferred_element_type=jnp.float32)


def group_sum(values):
    count = lax.axis_size(SHARD)
    blocks = values.reshape(values.shape[0], count, -1)
    total = blocks
    for mask in reversed(range(1, count)):
        arrived = swap(blocks, mask)
        total = total + jnp.stack([arrived[:, m ^ mask] for m in range(count)], axis=1)
    return total.reshape(values.shape)


def owner_scatter(values):
    owners = lax.axis_size(OWNER)
    values = values.reshape([2] * len(bits_of(owners)) + list(values.shape[1:]))
    for axis, bit in reversed(list(enumerate(reversed(bits_of(owners))))):
        index = (lax.axis_index(OWNER) // bit) % 2
        away = lax.dynamic_index_in_dim(values, 1 - index, axis, keepdims=False)
        kept = lax.dynamic_index_in_dim(values, index, axis, keepdims=False)
        arrived = swap(away, bit, OWNER)
        values = (kept.astype(jnp.float32) + arrived.astype(jnp.float32)).astype(jnp.bfloat16)
    return values


def place_kernel(heads_ref, values_ref, query_ref, key_ref, value_ref):
    parts, _, cols = values_ref.shape
    for p in range(parts):
        at = slice(p * cols, (p + 1) * cols)
        query_ref[:, at] = heads_ref[p, :, :cols].astype(jnp.float32)
        key_ref[:, at] = heads_ref[p, :, cols:].astype(jnp.float32)
        value_ref[:, at] = values_ref[p].astype(jnp.float32)


def place(heads, values):
    parts, rows, cols = values.shape
    shape = jax.ShapeDtypeStruct((rows, parts * cols), jnp.float32)
    return pl.pallas_call(place_kernel, out_shape=[shape] * 3)(heads, values)


def expert_hidden_kernel(parts, x_ref, cot_ref, weight_ref, *refs):
    gates, ups, downs = refs[:parts], refs[parts : 2 * parts], refs[2 * parts : 3 * parts]
    hidden_ref, gate_grad_ref, up_grad_ref, route_ref = refs[3 * parts :]
    cols = gates[0].shape[0]
    f32 = jnp.float32
    gate_lin = up_lin = back = 0.0
    for m in range(parts):
        x = x_ref[:, m * cols : (m + 1) * cols]
        gate_lin = gate_lin + jnp.dot(x, gates[m][...], preferred_element_type=f32)
        up_lin = up_lin + jnp.dot(x, ups[m][...], preferred_element_type=f32)
        back = back + dot_t(cot_ref[:, m * cols : (m + 1) * cols], downs[m][...])
    weight = weight_ref[...]
    sigmoid = jax.nn.sigmoid(gate_lin)
    swish = gate_lin * sigmoid
    hidden = swish * up_lin
    product = hidden * back
    route = product[:, :128]
    for k in range(1, product.shape[1] // 128):
        route = route + product[:, k * 128 : (k + 1) * 128]
    hidden_ref[...] = (hidden * weight).astype(jnp.bfloat16)
    grad = back * weight
    gate_grad_ref[...] = (grad * up_lin * sigmoid * (1.0 + gate_lin * (1.0 - sigmoid))).astype(
        jnp.bfloat16
    )
    up_grad_ref[...] = (grad * swish).astype(jnp.bfloat16)

    @pl.when(pl.program_id(2) == 0)
    def _():
        route_ref[...] = route

    @pl.when(pl.program_id(2) > 0)
    def _():
        route_ref[...] += route


def row_tile_of(rows):
    return min(rows, 1024)


def expert_hidden(x, cot, weights, gates, ups, downs, tile=256):
    rows, width = x.shape
    parts = len(gates)
    count, cols, ff = gates[0].shape
    row_tile = row_tile_of(rows)
    steps = ff // tile
    row_spec = pl.BlockSpec((row_tile, width), lambda r, e, f: (r, 0))
    in_piece = pl.BlockSpec((None, cols, tile), lambda r, e, f: (e, 0, f))
    out_piece = pl.BlockSpec((None, tile, cols), lambda r, e, f: (e, f, 0))
    wide_spec = pl.BlockSpec((row_tile, tile), lambda r, e, f: (r, e * steps + f))
    wide = jax.ShapeDtypeStruct((rows, count * ff), jnp.bfloat16)
    return pl.pallas_call(
functools.partial(expert_hidden_kernel, parts),
grid=(rows // row_tile, count, steps),
in_specs=[row_spec, row_spec, pl.BlockSpec((None, row_tile, 1), lambda r, e, f: (e, r, 0))]
+ [in_piece] * (2 * parts)
+ [out_piece] * parts,
out_specs=[wide_spec] * 3
+ [pl.BlockSpec((None, row_tile, 128), lambda r, e, f: (e, r, 0))],
out_shape=[wide] * 3 + [jax.ShapeDtypeStruct((count, rows, 128), jnp.float32)],
compiler_params=pltpu.CompilerParams(vmem_limit_bytes=60 * 1024 * 1024),
    )(x, cot, weights, *gates, *ups, *downs)


def back_rows_kernel(parts, gate_grad_ref, up_grad_ref, *refs):
    gates, ups = refs[:parts], refs[parts : 2 * parts]
    out_ref, sum_ref = refs[2 * parts :]
    cols = gates[0].shape[0]
    step = pl.program_id(1) * pl.num_programs(2) + pl.program_id(2)
    last = pl.num_programs(1) * pl.num_programs(2) - 1
    for m in range(parts):
        at = slice(m * cols, (m + 1) * cols)
        part = dot_t(gate_grad_ref[...], gates[m][...]) + dot_t(up_grad_ref[...], ups[m][...])

        @pl.when(step == 0)
        def _():
            sum_ref[:, at] = part

        @pl.when((step > 0) & (step < last))
        def _():
            sum_ref[:, at] += part

        @pl.when(step == last)
        def _():
            out_ref[:, at] = (sum_ref[:, at] + part).astype(jnp.bfloat16)


def back_rows(gate_grad, up_grad, gates, ups, tile=512):
    rows = gate_grad.shape[0]
    parts = len(gates)
    count, cols, ff = gates[0].shape
    row_tile = row_tile_of(rows)
    steps = ff // tile
    wide_spec = pl.BlockSpec((row_tile, tile), lambda r, e, f: (r, e * steps + f))
    piece = pl.BlockSpec((None, cols, tile), lambda r, e, f: (e, 0, f))
    return pl.pallas_call(
functools.partial(back_rows_kernel, parts),
grid=(rows // row_tile, count, steps),
in_specs=[wide_spec] * 2 + [piece] * (2 * parts),
out_specs=pl.BlockSpec((row_tile, parts * cols), lambda r, e, f: (r, 0)),
out_shape=jax.ShapeDtypeStruct((rows, parts * cols), jnp.bfloat16),
scratch_shapes=[pltpu.VMEM((row_tile, parts * cols), jnp.float32)],
compiler_params=pltpu.CompilerParams(vmem_limit_bytes=60 * 1024 * 1024),
    )(gate_grad, up_grad, *gates, *ups)


def local(
    tokens,
    doc_lengths,
    expert_ids,
    attn_gain,
    query_weight,
    key_weight,
    value_weight,
    query_gain,
    key_gain,
    output_weight,
    ffn_gain,
    router_weight,
    gate_weight,
    up_weight,
    down_weight,
    cotangent,
):
    bf16 = jnp.bfloat16
    f32 = jnp.float32
    rows, width = tokens.shape
    owners = lax.axis_size(OWNER)
    parts = lax.axis_size(SHARD)
    w_index = lax.axis_index(SHARD)
    experts = EXP_DEV * owners
    group = parts * rows
    cols = width // parts
    heads = HEADS // parts
    final_rows = width // (owners * parts)
    ff = gate_weight.shape[2]

    e_index = lax.axis_index(OWNER)
    half = cols // 2
    unit = 2 * w_index + e_index % 2
    units = 2 * parts

    docs = doc_lengths.shape[1]
    lengths_row = jnp.zeros((1, cols), bf16).at[:, :docs].set(doc_lengths.astype(bf16))
    small = jnp.concatenate(
        [attn_gain[None, :], ffn_gain[None, :], lengths_row, router_weight.T], axis=0
    )
    small_all = lax.all_gather(small, SHARD, axis=0)
    attn_gain_all = small_all[:, 0, :].reshape(width).astype(f32)
    ffn_gain_all = small_all[:, 1, :].reshape(width).astype(f32)
    lengths_all = small_all[:, 2, :docs].astype(jnp.int32)
    lengths_all = jnp.concatenate([block_of(lengths_all, w_index ^ m, parts, 0) for m in range(parts)])
    router_t = small_all[:, 3:, :].transpose(1, 0, 2).reshape(experts, width)

    *weights_in, tokens_in, _ = lax.optimization_barrier(
        (query_weight, key_weight, value_weight, tokens, small_all)
    )
    tokens_far = gather_far(tokens_in)
    tokens_all = jnp.concatenate(gather_near(tokens_far), axis=0)
    pieces = [None] * units
    for mask in reversed(range(parts)):
        piece = jnp.concatenate(
            [block_of(weight, w_index ^ mask, parts, 1) for weight in weights_in], axis=1
        )
        for side in range(2):
            pieces[2 * mask + side] = block_of(piece, side ^ (e_index % 2), 2, 0)
    for mask in reversed(range(1, parts)):
        pieces[2 * mask] = swap(pieces[2 * mask], mask)
        if mask == 1:
            pieces[3] = swap(pieces[3], 1)
    for mask in reversed(range(2, parts)):
        pieces[2 * mask + 1] = swap(pieces[2 * mask], 1, OWNER)
    cot_b = mixed_order(cotangent, w_index, parts).astype(bf16)
    cot_all = lax.all_gather(cot_b, OWNER, axis=0, tiled=True)
    down_in = after(down_weight, pieces[4])
    down_far = gather_far(down_in)

    unit_all, _ = rms_unit(tokens_all.astype(f32))
    attn_in = (unit_all * attn_gain_all).astype(bf16)
    attn_in_mixed = mixed_order(attn_in, unit, units)
    qkv = 0.0
    for at in [0, 1, 2, 3] + [2 * m for m in range(2, parts)] + [2 * m + 1 for m in range(2, parts)]:
        qkv = qkv + dot(attn_in_mixed[:, at * half : (at + 1) * half], pieces[at])
    query_lin, key_lin, value_lin = (qkv[:, i * cols : (i + 1) * cols] for i in range(3))
    squares = jnp.stack(
        [jnp.sum(query_lin * query_lin, axis=1), jnp.sum(key_lin * key_lin, axis=1)], axis=0
    )
    squares = group_sum(squares)
    inverses = lax.rsqrt(squares / width + epsilon)
    query_inverse = inverses[0][:, None]
    key_inverse = inverses[1][:, None]
    query_unit = query_lin * query_inverse
    key_unit = key_lin * key_inverse
    query_gain_f = query_gain.astype(f32)
    key_gain_f = key_gain.astype(f32)
    allowed, cosine, sine = block_tables(lengths_all, rows)
    scale = HEAD_DIM ** (-0.5)

    def by_head(array):
        return jnp.stack(
            [array[:, h * HEAD_DIM : (h + 1) * HEAD_DIM] for h in range(heads)], axis=0
        )

    def by_row(array):
        return jnp.concatenate([array[h] for h in range(heads)], axis=1)

    blocked = (heads, parts, rows, HEAD_DIM)
    whole = (heads, group, HEAD_DIM)
    queries = rotate(by_head(query_unit * query_gain_f), cosine, sine).astype(bf16)
    queries = queries.reshape(blocked)
    keys = rotate(by_head(key_unit * key_gain_f), cosine, sine).astype(bf16).reshape(blocked)
    values = by_head(value_lin).astype(bf16).reshape(blocked)
    scores = pair_dot(queries, keys, 3, 3) * scale
    scores = jnp.where(allowed[None, :, :, :], scores, -1e30)
    row_max = jnp.max(scores, axis=-1, keepdims=True)
    log_total = row_max + jnp.log(jnp.sum(jnp.exp(scores - row_max), axis=-1, keepdims=True))
    probs = jnp.exp(scores - log_total)
    probs_b = probs.astype(bf16)
    mixed = pair_dot(probs_b, values, 3, 2).astype(bf16)
    attn_mix = by_row(mixed.reshape(whole))
    attn_out = dot(attn_mix, output_weight)
    attn_out = scatter_pieces([attn_out[mask * rows : (mask + 1) * rows] for mask in range(parts)])
    attn_out, *pieces = lax.optimization_barrier((attn_out, *pieces))
    qkv_w = jnp.concatenate(pieces, axis=0)
    qkv_w = jnp.concatenate(
        [block_of(qkv_w, unit ^ k, units, 0) for k in range(units)], axis=0
    )

    residual = tokens.astype(f32)
    middle = residual + attn_out
    unit_two, inverse_two = rms_unit(middle)
    ffn_in = (unit_two * ffn_gain_all).astype(bf16)
    ffn_in_mixed = mixed_order(ffn_in, w_index, parts)
    gate_in, up_in, ffn_in_mixed, ffn_in = lax.optimization_barrier(
        (gate_weight, up_weight, ffn_in_mixed, ffn_in)
    )
    gate_far = gather_far(gate_in)
    up_far = gather_far(up_in)
    router_probs = softmax_rows(dot_t(ffn_in, router_t))
    expert_range = jnp.arange(experts, dtype=jnp.int32)
    named = jnp.any(expert_ids[:, :, None] == expert_range[None, None, :], axis=1)
    route_table = jnp.where(named, router_probs, 0.0)

    arrived = lax.all_gather(ffn_in_mixed, OWNER, axis=0, tiled=True)
    weights = lax.all_to_all(
        route_table.reshape(rows, owners, EXP_DEV).transpose(1, 2, 0),
        OWNER,
        split_axis=0,
        concat_axis=0,
        tiled=True,
    )
    weights = weights.transpose(1, 0, 2).reshape(EXP_DEV, owners * rows, 1)
    gate_pieces = gather_near(gate_far)
    up_pieces = gather_near(
        {m: after(p, weights, gate_pieces[-1]) if m else p for m, p in up_far.items()}
    )
    down_pieces = gather_near({m: after(p, attn_out) if m else p for m, p in down_far.items()})
    hidden_w, gate_grad_b, up_grad_b, route_part = expert_hidden(
        arrived, cot_all, weights, gate_pieces, up_pieces, down_pieces
    )
    row_partial = back_rows(gate_grad_b, up_grad_b, gate_pieces, up_pieces)
    row_grads = lax.psum_scatter(row_partial, OWNER, scatter_dimension=0, tiled=True)
    route_back = jnp.sum(route_part, axis=2)
    route_back = lax.all_to_all(
        route_back.reshape(EXP_DEV, owners, rows).transpose(1, 0, 2),
        OWNER,
        split_axis=0,
        concat_axis=0,
        tiled=True,
    )
    part_of = lambda array, mask: array[:, mask * cols : (mask + 1) * cols]
    order = sorted(range(parts), key=lambda m: (m < parts // 2, -m))

    def ordered_blocks(make):
        blocks = [None] * parts
        for mask in order:
            blocks[mask] = make(mask)
        return blocks

    gate_blocks = ordered_blocks(lambda m: t_dot(part_of(arrived, m), gate_grad_b))
    gate_near = scatter_near(gate_blocks)
    up_blocks = ordered_blocks(lambda m: t_dot(part_of(arrived, m), up_grad_b))
    up_near = scatter_near(up_blocks)
    hidden_w, qkv_w, *_ = lax.optimization_barrier((hidden_w, qkv_w, *gate_blocks, *up_blocks))
    down_blocks = ordered_blocks(lambda m: t_dot(hidden_w, part_of(cot_all, m)))
    down_near = scatter_near(down_blocks)
    gate_sum = scatter_far(gate_near)
    gate_weight_grad = jnp.stack([gate_sum[:, e * ff : (e + 1) * ff] for e in range(EXP_DEV)])
    down_all = jnp.concatenate(
        [piece.reshape(EXP_DEV * ff, cols) for piece in down_pieces], axis=1
    )
    out_partial = dot(hidden_w, down_all)
    out_partial = out_partial.astype(bf16)
    row_grads, route_back = lax.optimization_barrier((row_grads, route_back))
    moe_out = owner_scatter(out_partial.reshape(owners, rows, width))

    route_grad = route_back.reshape(experts, rows).T
    prob_grad = jnp.where(named, route_grad, 0.0)
    logit_grad = router_probs * (
        prob_grad - jnp.sum(router_probs * prob_grad, axis=1, keepdims=True)
    )
    logit_grad_b = logit_grad.astype(bf16)
    ffn_in_grad = mixed_order(row_grads, w_index, parts).astype(f32) + dot(logit_grad_b, router_t)
    middle_part, ffn_gain_grad = rms_backward(ffn_in_grad, unit_two, inverse_two, ffn_gain_all)
    middle_grad = cotangent + middle_part
    router_grad = t_dot(logit_grad_b, ffn_in)

    mid_pieces = gather_pieces(middle_grad.astype(bf16))
    mid_all = jnp.concatenate(mid_pieces, axis=0)
    output_part = t_dot(attn_mix, mid_all).astype(bf16)
    output_sum = owner_scatter(output_part.reshape(owners, final_rows, width))
    mix_grad = by_head(dot_t(mid_all, output_weight).astype(bf16)).reshape(blocked)
    delta = jnp.sum(mix_grad.astype(f32) * mixed.astype(f32), axis=-1, keepdims=True)
    prob_back = pair_dot(mix_grad, values, 3, 3)
    score_grad = (probs * (prob_back - delta)).astype(bf16)
    grad_queries = pair_dot(score_grad, keys, 3, 2)
    grad_keys = pair_dot(score_grad, queries, 2, 2)
    grad_values = pair_dot(probs_b, mix_grad, 2, 2)
    grad_queries = by_row(rotate((grad_queries * scale).reshape(whole), cosine, -sine))
    grad_keys = by_row(rotate((grad_keys * scale).reshape(whole), cosine, -sine))
    query_gain_grad = jnp.sum(grad_queries * query_unit, axis=0)
    key_gain_grad = jnp.sum(grad_keys * key_unit, axis=0)
    grad_queries = grad_queries * query_gain_f
    grad_keys = grad_keys * key_gain_f
    means = jnp.stack(
        [jnp.sum(grad_queries * query_unit, axis=1), jnp.sum(grad_keys * key_unit, axis=1)], axis=0
    )
    means = group_sum(means) / width
    up_sum = scatter_far(after(up_near, means))
    up_weight_grad = jnp.stack([up_sum[:, e * ff : (e + 1) * ff] for e in range(EXP_DEV)])
    query_grad_b = (query_inverse * (grad_queries - query_unit * means[0][:, None])).astype(bf16)
    key_grad_b = (key_inverse * (grad_keys - key_unit * means[1][:, None])).astype(bf16)
    value_grad_b = by_row(grad_values.reshape(whole)).astype(bf16)
    qkv_grad = jnp.concatenate([query_grad_b, key_grad_b, value_grad_b], axis=1)
    attn_in_part = dot_t(qkv_grad, qkv_w)
    attn_in_grad = scatter_pieces(
        [attn_in_part[mask * rows : (mask + 1) * rows] for mask in range(parts)]
    )
    value_part = t_dot(attn_in, value_grad_b).astype(bf16).reshape(owners, parts * final_rows, cols)
    down_weight_grad = scatter_far(after(down_near, attn_in_part)).reshape(EXP_DEV, ff, cols)
    value_sum = owner_scatter(value_part).reshape(parts, final_rows, cols)
    value_sum = lax.all_to_all(value_sum, SHARD, split_axis=0, concat_axis=0, tiled=True)
    qk_part = t_dot(attn_in, qkv_grad[:, : 2 * cols])
    qk_part = qk_part.astype(bf16)

    unit_one, inverse_one = rms_unit(residual)
    input_part, attn_gain_grad = rms_backward(
        attn_in_grad, unit_one, inverse_one, attn_gain_all
    )
    tokens_grad = middle_grad + input_part
    moe_out = after(moe_out, attn_in_part)
    block_output = middle + mixed_order(moe_out, w_index, parts).astype(f32)

    qk_sum = lax.psum_scatter(qk_part, OWNER, scatter_dimension=0, tiled=True)
    qk_sum = qk_sum.reshape(parts, final_rows, 2 * cols)
    qk_sum = lax.all_to_all(qk_sum, SHARD, split_axis=0, concat_axis=0, tiled=True)
    qkv_sum = place(qk_sum, value_sum)
    moves = []
    for e in range(owners):
        for w in range(parts):
            moves.append((e * parts + w, w * owners + e))
    output_sum = lax.ppermute(output_sum, (OWNER, SHARD), moves).astype(f32)

    own = jnp.zeros((2, parts, cols), f32)
    own = lax.dynamic_update_slice(
        own, jnp.stack([query_gain_grad, key_gain_grad])[:, None, :], (0, w_index, 0)
    ).reshape(2, width)
    table = jnp.concatenate([attn_gain_grad[None], ffn_gain_grad[None], own, router_grad], axis=0)
    count = table.shape[0]
    table = table.reshape(count, owners, parts * final_rows).transpose(1, 0, 2)
    table = lax.all_to_all(table, OWNER, split_axis=0, concat_axis=0, tiled=True)
    table = jnp.sum(table, axis=0)
    table = table.reshape(count, parts, final_rows).transpose(1, 0, 2)
    table = jnp.sum(
        lax.all_to_all(table, SHARD, split_axis=0, concat_axis=0, tiled=True), axis=0
    )
    return (
        block_output,
        tokens_grad,
        table[0],
        qkv_sum[0],
        qkv_sum[1],
        qkv_sum[2],
        table[2],
        table[3],
        output_sum,
        table[1],
        table[4:].T,
        gate_weight_grad,
        up_weight_grad,
        down_weight_grad,
    )


def solution(mesh):
    rows = P((OWNER, SHARD), None)
    line = P((OWNER, SHARD))
    part = P(SHARD)
    wide = P(SHARD, None)
    into = P(OWNER, SHARD, None)
    back = P(OWNER, None, SHARD)
    in_specs = (rows,) * 3 + (part, wide, wide, wide, part, part, wide, part, wide)
    in_specs = in_specs + (into, into, back, rows)
    out_specs = (rows, rows, line, rows, rows, rows, line, line, rows, line, rows)
    out_specs = out_specs + (into, into, back)

    return jax.shard_map(local, mesh=mesh, in_specs=in_specs, out_specs=out_specs, check_vma=False)
```

```python
import functools

import jax
import jax.numpy as jnp
from jax import lax
from jax.experimental import pallas as pl
from jax.experimental.pallas import tpu as pltpu
from jax.sharding import PartitionSpec as P


HEADS = 16
HEAD_DIM = 128
EXP_DEV = 2
OWNER = "expert"
SHARD = "wshard"


epsilon = 1e-05
theta_base = 10000.0


def rms_unit(activation):
    inverse = lax.rsqrt(jnp.mean(activation * activation, axis=-1, keepdims=True) + epsilon)
    return (activation * inverse, inverse)


def rms_backward(grad_out, normed, inverse, gain):
    gain_grad = jnp.sum(grad_out * normed, axis=0)
    grad_normed = grad_out * gain
    centred = grad_normed - normed * jnp.mean(grad_normed * normed, axis=-1, keepdims=True)
    return (inverse * centred, gain_grad)


def block_tables(lengths, rows):
    ends = jnp.cumsum(lengths, axis=1)
    row_index = jnp.arange(rows, dtype=jnp.int32)
    passed = (row_index[None, :, None] >= ends[:, None, :]).astype(jnp.int32)
    start = jnp.sum(passed * lengths[:, None, :], axis=2)
    allowed = (row_index[None, None, :] <= row_index[None, :, None]) & (
        row_index[None, None, :] >= start[:, :, None]
    )
    offsets = (row_index[None, :] - start).reshape(-1)
    half_dim = HEAD_DIM // 2
    frequency = theta_base ** (-2.0 * jnp.arange(half_dim, dtype=jnp.float32) / HEAD_DIM)
    angles = offsets.astype(jnp.float32)[:, None] * frequency[None, :]
    return (allowed, jnp.cos(angles), jnp.sin(angles))


def rotate(rows, cosine, sine):
    half_dim = HEAD_DIM // 2
    first = rows[..., :half_dim]
    second = rows[..., half_dim:]
    cosine = cosine[None, :, :]
    sine = sine[None, :, :]
    return jnp.concatenate([first * cosine - second * sine, second * cosine + first * sine], axis=-1)


def softmax_rows(logits):
    row_max = jnp.max(logits, axis=-1, keepdims=True)
    shifted = jnp.exp(logits - row_max)
    return shifted / jnp.sum(shifted, axis=-1, keepdims=True)


def dot(a, b):
    return jnp.dot(a, b, preferred_element_type=jnp.float32)


def dot_t(a, b):
    return lax.dot_general(a, b, (((1,), (1,)), ((), ())), preferred_element_type=jnp.float32)


def t_dot(a, b):
    return lax.dot_general(a, b, (((0,), (0,)), ((), ())), preferred_element_type=jnp.float32)


def swap(values, mask, axis_name=SHARD):
    count = lax.axis_size(axis_name)
    return lax.ppermute(values, axis_name, [(i, i ^ mask) for i in range(count)])


def after(values, *others):
    return lax.optimization_barrier((values, *others))[0]


def bits_of(count):
    return [1 << k for k in range(count.bit_length() - 1)]


def gather_far(shard):
    pieces = {0: shard}
    for bit in reversed(bits_of(lax.axis_size(SHARD))[1:]):
        for mask in list(pieces):
            pieces[mask ^ bit] = swap(pieces[mask], bit)
    return pieces


def gather_near(pieces):
    pieces = dict(pieces)
    for mask in list(pieces):
        pieces[mask ^ 1] = swap(pieces[mask], 1)
    return [pieces[mask] for mask in sorted(pieces)]


def gather_pieces(shard):
    return gather_near(gather_far(shard))


def scatter_stage(blocks, bit):
    masks = sorted(blocks, reverse=True)
    arrived = {m ^ bit: swap(blocks[m].astype(jnp.bfloat16), bit) for m in masks if m & bit}
    return {m: blocks[m] + arrived[m].astype(jnp.float32) for m in arrived}


def scatter_near(blocks):
    return scatter_stage(dict(enumerate(blocks)), 1)


def scatter_far(blocks):
    for bit in bits_of(lax.axis_size(SHARD))[1:]:
        blocks = scatter_stage(blocks, bit)
    return blocks[0]


def scatter_pieces(blocks):
    return scatter_far(scatter_near(blocks))


def block_of(array, index, count, axis):
    size = array.shape[axis] // count
    return lax.dynamic_slice_in_dim(array, index * size, size, axis)


def mixed_order(array, w_index, count):
    return jnp.concatenate(
        [block_of(array, w_index ^ mask, count, array.ndim - 1) for mask in range(count)], axis=-1
    )


def pair_dot(a, b, a_axis, b_axis):
    dims = (((a_axis,), (b_axis,)), ((0, 1), (0, 1)))
    return lax.dot_general(a, b, dims, preferred_element_type=jnp.float32)


def group_sum(values):
    count = lax.axis_size(SHARD)
    blocks = values.reshape(values.shape[0], count, -1)
    total = blocks
    for mask in reversed(range(1, count)):
        arrived = swap(blocks, mask)
        total = total + jnp.stack([arrived[:, m ^ mask] for m in range(count)], axis=1)
    return total.reshape(values.shape)


def owner_bits():
    return bits_of(lax.axis_size(OWNER))[::-1]


def owner_split(values):
    return values.reshape([2] * len(owner_bits()) + list(values.shape[1:]))


def owner_stage(values, left, bit):
    index = (lax.axis_index(OWNER) // bit) % 2
    axis = left.index(bit)
    away = lax.dynamic_index_in_dim(values, 1 - index, axis, keepdims=False)
    kept = lax.dynamic_index_in_dim(values, index, axis, keepdims=False)
    arrived = swap(away, bit, OWNER)
    total = kept.astype(jnp.float32) + arrived.astype(jnp.float32)
    return total.astype(jnp.bfloat16), [b for b in left if b != bit]


def owner_scatter(values):
    values, left = owner_split(values), owner_bits()
    for bit in left[::-1]:
        values, left = owner_stage(values, left, bit)
    return values


def owner_scatter_pair(first, second):
    first, second = owner_split(first), owner_split(second)
    left, left_two = owner_bits(), owner_bits()
    order = left[::-1]
    for bit, bit_two in zip(order, order[1:] + order[:1]):
        first, left = owner_stage(first, left, bit)
        second, left_two = owner_stage(second, left_two, bit_two)
        first, second = lax.optimization_barrier((first, second))
    return first, second


def place_kernel(values_ref, *out_refs):
    parts, _, cols = values_ref.shape
    cols = cols // 3
    for k in range(3):
        for p in range(parts):
            out_refs[k][:, p * cols : (p + 1) * cols] = values_ref[
                p, :, k * cols : (k + 1) * cols
            ].astype(jnp.float32)


def place(values):
    parts, rows, cols = values.shape
    shape = jax.ShapeDtypeStruct((rows, parts * cols // 3), jnp.float32)
    return pl.pallas_call(place_kernel, out_shape=[shape] * 3)(values)


def expert_hidden_kernel(parts, x_ref, cot_ref, weight_ref, *refs):
    gates, ups, downs = refs[:parts], refs[parts : 2 * parts], refs[2 * parts : 3 * parts]
    hidden_ref, gate_grad_ref, up_grad_ref, route_ref = refs[3 * parts :]
    cols = gates[0].shape[0]
    f32 = jnp.float32
    gate_lin = up_lin = back = 0.0
    for m in range(parts):
        x = x_ref[:, m * cols : (m + 1) * cols]
        gate_lin = gate_lin + jnp.dot(x, gates[m][...], preferred_element_type=f32)
        up_lin = up_lin + jnp.dot(x, ups[m][...], preferred_element_type=f32)
        back = back + dot_t(cot_ref[:, m * cols : (m + 1) * cols], downs[m][...])
    weight = weight_ref[...]
    sigmoid = jax.nn.sigmoid(gate_lin)
    swish = gate_lin * sigmoid
    hidden = swish * up_lin
    product = hidden * back
    route = product[:, :128]
    for k in range(1, product.shape[1] // 128):
        route = route + product[:, k * 128 : (k + 1) * 128]
    hidden_ref[...] = (hidden * weight).astype(jnp.bfloat16)
    grad = back * weight
    gate_grad_ref[...] = (grad * up_lin * sigmoid * (1.0 + gate_lin * (1.0 - sigmoid))).astype(
        jnp.bfloat16
    )
    up_grad_ref[...] = (grad * swish).astype(jnp.bfloat16)

    @pl.when(pl.program_id(2) == 0)
    def _():
        route_ref[...] = route

    @pl.when(pl.program_id(2) > 0)
    def _():
        route_ref[...] += route


def row_tile_of(rows):
    return min(rows, 1024)


def expert_hidden(x, cot, weights, gates, ups, downs, tile=256):
    rows, width = x.shape
    parts = len(gates)
    count, cols, ff = gates[0].shape
    row_tile = row_tile_of(rows)
    steps = ff // tile
    row_spec = pl.BlockSpec((row_tile, width), lambda r, e, f: (r, 0))
    in_piece = pl.BlockSpec((None, cols, tile), lambda r, e, f: (e, 0, f))
    out_piece = pl.BlockSpec((None, tile, cols), lambda r, e, f: (e, f, 0))
    wide_spec = pl.BlockSpec((row_tile, tile), lambda r, e, f: (r, e * steps + f))
    wide = jax.ShapeDtypeStruct((rows, count * ff), jnp.bfloat16)
    return pl.pallas_call(
functools.partial(expert_hidden_kernel, parts),
grid=(rows // row_tile, count, steps),
in_specs=[row_spec, row_spec, pl.BlockSpec((None, row_tile, 1), lambda r, e, f: (e, r, 0))]
+ [in_piece] * (2 * parts)
+ [out_piece] * parts,
out_specs=[wide_spec] * 3
+ [pl.BlockSpec((None, row_tile, 128), lambda r, e, f: (e, r, 0))],
out_shape=[wide] * 3 + [jax.ShapeDtypeStruct((count, rows, 128), jnp.float32)],
compiler_params=pltpu.CompilerParams(vmem_limit_bytes=60 * 1024 * 1024),
    )(x, cot, weights, *gates, *ups, *downs)


def back_rows_kernel(parts, gate_grad_ref, up_grad_ref, *refs):
    gates, ups = refs[:parts], refs[parts : 2 * parts]
    out_ref, sum_ref = refs[2 * parts :]
    cols = gates[0].shape[0]
    step = pl.program_id(1) * pl.num_programs(2) + pl.program_id(2)
    last = pl.num_programs(1) * pl.num_programs(2) - 1
    for m in range(parts):
        at = slice(m * cols, (m + 1) * cols)
        part = dot_t(gate_grad_ref[...], gates[m][...]) + dot_t(up_grad_ref[...], ups[m][...])

        @pl.when(step == 0)
        def _():
            sum_ref[:, at] = part

        @pl.when((step > 0) & (step < last))
        def _():
            sum_ref[:, at] += part

        @pl.when(step == last)
        def _():
            out_ref[:, at] = (sum_ref[:, at] + part).astype(jnp.bfloat16)


def back_rows(gate_grad, up_grad, gates, ups, tile=512):
    rows = gate_grad.shape[0]
    parts = len(gates)
    count, cols, ff = gates[0].shape
    row_tile = row_tile_of(rows)
    steps = ff // tile
    wide_spec = pl.BlockSpec((row_tile, tile), lambda r, e, f: (r, e * steps + f))
    piece = pl.BlockSpec((None, cols, tile), lambda r, e, f: (e, 0, f))
    return pl.pallas_call(
functools.partial(back_rows_kernel, parts),
grid=(rows // row_tile, count, steps),
in_specs=[wide_spec] * 2 + [piece] * (2 * parts),
out_specs=pl.BlockSpec((row_tile, parts * cols), lambda r, e, f: (r, 0)),
out_shape=jax.ShapeDtypeStruct((rows, parts * cols), jnp.bfloat16),
scratch_shapes=[pltpu.VMEM((row_tile, parts * cols), jnp.float32)],
compiler_params=pltpu.CompilerParams(vmem_limit_bytes=60 * 1024 * 1024),
    )(gate_grad, up_grad, *gates, *ups)


def local(
    tokens,
    doc_lengths,
    expert_ids,
    attn_gain,
    query_weight,
    key_weight,
    value_weight,
    query_gain,
    key_gain,
    output_weight,
    ffn_gain,
    router_weight,
    gate_weight,
    up_weight,
    down_weight,
    cotangent,
):
    bf16 = jnp.bfloat16
    f32 = jnp.float32
    rows, width = tokens.shape
    owners = lax.axis_size(OWNER)
    parts = lax.axis_size(SHARD)
    w_index = lax.axis_index(SHARD)
    experts = EXP_DEV * owners
    group = parts * rows
    cols = width // parts
    heads = HEADS // parts
    final_rows = width // (owners * parts)
    ff = gate_weight.shape[2]

    e_index = lax.axis_index(OWNER)
    half = cols // 2
    unit = 2 * w_index + e_index % 2
    units = 2 * parts

    docs = doc_lengths.shape[1]
    lengths_row = jnp.zeros((1, cols), bf16).at[:, :docs].set(doc_lengths.astype(bf16))
    small = jnp.concatenate(
        [attn_gain[None, :], ffn_gain[None, :], lengths_row, router_weight.T], axis=0
    )
    small_all = lax.all_gather(small, SHARD, axis=0)
    attn_gain_all = small_all[:, 0, :].reshape(width).astype(f32)
    ffn_gain_all = small_all[:, 1, :].reshape(width).astype(f32)
    lengths_all = small_all[:, 2, :docs].astype(jnp.int32)
    lengths_all = jnp.concatenate([block_of(lengths_all, w_index ^ m, parts, 0) for m in range(parts)])
    router_t = small_all[:, 3:, :].transpose(1, 0, 2).reshape(experts, width)

    *weights_in, tokens_in, _ = lax.optimization_barrier(
        (query_weight, key_weight, value_weight, tokens, small_all)
    )
    tokens_far = gather_far(tokens_in)
    tokens_all = jnp.concatenate(gather_near(tokens_far), axis=0)
    pieces = [None] * units
    for mask in reversed(range(parts)):
        piece = jnp.concatenate(
            [block_of(weight, w_index ^ mask, parts, 1) for weight in weights_in], axis=1
        )
        for side in range(2):
            pieces[2 * mask + side] = block_of(piece, side ^ (e_index % 2), 2, 0)
    for mask in reversed(range(1, parts)):
        pieces[2 * mask] = swap(pieces[2 * mask], mask)
        if mask == 1:
            pieces[3] = swap(pieces[3], 1)
    for mask in reversed(range(2, parts)):
        pieces[2 * mask + 1] = swap(pieces[2 * mask], 1, OWNER)
    cot_b = mixed_order(cotangent, w_index, parts).astype(bf16)
    cot_all = lax.all_gather(cot_b, OWNER, axis=0, tiled=True)
    down_in = after(down_weight, pieces[4])
    down_far = gather_far(down_in)

    unit_all, _ = rms_unit(tokens_all.astype(f32))
    attn_in = (unit_all * attn_gain_all).astype(bf16)
    attn_in_mixed = mixed_order(attn_in, unit, units)
    qkv = 0.0
    for at in [0, 1, 2, 3] + [2 * m for m in range(2, parts)] + [2 * m + 1 for m in range(2, parts)]:
        qkv = qkv + dot(attn_in_mixed[:, at * half : (at + 1) * half], pieces[at])
    query_lin, key_lin, value_lin = (qkv[:, i * cols : (i + 1) * cols] for i in range(3))
    squares = jnp.stack(
        [jnp.sum(query_lin * query_lin, axis=1), jnp.sum(key_lin * key_lin, axis=1)], axis=0
    )
    squares = group_sum(squares)
    inverses = lax.rsqrt(squares / width + epsilon)
    query_inverse = inverses[0][:, None]
    key_inverse = inverses[1][:, None]
    query_unit = query_lin * query_inverse
    key_unit = key_lin * key_inverse
    query_gain_f = query_gain.astype(f32)
    key_gain_f = key_gain.astype(f32)
    allowed, cosine, sine = block_tables(lengths_all, rows)
    scale = HEAD_DIM ** (-0.5)

    def by_head(array):
        return jnp.stack(
            [array[:, h * HEAD_DIM : (h + 1) * HEAD_DIM] for h in range(heads)], axis=0
        )

    def by_row(array):
        return jnp.concatenate([array[h] for h in range(heads)], axis=1)

    blocked = (heads, parts, rows, HEAD_DIM)
    whole = (heads, group, HEAD_DIM)
    queries = rotate(by_head(query_unit * query_gain_f), cosine, sine).astype(bf16)
    queries = queries.reshape(blocked)
    keys = rotate(by_head(key_unit * key_gain_f), cosine, sine).astype(bf16).reshape(blocked)
    values = by_head(value_lin).astype(bf16).reshape(blocked)
    scores = pair_dot(queries, keys, 3, 3) * scale
    scores = jnp.where(allowed[None, :, :, :], scores, -1e30)
    row_max = jnp.max(scores, axis=-1, keepdims=True)
    log_total = row_max + jnp.log(jnp.sum(jnp.exp(scores - row_max), axis=-1, keepdims=True))
    probs = jnp.exp(scores - log_total)
    probs_b = probs.astype(bf16)
    mixed = pair_dot(probs_b, values, 3, 2).astype(bf16)
    attn_mix = by_row(mixed.reshape(whole))
    attn_out = dot(attn_mix, output_weight)
    attn_out = scatter_pieces([attn_out[mask * rows : (mask + 1) * rows] for mask in range(parts)])
    attn_out, *pieces = lax.optimization_barrier((attn_out, *pieces))
    qkv_w = jnp.concatenate(pieces, axis=0)
    qkv_w = jnp.concatenate(
        [block_of(qkv_w, unit ^ k, units, 0) for k in range(units)], axis=0
    )

    residual = tokens.astype(f32)
    middle = residual + attn_out
    unit_two, inverse_two = rms_unit(middle)
    ffn_in = (unit_two * ffn_gain_all).astype(bf16)
    ffn_in_mixed = mixed_order(ffn_in, w_index, parts)
    gate_in, up_in, ffn_in_mixed, ffn_in = lax.optimization_barrier(
        (gate_weight, up_weight, ffn_in_mixed, ffn_in)
    )
    gate_far = gather_far(gate_in)
    up_far = gather_far(up_in)
    router_probs = softmax_rows(dot_t(ffn_in, router_t))
    expert_range = jnp.arange(experts, dtype=jnp.int32)
    named = jnp.any(expert_ids[:, :, None] == expert_range[None, None, :], axis=1)
    route_table = jnp.where(named, router_probs, 0.0)

    arrived = lax.all_gather(ffn_in_mixed, OWNER, axis=0, tiled=True)
    weights = lax.all_to_all(
        route_table.reshape(rows, owners, EXP_DEV).transpose(1, 2, 0),
        OWNER,
        split_axis=0,
        concat_axis=0,
        tiled=True,
    )
    weights = weights.transpose(1, 0, 2).reshape(EXP_DEV, owners * rows, 1)
    gate_pieces = gather_near(gate_far)
    up_pieces = gather_near(
        {m: after(p, weights, gate_pieces[-1]) if m else p for m, p in up_far.items()}
    )
    down_pieces = gather_near({m: after(p, attn_out) if m else p for m, p in down_far.items()})
    hidden_w, gate_grad_b, up_grad_b, route_part = expert_hidden(
        arrived, cot_all, weights, gate_pieces, up_pieces, down_pieces
    )
    row_partial = back_rows(gate_grad_b, up_grad_b, gate_pieces, up_pieces)
    row_grads = lax.psum_scatter(row_partial, OWNER, scatter_dimension=0, tiled=True)
    route_back = jnp.sum(route_part, axis=2)
    route_back = lax.all_to_all(
        route_back.reshape(EXP_DEV, owners, rows).transpose(1, 0, 2),
        OWNER,
        split_axis=0,
        concat_axis=0,
        tiled=True,
    )
    part_of = lambda array, mask: array[:, mask * cols : (mask + 1) * cols]
    order = sorted(range(parts), key=lambda m: (m < parts // 2, -m))

    def ordered_blocks(make):
        blocks = [None] * parts
        for mask in order:
            blocks[mask] = make(mask)
        return blocks

    gate_blocks = ordered_blocks(lambda m: t_dot(part_of(arrived, m), gate_grad_b))
    gate_near = scatter_near(gate_blocks)
    up_blocks = ordered_blocks(lambda m: t_dot(part_of(arrived, m), up_grad_b))
    up_near = scatter_near(up_blocks)
    hidden_w, qkv_w, *_ = lax.optimization_barrier((hidden_w, qkv_w, *gate_blocks, *up_blocks))
    down_blocks = ordered_blocks(lambda m: t_dot(hidden_w, part_of(cot_all, m)))
    down_near = scatter_near(down_blocks)
    gate_sum = scatter_far(gate_near)
    gate_weight_grad = jnp.stack([gate_sum[:, e * ff : (e + 1) * ff] for e in range(EXP_DEV)])
    down_all = jnp.concatenate(
        [piece.reshape(EXP_DEV * ff, cols) for piece in down_pieces], axis=1
    )
    out_partial = dot(hidden_w, down_all)
    out_partial = out_partial.astype(bf16)
    row_grads, route_back = lax.optimization_barrier((row_grads, route_back))
    moe_out = owner_scatter(out_partial.reshape(owners, rows, width))

    route_grad = route_back.reshape(experts, rows).T
    prob_grad = jnp.where(named, route_grad, 0.0)
    logit_grad = router_probs * (
        prob_grad - jnp.sum(router_probs * prob_grad, axis=1, keepdims=True)
    )
    logit_grad_b = logit_grad.astype(bf16)
    ffn_in_grad = mixed_order(row_grads, w_index, parts).astype(f32) + dot(logit_grad_b, router_t)
    middle_part, ffn_gain_grad = rms_backward(ffn_in_grad, unit_two, inverse_two, ffn_gain_all)
    middle_grad = cotangent + middle_part
    router_grad = t_dot(logit_grad_b, ffn_in)

    mid_pieces = gather_pieces(middle_grad.astype(bf16))
    mid_all = jnp.concatenate(mid_pieces, axis=0)
    output_part = t_dot(attn_mix, mid_all).astype(bf16)
    output_sum = owner_scatter(output_part.reshape(owners, final_rows, width))
    mix_grad = by_head(dot_t(mid_all, output_weight).astype(bf16)).reshape(blocked)
    delta = jnp.sum(mix_grad.astype(f32) * mixed.astype(f32), axis=-1, keepdims=True)
    prob_back = pair_dot(mix_grad, values, 3, 3)
    score_grad = (probs * (prob_back - delta)).astype(bf16)
    grad_queries = pair_dot(score_grad, keys, 3, 2)
    grad_keys = pair_dot(score_grad, queries, 2, 2)
    grad_values = pair_dot(probs_b, mix_grad, 2, 2)
    grad_queries = by_row(rotate((grad_queries * scale).reshape(whole), cosine, -sine))
    grad_keys = by_row(rotate((grad_keys * scale).reshape(whole), cosine, -sine))
    query_gain_grad = jnp.sum(grad_queries * query_unit, axis=0)
    key_gain_grad = jnp.sum(grad_keys * key_unit, axis=0)
    grad_queries = grad_queries * query_gain_f
    grad_keys = grad_keys * key_gain_f
    means = jnp.stack(
        [jnp.sum(grad_queries * query_unit, axis=1), jnp.sum(grad_keys * key_unit, axis=1)], axis=0
    )
    means = group_sum(means) / width
    up_sum = scatter_far(after(up_near, means))
    up_weight_grad = jnp.stack([up_sum[:, e * ff : (e + 1) * ff] for e in range(EXP_DEV)])
    query_grad_b = (query_inverse * (grad_queries - query_unit * means[0][:, None])).astype(bf16)
    key_grad_b = (key_inverse * (grad_keys - key_unit * means[1][:, None])).astype(bf16)
    value_grad_b = by_row(grad_values.reshape(whole)).astype(bf16)
    qkv_grad = jnp.concatenate([query_grad_b, key_grad_b, value_grad_b], axis=1)
    query_part = t_dot(attn_in, query_grad_b)
    key_part = t_dot(attn_in, key_grad_b)
    query_part, key_part = query_part.astype(bf16), key_part.astype(bf16)
    qkv_grad = after(qkv_grad, query_part, key_part)
    attn_in_part = dot_t(qkv_grad, qkv_w)
    attn_in_grad = scatter_pieces(
        [attn_in_part[mask * rows : (mask + 1) * rows] for mask in range(parts)]
    )
    value_part = t_dot(attn_in, value_grad_b).astype(bf16).reshape(owners, parts * final_rows, cols)
    down_weight_grad = scatter_far(after(down_near, attn_in_part)).reshape(EXP_DEV, ff, cols)
    value_sum = owner_scatter(value_part)
    cut = (owners, parts * final_rows, cols)
    query_sum, key_sum = owner_scatter_pair(query_part.reshape(cut), key_part.reshape(cut))

    unit_one, inverse_one = rms_unit(residual)
    input_part, attn_gain_grad = rms_backward(
        attn_in_grad, unit_one, inverse_one, attn_gain_all
    )
    tokens_grad = middle_grad + input_part
    moe_out = after(moe_out, attn_in_part)
    block_output = middle + mixed_order(moe_out, w_index, parts).astype(f32)

    qkv_sum = jnp.concatenate([query_sum, key_sum, value_sum], axis=1)
    qkv_sum = qkv_sum.reshape(parts, final_rows, 3 * cols)
    qkv_sum = lax.all_to_all(qkv_sum, SHARD, split_axis=0, concat_axis=0, tiled=True)
    qkv_sum = place(qkv_sum)
    moves = []
    for e in range(owners):
        for w in range(parts):
            moves.append((e * parts + w, w * owners + e))
    output_sum = lax.ppermute(output_sum, (OWNER, SHARD), moves).astype(f32)

    own = jnp.zeros((2, parts, cols), f32)
    own = lax.dynamic_update_slice(
        own, jnp.stack([query_gain_grad, key_gain_grad])[:, None, :], (0, w_index, 0)
    ).reshape(2, width)
    table = jnp.concatenate([attn_gain_grad[None], ffn_gain_grad[None], own, router_grad], axis=0)
    count = table.shape[0]
    table = table.reshape(count, owners, parts * final_rows).transpose(1, 0, 2)
    table = lax.all_to_all(table, OWNER, split_axis=0, concat_axis=0, tiled=True)
    table = jnp.sum(table, axis=0)
    table = table.reshape(count, parts, final_rows).transpose(1, 0, 2)
    table = jnp.sum(
        lax.all_to_all(table, SHARD, split_axis=0, concat_axis=0, tiled=True), axis=0
    )
    return (
        block_output,
        tokens_grad,
        table[0],
        qkv_sum[0],
        qkv_sum[1],
        qkv_sum[2],
        table[2],
        table[3],
        output_sum,
        table[1],
        table[4:].T,
        gate_weight_grad,
        up_weight_grad,
        down_weight_grad,
    )


def solution(mesh):
    rows = P((OWNER, SHARD), None)
    line = P((OWNER, SHARD))
    part = P(SHARD)
    wide = P(SHARD, None)
    into = P(OWNER, SHARD, None)
    back = P(OWNER, None, SHARD)
    in_specs = (rows,) * 3 + (part, wide, wide, wide, part, part, wide, part, wide)
    in_specs = in_specs + (into, into, back, rows)
    out_specs = (rows, rows, line, rows, rows, rows, line, line, rows, line, rows)
    out_specs = out_specs + (into, into, back)

    return jax.shard_map(local, mesh=mesh, in_specs=in_specs, out_specs=out_specs, check_vma=False)
```

```python
import functools

import jax
import jax.numpy as jnp
from jax import lax
from jax.experimental import pallas as pl
from jax.experimental.pallas import tpu as pltpu
from jax.sharding import PartitionSpec as P


HEADS = 16
HEAD_DIM = 128
EXP_DEV = 2
OWNER = "expert"
SHARD = "wshard"


epsilon = 1e-05
theta_base = 10000.0


def rms_unit(activation):
    inverse = lax.rsqrt(jnp.mean(activation * activation, axis=-1, keepdims=True) + epsilon)
    return (activation * inverse, inverse)


def rms_backward(grad_out, normed, inverse, gain):
    gain_grad = jnp.sum(grad_out * normed, axis=0)
    grad_normed = grad_out * gain
    centred = grad_normed - normed * jnp.mean(grad_normed * normed, axis=-1, keepdims=True)
    return (inverse * centred, gain_grad)


def block_tables(lengths, rows):
    ends = jnp.cumsum(lengths, axis=1)
    row_index = jnp.arange(rows, dtype=jnp.int32)
    passed = (row_index[None, :, None] >= ends[:, None, :]).astype(jnp.int32)
    start = jnp.sum(passed * lengths[:, None, :], axis=2)
    allowed = (row_index[None, None, :] <= row_index[None, :, None]) & (
        row_index[None, None, :] >= start[:, :, None]
    )
    offsets = (row_index[None, :] - start).reshape(-1)
    half_dim = HEAD_DIM // 2
    frequency = theta_base ** (-2.0 * jnp.arange(half_dim, dtype=jnp.float32) / HEAD_DIM)
    angles = offsets.astype(jnp.float32)[:, None] * frequency[None, :]
    return (allowed, jnp.cos(angles), jnp.sin(angles))


def rotate(rows, cosine, sine):
    half_dim = HEAD_DIM // 2
    first = rows[..., :half_dim]
    second = rows[..., half_dim:]
    cosine = cosine[None, :, :]
    sine = sine[None, :, :]
    return jnp.concatenate([first * cosine - second * sine, second * cosine + first * sine], axis=-1)


def softmax_rows(logits):
    row_max = jnp.max(logits, axis=-1, keepdims=True)
    shifted = jnp.exp(logits - row_max)
    return shifted / jnp.sum(shifted, axis=-1, keepdims=True)


def dot(a, b):
    return jnp.dot(a, b, preferred_element_type=jnp.float32)


def dot_t(a, b):
    return lax.dot_general(a, b, (((1,), (1,)), ((), ())), preferred_element_type=jnp.float32)


def t_dot(a, b):
    return lax.dot_general(a, b, (((0,), (0,)), ((), ())), preferred_element_type=jnp.float32)


def swap(values, mask, axis_name=SHARD):
    count = lax.axis_size(axis_name)
    return lax.ppermute(values, axis_name, [(i, i ^ mask) for i in range(count)])


def after(values, *others):
    return lax.optimization_barrier((values, *others))[0]


def bits_of(count):
    return [1 << k for k in range(count.bit_length() - 1)]


def gather_far(shard):
    pieces = {0: shard}
    for bit in reversed(bits_of(lax.axis_size(SHARD))[1:]):
        for mask in list(pieces):
            pieces[mask ^ bit] = swap(pieces[mask], bit)
    return pieces


def gather_near(pieces):
    pieces = dict(pieces)
    for mask in list(pieces):
        pieces[mask ^ 1] = swap(pieces[mask], 1)
    return [pieces[mask] for mask in sorted(pieces)]


def gather_pieces(shard):
    return gather_near(gather_far(shard))


def scatter_stage(blocks, bit):
    masks = sorted(blocks, reverse=True)
    arrived = {m ^ bit: swap(blocks[m].astype(jnp.bfloat16), bit) for m in masks if m & bit}
    return {m: blocks[m] + arrived[m].astype(jnp.float32) for m in arrived}


def scatter_near(blocks):
    return scatter_stage(dict(enumerate(blocks)), 1)


def scatter_far(blocks):
    for bit in bits_of(lax.axis_size(SHARD))[1:]:
        blocks = scatter_stage(blocks, bit)
    return blocks[0]


def scatter_pieces(blocks):
    return scatter_far(scatter_near(blocks))


def block_of(array, index, count, axis):
    size = array.shape[axis] // count
    return lax.dynamic_slice_in_dim(array, index * size, size, axis)


def mixed_order(array, w_index, count):
    return jnp.concatenate(
        [block_of(array, w_index ^ mask, count, array.ndim - 1) for mask in range(count)], axis=-1
    )


def pair_dot(a, b, a_axis, b_axis):
    dims = (((a_axis,), (b_axis,)), ((0, 1), (0, 1)))
    return lax.dot_general(a, b, dims, preferred_element_type=jnp.float32)


def group_sum(values):
    count = lax.axis_size(SHARD)
    blocks = values.reshape(values.shape[0], count, -1)
    total = blocks
    for mask in reversed(range(1, count)):
        arrived = swap(blocks, mask)
        total = total + jnp.stack([arrived[:, m ^ mask] for m in range(count)], axis=1)
    return total.reshape(values.shape)


def owner_bits():
    return bits_of(lax.axis_size(OWNER))[::-1]


def owner_split(values):
    return values.reshape([2] * len(owner_bits()) + list(values.shape[1:]))


def owner_stage(values, left, bit):
    index = (lax.axis_index(OWNER) // bit) % 2
    axis = left.index(bit)
    away = lax.dynamic_index_in_dim(values, 1 - index, axis, keepdims=False)
    kept = lax.dynamic_index_in_dim(values, index, axis, keepdims=False)
    arrived = swap(away, bit, OWNER)
    total = kept.astype(jnp.float32) + arrived.astype(jnp.float32)
    return total.astype(jnp.bfloat16), [b for b in left if b != bit]


def owner_scatter(values):
    values, left = owner_split(values), owner_bits()
    for bit in left[::-1]:
        values, left = owner_stage(values, left, bit)
    return values


def place_kernel(values_ref, *out_refs):
    parts, _, cols = values_ref.shape
    cols = cols // 3
    for k in range(3):
        for p in range(parts):
            out_refs[k][:, p * cols : (p + 1) * cols] = values_ref[
                p, :, k * cols : (k + 1) * cols
            ].astype(jnp.float32)


def place(values):
    parts, rows, cols = values.shape
    shape = jax.ShapeDtypeStruct((rows, parts * cols // 3), jnp.float32)
    return pl.pallas_call(place_kernel, out_shape=[shape] * 3)(values)


def expert_hidden_kernel(parts, x_ref, cot_ref, weight_ref, *refs):
    gates, ups, downs = refs[:parts], refs[parts : 2 * parts], refs[2 * parts : 3 * parts]
    hidden_ref, gate_grad_ref, up_grad_ref, route_ref = refs[3 * parts :]
    cols = gates[0].shape[0]
    f32 = jnp.float32
    gate_lin = up_lin = back = 0.0
    for m in range(parts):
        x = x_ref[:, m * cols : (m + 1) * cols]
        gate_lin = gate_lin + jnp.dot(x, gates[m][...], preferred_element_type=f32)
        up_lin = up_lin + jnp.dot(x, ups[m][...], preferred_element_type=f32)
        back = back + dot_t(cot_ref[:, m * cols : (m + 1) * cols], downs[m][...])
    weight = weight_ref[...]
    sigmoid = jax.nn.sigmoid(gate_lin)
    swish = gate_lin * sigmoid
    hidden = swish * up_lin
    product = hidden * back
    route = product[:, :128]
    for k in range(1, product.shape[1] // 128):
        route = route + product[:, k * 128 : (k + 1) * 128]
    hidden_ref[...] = (hidden * weight).astype(jnp.bfloat16)
    grad = back * weight
    gate_grad_ref[...] = (grad * up_lin * sigmoid * (1.0 + gate_lin * (1.0 - sigmoid))).astype(
        jnp.bfloat16
    )
    up_grad_ref[...] = (grad * swish).astype(jnp.bfloat16)

    @pl.when(pl.program_id(2) == 0)
    def _():
        route_ref[...] = route

    @pl.when(pl.program_id(2) > 0)
    def _():
        route_ref[...] += route


def row_tile_of(rows):
    return min(rows, 1024)


def expert_hidden(x, cot, weights, gates, ups, downs, tile=256):
    rows, width = x.shape
    parts = len(gates)
    count, cols, ff = gates[0].shape
    row_tile = row_tile_of(rows)
    steps = ff // tile
    row_spec = pl.BlockSpec((row_tile, width), lambda r, e, f: (r, 0))
    in_piece = pl.BlockSpec((None, cols, tile), lambda r, e, f: (e, 0, f))
    out_piece = pl.BlockSpec((None, tile, cols), lambda r, e, f: (e, f, 0))
    wide_spec = pl.BlockSpec((row_tile, tile), lambda r, e, f: (r, e * steps + f))
    wide = jax.ShapeDtypeStruct((rows, count * ff), jnp.bfloat16)
    return pl.pallas_call(
functools.partial(expert_hidden_kernel, parts),
grid=(rows // row_tile, count, steps),
in_specs=[row_spec, row_spec, pl.BlockSpec((None, row_tile, 1), lambda r, e, f: (e, r, 0))]
+ [in_piece] * (2 * parts)
+ [out_piece] * parts,
out_specs=[wide_spec] * 3
+ [pl.BlockSpec((None, row_tile, 128), lambda r, e, f: (e, r, 0))],
out_shape=[wide] * 3 + [jax.ShapeDtypeStruct((count, rows, 128), jnp.float32)],
compiler_params=pltpu.CompilerParams(vmem_limit_bytes=60 * 1024 * 1024),
    )(x, cot, weights, *gates, *ups, *downs)


def back_rows_kernel(parts, gate_grad_ref, up_grad_ref, *refs):
    gates, ups = refs[:parts], refs[parts : 2 * parts]
    out_ref, sum_ref = refs[2 * parts :]
    cols = gates[0].shape[0]
    step = pl.program_id(1) * pl.num_programs(2) + pl.program_id(2)
    last = pl.num_programs(1) * pl.num_programs(2) - 1
    for m in range(parts):
        at = slice(m * cols, (m + 1) * cols)
        part = dot_t(gate_grad_ref[...], gates[m][...]) + dot_t(up_grad_ref[...], ups[m][...])

        @pl.when(step == 0)
        def _():
            sum_ref[:, at] = part

        @pl.when((step > 0) & (step < last))
        def _():
            sum_ref[:, at] += part

        @pl.when(step == last)
        def _():
            out_ref[:, at] = (sum_ref[:, at] + part).astype(jnp.bfloat16)


def back_rows(gate_grad, up_grad, gates, ups, tile=512):
    rows = gate_grad.shape[0]
    parts = len(gates)
    count, cols, ff = gates[0].shape
    row_tile = row_tile_of(rows)
    steps = ff // tile
    wide_spec = pl.BlockSpec((row_tile, tile), lambda r, e, f: (r, e * steps + f))
    piece = pl.BlockSpec((None, cols, tile), lambda r, e, f: (e, 0, f))
    return pl.pallas_call(
functools.partial(back_rows_kernel, parts),
grid=(rows // row_tile, count, steps),
in_specs=[wide_spec] * 2 + [piece] * (2 * parts),
out_specs=pl.BlockSpec((row_tile, parts * cols), lambda r, e, f: (r, 0)),
out_shape=jax.ShapeDtypeStruct((rows, parts * cols), jnp.bfloat16),
scratch_shapes=[pltpu.VMEM((row_tile, parts * cols), jnp.float32)],
compiler_params=pltpu.CompilerParams(vmem_limit_bytes=60 * 1024 * 1024),
    )(gate_grad, up_grad, *gates, *ups)


def local(
    tokens,
    doc_lengths,
    expert_ids,
    attn_gain,
    query_weight,
    key_weight,
    value_weight,
    query_gain,
    key_gain,
    output_weight,
    ffn_gain,
    router_weight,
    gate_weight,
    up_weight,
    down_weight,
    cotangent,
):
    bf16 = jnp.bfloat16
    f32 = jnp.float32
    rows, width = tokens.shape
    owners = lax.axis_size(OWNER)
    parts = lax.axis_size(SHARD)
    w_index = lax.axis_index(SHARD)
    experts = EXP_DEV * owners
    group = parts * rows
    cols = width // parts
    heads = HEADS // parts
    final_rows = width // (owners * parts)
    ff = gate_weight.shape[2]

    e_index = lax.axis_index(OWNER)
    half = cols // 2
    unit = 2 * w_index + e_index % 2
    units = 2 * parts

    docs = doc_lengths.shape[1]
    lengths_row = jnp.zeros((1, cols), bf16).at[:, :docs].set(doc_lengths.astype(bf16))
    small = jnp.concatenate(
        [attn_gain[None, :], ffn_gain[None, :], lengths_row, router_weight.T], axis=0
    )
    small_all = lax.all_gather(small, SHARD, axis=0)
    attn_gain_all = small_all[:, 0, :].reshape(width).astype(f32)
    ffn_gain_all = small_all[:, 1, :].reshape(width).astype(f32)
    lengths_all = small_all[:, 2, :docs].astype(jnp.int32)
    lengths_all = jnp.concatenate([block_of(lengths_all, w_index ^ m, parts, 0) for m in range(parts)])
    router_t = small_all[:, 3:, :].transpose(1, 0, 2).reshape(experts, width)

    *weights_in, tokens_in, _ = lax.optimization_barrier(
        (query_weight, key_weight, value_weight, tokens, small_all)
    )
    tokens_far = gather_far(tokens_in)
    tokens_all = jnp.concatenate(gather_near(tokens_far), axis=0)
    pieces = [None] * units
    for mask in reversed(range(parts)):
        piece = jnp.concatenate(
            [block_of(weight, w_index ^ mask, parts, 1) for weight in weights_in], axis=1
        )
        for side in range(2):
            pieces[2 * mask + side] = block_of(piece, side ^ (e_index % 2), 2, 0)
    for mask in reversed(range(1, parts)):
        pieces[2 * mask] = swap(pieces[2 * mask], mask)
        if mask == 1:
            pieces[3] = swap(pieces[3], 1)
    for mask in reversed(range(2, parts)):
        pieces[2 * mask + 1] = swap(pieces[2 * mask], 1, OWNER)
    cot_b = mixed_order(cotangent, w_index, parts).astype(bf16)
    cot_all = lax.all_gather(cot_b, OWNER, axis=0, tiled=True)
    down_in = after(down_weight, pieces[4])
    down_far = gather_far(down_in)

    unit_all, _ = rms_unit(tokens_all.astype(f32))
    attn_in = (unit_all * attn_gain_all).astype(bf16)
    attn_in_mixed = mixed_order(attn_in, unit, units)
    qkv = 0.0
    for at in [0, 1, 2, 3] + [2 * m for m in range(2, parts)] + [2 * m + 1 for m in range(2, parts)]:
        qkv = qkv + dot(attn_in_mixed[:, at * half : (at + 1) * half], pieces[at])
    query_lin, key_lin, value_lin = (qkv[:, i * cols : (i + 1) * cols] for i in range(3))
    squares = jnp.stack(
        [jnp.sum(query_lin * query_lin, axis=1), jnp.sum(key_lin * key_lin, axis=1)], axis=0
    )
    squares = group_sum(squares)
    inverses = lax.rsqrt(squares / width + epsilon)
    query_inverse = inverses[0][:, None]
    key_inverse = inverses[1][:, None]
    query_unit = query_lin * query_inverse
    key_unit = key_lin * key_inverse
    query_gain_f = query_gain.astype(f32)
    key_gain_f = key_gain.astype(f32)
    allowed, cosine, sine = block_tables(lengths_all, rows)
    scale = HEAD_DIM ** (-0.5)

    def by_head(array):
        return jnp.stack(
            [array[:, h * HEAD_DIM : (h + 1) * HEAD_DIM] for h in range(heads)], axis=0
        )

    def by_row(array):
        return jnp.concatenate([array[h] for h in range(heads)], axis=1)

    blocked = (heads, parts, rows, HEAD_DIM)
    whole = (heads, group, HEAD_DIM)
    queries = rotate(by_head(query_unit * query_gain_f), cosine, sine).astype(bf16)
    queries = queries.reshape(blocked)
    keys = rotate(by_head(key_unit * key_gain_f), cosine, sine).astype(bf16).reshape(blocked)
    values = by_head(value_lin).astype(bf16).reshape(blocked)
    scores = pair_dot(queries, keys, 3, 3) * scale
    scores = jnp.where(allowed[None, :, :, :], scores, -1e30)
    row_max = jnp.max(scores, axis=-1, keepdims=True)
    log_total = row_max + jnp.log(jnp.sum(jnp.exp(scores - row_max), axis=-1, keepdims=True))
    probs = jnp.exp(scores - log_total)
    probs_b = probs.astype(bf16)
    mixed = pair_dot(probs_b, values, 3, 2).astype(bf16)
    attn_mix = by_row(mixed.reshape(whole))
    attn_out = dot(attn_mix, output_weight)
    attn_out = scatter_pieces([attn_out[mask * rows : (mask + 1) * rows] for mask in range(parts)])
    attn_out, *pieces = lax.optimization_barrier((attn_out, *pieces))
    qkv_w = jnp.concatenate(pieces, axis=0)
    qkv_w = jnp.concatenate(
        [block_of(qkv_w, unit ^ k, units, 0) for k in range(units)], axis=0
    )

    residual = tokens.astype(f32)
    middle = residual + attn_out
    unit_two, inverse_two = rms_unit(middle)
    ffn_in = (unit_two * ffn_gain_all).astype(bf16)
    ffn_in_mixed = mixed_order(ffn_in, w_index, parts)
    gate_in, up_in, ffn_in_mixed, ffn_in = lax.optimization_barrier(
        (gate_weight, up_weight, ffn_in_mixed, ffn_in)
    )
    gate_far = gather_far(gate_in)
    up_far = gather_far(up_in)
    router_probs = softmax_rows(dot_t(ffn_in, router_t))
    expert_range = jnp.arange(experts, dtype=jnp.int32)
    named = jnp.any(expert_ids[:, :, None] == expert_range[None, None, :], axis=1)
    route_table = jnp.where(named, router_probs, 0.0)

    arrived = lax.all_gather(ffn_in_mixed, OWNER, axis=0, tiled=True)
    weights = lax.all_to_all(
        route_table.reshape(rows, owners, EXP_DEV).transpose(1, 2, 0),
        OWNER,
        split_axis=0,
        concat_axis=0,
        tiled=True,
    )
    weights = weights.transpose(1, 0, 2).reshape(EXP_DEV, owners * rows, 1)
    gate_pieces = gather_near(gate_far)
    up_pieces = gather_near(
        {m: after(p, weights, gate_pieces[-1]) if m else p for m, p in up_far.items()}
    )
    down_pieces = gather_near({m: after(p, attn_out) if m else p for m, p in down_far.items()})
    hidden_w, gate_grad_b, up_grad_b, route_part = expert_hidden(
        arrived, cot_all, weights, gate_pieces, up_pieces, down_pieces
    )
    row_partial = back_rows(gate_grad_b, up_grad_b, gate_pieces, up_pieces)
    row_grads = lax.psum_scatter(row_partial, OWNER, scatter_dimension=0, tiled=True)
    route_back = jnp.sum(route_part, axis=2)
    route_back = lax.all_to_all(
        route_back.reshape(EXP_DEV, owners, rows).transpose(1, 0, 2),
        OWNER,
        split_axis=0,
        concat_axis=0,
        tiled=True,
    )
    part_of = lambda array, mask: array[:, mask * cols : (mask + 1) * cols]
    order = sorted(range(parts), key=lambda m: (m < parts // 2, -m))

    def ordered_blocks(make):
        blocks = [None] * parts
        for mask in order:
            blocks[mask] = make(mask)
        return blocks

    gate_blocks = ordered_blocks(lambda m: t_dot(part_of(arrived, m), gate_grad_b))
    gate_near = scatter_near(gate_blocks)
    up_blocks = ordered_blocks(lambda m: t_dot(part_of(arrived, m), up_grad_b))
    up_near = scatter_near(up_blocks)
    hidden_w, qkv_w, *_ = lax.optimization_barrier((hidden_w, qkv_w, *gate_blocks, *up_blocks))
    down_blocks = ordered_blocks(lambda m: t_dot(hidden_w, part_of(cot_all, m)))
    down_near = scatter_near(down_blocks)
    gate_sum = scatter_far(gate_near)
    gate_weight_grad = jnp.stack([gate_sum[:, e * ff : (e + 1) * ff] for e in range(EXP_DEV)])
    down_all = jnp.concatenate(
        [piece.reshape(EXP_DEV * ff, cols) for piece in down_pieces], axis=1
    )
    out_partial = dot(hidden_w, down_all)
    out_partial = out_partial.astype(bf16)
    row_grads, route_back = lax.optimization_barrier((row_grads, route_back))
    moe_out = owner_scatter(out_partial.reshape(owners, rows, width))

    route_grad = route_back.reshape(experts, rows).T
    prob_grad = jnp.where(named, route_grad, 0.0)
    logit_grad = router_probs * (
        prob_grad - jnp.sum(router_probs * prob_grad, axis=1, keepdims=True)
    )
    logit_grad_b = logit_grad.astype(bf16)
    ffn_in_grad = mixed_order(row_grads, w_index, parts).astype(f32) + dot(logit_grad_b, router_t)
    middle_part, ffn_gain_grad = rms_backward(ffn_in_grad, unit_two, inverse_two, ffn_gain_all)
    middle_grad = cotangent + middle_part
    router_grad = t_dot(logit_grad_b, ffn_in)

    mid_pieces = gather_pieces(middle_grad.astype(bf16))
    mid_all = jnp.concatenate(mid_pieces, axis=0)
    output_part = t_dot(attn_mix, mid_all).astype(bf16)
    output_sum = owner_scatter(output_part.reshape(owners, final_rows, width))
    mix_grad = by_head(dot_t(mid_all, output_weight).astype(bf16)).reshape(blocked)
    delta = jnp.sum(mix_grad.astype(f32) * mixed.astype(f32), axis=-1, keepdims=True)
    prob_back = pair_dot(mix_grad, values, 3, 3)
    score_grad = (probs * (prob_back - delta)).astype(bf16)
    grad_queries = pair_dot(score_grad, keys, 3, 2)
    grad_keys = pair_dot(score_grad, queries, 2, 2)
    grad_values = pair_dot(probs_b, mix_grad, 2, 2)
    grad_queries = by_row(rotate((grad_queries * scale).reshape(whole), cosine, -sine))
    grad_keys = by_row(rotate((grad_keys * scale).reshape(whole), cosine, -sine))
    query_gain_grad = jnp.sum(grad_queries * query_unit, axis=0)
    key_gain_grad = jnp.sum(grad_keys * key_unit, axis=0)
    grad_queries = grad_queries * query_gain_f
    grad_keys = grad_keys * key_gain_f
    means = jnp.stack(
        [jnp.sum(grad_queries * query_unit, axis=1), jnp.sum(grad_keys * key_unit, axis=1)], axis=0
    )
    means = group_sum(means) / width
    up_sum = scatter_far(after(up_near, means))
    up_weight_grad = jnp.stack([up_sum[:, e * ff : (e + 1) * ff] for e in range(EXP_DEV)])
    query_grad_b = (query_inverse * (grad_queries - query_unit * means[0][:, None])).astype(bf16)
    key_grad_b = (key_inverse * (grad_keys - key_unit * means[1][:, None])).astype(bf16)
    value_grad_b = by_row(grad_values.reshape(whole)).astype(bf16)
    qkv_grad = jnp.concatenate([query_grad_b, key_grad_b, value_grad_b], axis=1)
    query_part = t_dot(attn_in, query_grad_b)
    key_part = t_dot(attn_in, key_grad_b)
    query_part, key_part = query_part.astype(bf16), key_part.astype(bf16)
    qkv_grad = after(qkv_grad, query_part, key_part)
    attn_in_part = dot_t(qkv_grad, qkv_w)
    attn_in_grad = scatter_pieces(
        [attn_in_part[mask * rows : (mask + 1) * rows] for mask in range(parts)]
    )
    value_part = t_dot(attn_in, value_grad_b).astype(bf16).reshape(owners, parts * final_rows, cols)
    down_weight_grad = scatter_far(after(down_near, attn_in_part)).reshape(EXP_DEV, ff, cols)
    value_sum = owner_scatter(value_part)
    cut = (owners, parts * final_rows, cols)
    query_sum = owner_scatter(query_part.reshape(cut))
    key_sum = owner_scatter(key_part.reshape(cut))

    unit_one, inverse_one = rms_unit(residual)
    input_part, attn_gain_grad = rms_backward(
        attn_in_grad, unit_one, inverse_one, attn_gain_all
    )
    tokens_grad = middle_grad + input_part
    moe_out = after(moe_out, attn_in_part)
    block_output = middle + mixed_order(moe_out, w_index, parts).astype(f32)

    qkv_sum = jnp.concatenate([query_sum, key_sum, value_sum], axis=1)
    qkv_sum = qkv_sum.reshape(parts, final_rows, 3 * cols)
    qkv_sum = lax.all_to_all(qkv_sum, SHARD, split_axis=0, concat_axis=0, tiled=True)
    qkv_sum = place(qkv_sum)
    moves = []
    for e in range(owners):
        for w in range(parts):
            moves.append((e * parts + w, w * owners + e))
    output_sum = lax.ppermute(output_sum, (OWNER, SHARD), moves).astype(f32)

    own = jnp.zeros((2, parts, cols), f32)
    own = lax.dynamic_update_slice(
        own, jnp.stack([query_gain_grad, key_gain_grad])[:, None, :], (0, w_index, 0)
    ).reshape(2, width)
    table = jnp.concatenate([attn_gain_grad[None], ffn_gain_grad[None], own, router_grad], axis=0)
    count = table.shape[0]
    table = table.reshape(count, owners, parts * final_rows).transpose(1, 0, 2)
    table = lax.all_to_all(table, OWNER, split_axis=0, concat_axis=0, tiled=True)
    table = jnp.sum(table, axis=0)
    table = table.reshape(count, parts, final_rows).transpose(1, 0, 2)
    table = jnp.sum(
        lax.all_to_all(table, SHARD, split_axis=0, concat_axis=0, tiled=True), axis=0
    )
    return (
        block_output,
        tokens_grad,
        table[0],
        qkv_sum[0],
        qkv_sum[1],
        qkv_sum[2],
        table[2],
        table[3],
        output_sum,
        table[1],
        table[4:].T,
        gate_weight_grad,
        up_weight_grad,
        down_weight_grad,
    )


def solution(mesh):
    rows = P((OWNER, SHARD), None)
    line = P((OWNER, SHARD))
    part = P(SHARD)
    wide = P(SHARD, None)
    into = P(OWNER, SHARD, None)
    back = P(OWNER, None, SHARD)
    in_specs = (rows,) * 3 + (part, wide, wide, wide, part, part, wide, part, wide)
    in_specs = in_specs + (into, into, back, rows)
    out_specs = (rows, rows, line, rows, rows, rows, line, line, rows, line, rows)
    out_specs = out_specs + (into, into, back)

    return jax.shard_map(local, mesh=mesh, in_specs=in_specs, out_specs=out_specs, check_vma=False)
```

```python
import functools

import jax
import jax.numpy as jnp
from jax import lax
from jax.experimental import pallas as pl
from jax.experimental.pallas import tpu as pltpu
from jax.sharding import PartitionSpec as P


HEADS = 16
HEAD_DIM = 128
EXP_DEV = 2
OWNER = "expert"
SHARD = "wshard"


epsilon = 1e-05
theta_base = 10000.0


def rms_unit(activation):
    inverse = lax.rsqrt(jnp.mean(activation * activation, axis=-1, keepdims=True) + epsilon)
    return (activation * inverse, inverse)


def rms_backward(grad_out, normed, inverse, gain):
    gain_grad = jnp.sum(grad_out * normed, axis=0)
    grad_normed = grad_out * gain
    centred = grad_normed - normed * jnp.mean(grad_normed * normed, axis=-1, keepdims=True)
    return (inverse * centred, gain_grad)


def block_tables(lengths, rows):
    ends = jnp.cumsum(lengths, axis=1)
    row_index = jnp.arange(rows, dtype=jnp.int32)
    passed = (row_index[None, :, None] >= ends[:, None, :]).astype(jnp.int32)
    start = jnp.sum(passed * lengths[:, None, :], axis=2)
    allowed = (row_index[None, None, :] <= row_index[None, :, None]) & (
        row_index[None, None, :] >= start[:, :, None]
    )
    offsets = (row_index[None, :] - start).reshape(-1)
    half_dim = HEAD_DIM // 2
    frequency = theta_base ** (-2.0 * jnp.arange(half_dim, dtype=jnp.float32) / HEAD_DIM)
    angles = offsets.astype(jnp.float32)[:, None] * frequency[None, :]
    return (allowed, jnp.cos(angles), jnp.sin(angles))


def rotate(rows, cosine, sine):
    half_dim = HEAD_DIM // 2
    first = rows[..., :half_dim]
    second = rows[..., half_dim:]
    cosine = cosine[None, :, :]
    sine = sine[None, :, :]
    return jnp.concatenate([first * cosine - second * sine, second * cosine + first * sine], axis=-1)


def softmax_rows(logits):
    row_max = jnp.max(logits, axis=-1, keepdims=True)
    shifted = jnp.exp(logits - row_max)
    return shifted / jnp.sum(shifted, axis=-1, keepdims=True)


def dot(a, b):
    return jnp.dot(a, b, preferred_element_type=jnp.float32)


def dot_t(a, b):
    return lax.dot_general(a, b, (((1,), (1,)), ((), ())), preferred_element_type=jnp.float32)


def t_dot(a, b):
    return lax.dot_general(a, b, (((0,), (0,)), ((), ())), preferred_element_type=jnp.float32)


def swap(values, mask, axis_name=SHARD):
    count = lax.axis_size(axis_name)
    return lax.ppermute(values, axis_name, [(i, i ^ mask) for i in range(count)])


def after(values, *others):
    return lax.optimization_barrier((values, *others))[0]


def bits_of(count):
    return [1 << k for k in range(count.bit_length() - 1)]


def gather_far(shard):
    pieces = {0: shard}
    for bit in reversed(bits_of(lax.axis_size(SHARD))[1:]):
        for mask in list(pieces):
            pieces[mask ^ bit] = swap(pieces[mask], bit)
    return pieces


def gather_near(pieces):
    pieces = dict(pieces)
    for mask in list(pieces):
        pieces[mask ^ 1] = swap(pieces[mask], 1)
    return [pieces[mask] for mask in sorted(pieces)]


def gather_pieces(shard):
    return gather_near(gather_far(shard))


def scatter_stage(blocks, bit):
    masks = sorted(blocks, reverse=True)
    arrived = {m ^ bit: swap(blocks[m].astype(jnp.bfloat16), bit) for m in masks if m & bit}
    return {m: blocks[m] + arrived[m].astype(jnp.float32) for m in arrived}


def scatter_near(blocks):
    return scatter_stage(dict(enumerate(blocks)), 1)


def scatter_far(blocks):
    for bit in bits_of(lax.axis_size(SHARD))[1:]:
        blocks = scatter_stage(blocks, bit)
    return blocks[0]


def scatter_pieces(blocks):
    return scatter_far(scatter_near(blocks))


def block_of(array, index, count, axis):
    size = array.shape[axis] // count
    return lax.dynamic_slice_in_dim(array, index * size, size, axis)


def mixed_order(array, w_index, count):
    return jnp.concatenate(
        [block_of(array, w_index ^ mask, count, array.ndim - 1) for mask in range(count)], axis=-1
    )


def pair_dot(a, b, a_axis, b_axis):
    dims = (((a_axis,), (b_axis,)), ((0, 1), (0, 1)))
    return lax.dot_general(a, b, dims, preferred_element_type=jnp.float32)


def group_sum(values):
    count = lax.axis_size(SHARD)
    blocks = values.reshape(values.shape[0], count, -1)
    total = blocks
    for mask in reversed(range(1, count)):
        arrived = swap(blocks, mask)
        total = total + jnp.stack([arrived[:, m ^ mask] for m in range(count)], axis=1)
    return total.reshape(values.shape)


def owner_bits():
    return bits_of(lax.axis_size(OWNER))[::-1]


def owner_split(values):
    return values.reshape([2] * len(owner_bits()) + list(values.shape[1:]))


def owner_stage(values, left, bit):
    index = (lax.axis_index(OWNER) // bit) % 2
    axis = left.index(bit)
    away = lax.dynamic_index_in_dim(values, 1 - index, axis, keepdims=False)
    kept = lax.dynamic_index_in_dim(values, index, axis, keepdims=False)
    arrived = swap(away, bit, OWNER)
    total = (kept.astype(jnp.float32) + arrived.astype(jnp.float32)).astype(jnp.bfloat16)
    return total, [b for b in left if b != bit]


def owner_scatter(values):
    values, left = owner_split(values), owner_bits()
    for bit in left[::-1]:
        values, left = owner_stage(values, left, bit)
    return values


def place_kernel(values_ref, *out_refs):
    parts, _, cols = values_ref.shape
    cols = cols // 3
    for k in range(3):
        for p in range(parts):
            out_refs[k][:, p * cols : (p + 1) * cols] = values_ref[
                p, :, k * cols : (k + 1) * cols
            ].astype(jnp.float32)


def place(values):
    parts, rows, cols = values.shape
    shape = jax.ShapeDtypeStruct((rows, parts * cols // 3), jnp.float32)
    return pl.pallas_call(place_kernel, out_shape=[shape] * 3)(values)


def expert_hidden_kernel(parts, x_ref, cot_ref, weight_ref, *refs):
    gates, ups, downs = refs[:parts], refs[parts : 2 * parts], refs[2 * parts : 3 * parts]
    hidden_ref, gate_grad_ref, up_grad_ref, route_ref = refs[3 * parts :]
    cols = gates[0].shape[0]
    f32 = jnp.float32
    gate_lin = up_lin = back = 0.0
    for m in range(parts):
        x = x_ref[:, m * cols : (m + 1) * cols]
        gate_lin = gate_lin + jnp.dot(x, gates[m][...], preferred_element_type=f32)
        up_lin = up_lin + jnp.dot(x, ups[m][...], preferred_element_type=f32)
        back = back + dot_t(cot_ref[:, m * cols : (m + 1) * cols], downs[m][...])
    weight = weight_ref[...]
    sigmoid = jax.nn.sigmoid(gate_lin)
    swish = gate_lin * sigmoid
    hidden = swish * up_lin
    product = hidden * back
    route = product[:, :128]
    for k in range(1, product.shape[1] // 128):
        route = route + product[:, k * 128 : (k + 1) * 128]
    hidden_ref[...] = (hidden * weight).astype(jnp.bfloat16)
    grad = back * weight
    gate_grad_ref[...] = (grad * up_lin * sigmoid * (1.0 + gate_lin * (1.0 - sigmoid))).astype(
        jnp.bfloat16
    )
    up_grad_ref[...] = (grad * swish).astype(jnp.bfloat16)

    @pl.when(pl.program_id(2) == 0)
    def _():
        route_ref[...] = route

    @pl.when(pl.program_id(2) > 0)
    def _():
        route_ref[...] += route


def attend_back_kernel(
    grad_ref, query_ref, key_ref, value_ref, mix_ref, probs_ref, cos_ref, sin_ref, *out_refs
):
    query_out, key_out, value_out = out_refs
    f32, bf16 = jnp.float32, jnp.bfloat16
    scale = HEAD_DIM ** (-0.5)
    cosine = cos_ref[...]
    sine = sin_ref[...]
    for h in range(query_ref.shape[0]):
        at = slice(h * HEAD_DIM, (h + 1) * HEAD_DIM)
        grad = grad_ref[:, at]
        probs = probs_ref[h]
        delta = jnp.sum(grad.astype(f32) * mix_ref[h].astype(f32), axis=1, keepdims=True)
        score = probs * (dot_t(grad, value_ref[h]) - delta)
        query = jnp.dot(score.astype(bf16), key_ref[h], preferred_element_type=f32) * scale
        key = jnp.dot(score.T.astype(bf16), query_ref[h], preferred_element_type=f32) * scale
        value = jnp.dot(probs.T.astype(bf16), grad, preferred_element_type=f32)
        query = query * cosine + pltpu.roll(query, HEAD_DIM // 2, 1) * sine
        key = key * cosine + pltpu.roll(key, HEAD_DIM // 2, 1) * sine
        query_out[:, at] = query
        key_out[:, at] = key
        value_out[:, at] = value.astype(bf16)


def attend_back(grad, queries, keys, values, mixed, probs, cosine, sine):
    heads, blocks, rows, _ = queries.shape
    cols = grad.shape[1]
    head = pl.BlockSpec((heads, None, rows, HEAD_DIM), lambda b: (0, b, 0, 0))
    line = pl.BlockSpec((rows, cols), lambda b: (b, 0))
    table = pl.BlockSpec((rows, HEAD_DIM), lambda b: (b, 0))
    wide = jax.ShapeDtypeStruct(grad.shape, jnp.float32)
    return pl.pallas_call(
        attend_back_kernel,
        grid=(blocks,),
        in_specs=[line] + [head] * 4
        + [pl.BlockSpec((heads, None, rows, rows), lambda b: (0, b, 0, 0)), table, table],
        out_specs=[line] * 3,
        out_shape=[wide, wide, jax.ShapeDtypeStruct(grad.shape, jnp.bfloat16)],
    )(grad, queries, keys, values, mixed, probs, cosine, sine)


def row_tile_of(rows):
    return min(rows, 1024)


def expert_hidden(x, cot, weights, gates, ups, downs, tile=256):
    rows, width = x.shape
    parts = len(gates)
    count, cols, ff = gates[0].shape
    row_tile = row_tile_of(rows)
    steps = ff // tile
    row_spec = pl.BlockSpec((row_tile, width), lambda r, e, f: (r, 0))
    in_piece = pl.BlockSpec((None, cols, tile), lambda r, e, f: (e, 0, f))
    out_piece = pl.BlockSpec((None, tile, cols), lambda r, e, f: (e, f, 0))
    wide_spec = pl.BlockSpec((row_tile, tile), lambda r, e, f: (r, e * steps + f))
    wide = jax.ShapeDtypeStruct((rows, count * ff), jnp.bfloat16)
    return pl.pallas_call(
functools.partial(expert_hidden_kernel, parts),
grid=(rows // row_tile, count, steps),
in_specs=[row_spec, row_spec, pl.BlockSpec((None, row_tile, 1), lambda r, e, f: (e, r, 0))]
+ [in_piece] * (2 * parts)
+ [out_piece] * parts,
out_specs=[wide_spec] * 3
+ [pl.BlockSpec((None, row_tile, 128), lambda r, e, f: (e, r, 0))],
out_shape=[wide] * 3 + [jax.ShapeDtypeStruct((count, rows, 128), jnp.float32)],
compiler_params=pltpu.CompilerParams(vmem_limit_bytes=60 * 1024 * 1024),
    )(x, cot, weights, *gates, *ups, *downs)


def back_rows_kernel(parts, gate_grad_ref, up_grad_ref, *refs):
    gates, ups = refs[:parts], refs[parts : 2 * parts]
    out_ref, sum_ref = refs[2 * parts :]
    cols = gates[0].shape[0]
    step = pl.program_id(1) * pl.num_programs(2) + pl.program_id(2)
    last = pl.num_programs(1) * pl.num_programs(2) - 1
    for m in range(parts):
        at = slice(m * cols, (m + 1) * cols)
        part = dot_t(gate_grad_ref[...], gates[m][...]) + dot_t(up_grad_ref[...], ups[m][...])

        @pl.when(step == 0)
        def _():
            sum_ref[:, at] = part

        @pl.when((step > 0) & (step < last))
        def _():
            sum_ref[:, at] += part

        @pl.when(step == last)
        def _():
            out_ref[:, at] = (sum_ref[:, at] + part).astype(jnp.bfloat16)


def back_rows(gate_grad, up_grad, gates, ups, tile=512):
    rows = gate_grad.shape[0]
    parts = len(gates)
    count, cols, ff = gates[0].shape
    row_tile = row_tile_of(rows)
    steps = ff // tile
    wide_spec = pl.BlockSpec((row_tile, tile), lambda r, e, f: (r, e * steps + f))
    piece = pl.BlockSpec((None, cols, tile), lambda r, e, f: (e, 0, f))
    return pl.pallas_call(
functools.partial(back_rows_kernel, parts),
grid=(rows // row_tile, count, steps),
in_specs=[wide_spec] * 2 + [piece] * (2 * parts),
out_specs=pl.BlockSpec((row_tile, parts * cols), lambda r, e, f: (r, 0)),
out_shape=jax.ShapeDtypeStruct((rows, parts * cols), jnp.bfloat16),
scratch_shapes=[pltpu.VMEM((row_tile, parts * cols), jnp.float32)],
compiler_params=pltpu.CompilerParams(vmem_limit_bytes=60 * 1024 * 1024),
    )(gate_grad, up_grad, *gates, *ups)


def local(
    tokens,
    doc_lengths,
    expert_ids,
    attn_gain,
    query_weight,
    key_weight,
    value_weight,
    query_gain,
    key_gain,
    output_weight,
    ffn_gain,
    router_weight,
    gate_weight,
    up_weight,
    down_weight,
    cotangent,
):
    bf16 = jnp.bfloat16
    f32 = jnp.float32
    rows, width = tokens.shape
    owners = lax.axis_size(OWNER)
    parts = lax.axis_size(SHARD)
    w_index = lax.axis_index(SHARD)
    experts = EXP_DEV * owners
    group = parts * rows
    cols = width // parts
    heads = HEADS // parts
    final_rows = width // (owners * parts)
    ff = gate_weight.shape[2]

    e_index = lax.axis_index(OWNER)
    half = cols // 2
    unit = 2 * w_index + e_index % 2
    units = 2 * parts

    docs = doc_lengths.shape[1]
    lengths_row = jnp.zeros((1, cols), bf16).at[:, :docs].set(doc_lengths.astype(bf16))
    small = jnp.concatenate(
        [attn_gain[None, :], ffn_gain[None, :], lengths_row, router_weight.T], axis=0
    )
    small_all = lax.all_gather(small, SHARD, axis=0)
    attn_gain_all = small_all[:, 0, :].reshape(width).astype(f32)
    ffn_gain_all = small_all[:, 1, :].reshape(width).astype(f32)
    lengths_all = small_all[:, 2, :docs].astype(jnp.int32)
    lengths_all = jnp.concatenate([block_of(lengths_all, w_index ^ m, parts, 0) for m in range(parts)])
    router_t = small_all[:, 3:, :].transpose(1, 0, 2).reshape(experts, width)

    *weights_in, tokens_in, _ = lax.optimization_barrier(
        (query_weight, key_weight, value_weight, tokens, small_all)
    )
    tokens_far = gather_far(tokens_in)
    tokens_all = jnp.concatenate(gather_near(tokens_far), axis=0)
    pieces = [None] * units
    for mask in reversed(range(parts)):
        piece = jnp.concatenate(
            [block_of(weight, w_index ^ mask, parts, 1) for weight in weights_in], axis=1
        )
        for side in range(2):
            pieces[2 * mask + side] = block_of(piece, side ^ (e_index % 2), 2, 0)
    for mask in reversed(range(1, parts)):
        pieces[2 * mask] = swap(pieces[2 * mask], mask)
        if mask == 1:
            pieces[3] = swap(pieces[3], 1)
    for mask in reversed(range(2, parts)):
        pieces[2 * mask + 1] = swap(pieces[2 * mask], 1, OWNER)
    cot_b = mixed_order(cotangent, w_index, parts).astype(bf16)
    cot_all = lax.all_gather(cot_b, OWNER, axis=0, tiled=True)
    down_in = after(down_weight, pieces[4])
    down_far = gather_far(down_in)

    unit_all, _ = rms_unit(tokens_all.astype(f32))
    attn_in = (unit_all * attn_gain_all).astype(bf16)
    attn_in_mixed = mixed_order(attn_in, unit, units)
    qkv = 0.0
    for at in [0, 1, 2, 3] + [2 * m for m in range(2, parts)] + [2 * m + 1 for m in range(2, parts)]:
        qkv = qkv + dot(attn_in_mixed[:, at * half : (at + 1) * half], pieces[at])
    query_lin, key_lin, value_lin = (qkv[:, i * cols : (i + 1) * cols] for i in range(3))
    squares = jnp.stack(
        [jnp.sum(query_lin * query_lin, axis=1), jnp.sum(key_lin * key_lin, axis=1)], axis=0
    )
    squares = group_sum(squares)
    inverses = lax.rsqrt(squares / width + epsilon)
    query_inverse = inverses[0][:, None]
    key_inverse = inverses[1][:, None]
    query_unit = query_lin * query_inverse
    key_unit = key_lin * key_inverse
    query_gain_f = query_gain.astype(f32)
    key_gain_f = key_gain.astype(f32)
    allowed, cosine, sine = block_tables(lengths_all, rows)
    scale = HEAD_DIM ** (-0.5)

    def by_head(array):
        return jnp.stack(
            [array[:, h * HEAD_DIM : (h + 1) * HEAD_DIM] for h in range(heads)], axis=0
        )

    def by_row(array):
        return jnp.concatenate([array[h] for h in range(heads)], axis=1)

    blocked = (heads, parts, rows, HEAD_DIM)
    whole = (heads, group, HEAD_DIM)
    queries = rotate(by_head(query_unit * query_gain_f), cosine, sine).astype(bf16)
    queries = queries.reshape(blocked)
    keys = rotate(by_head(key_unit * key_gain_f), cosine, sine).astype(bf16).reshape(blocked)
    values = by_head(value_lin).astype(bf16).reshape(blocked)
    scores = pair_dot(queries, keys, 3, 3) * scale
    scores = jnp.where(allowed[None, :, :, :], scores, -1e30)
    row_max = jnp.max(scores, axis=-1, keepdims=True)
    log_total = row_max + jnp.log(jnp.sum(jnp.exp(scores - row_max), axis=-1, keepdims=True))
    probs = jnp.exp(scores - log_total)
    probs_b = probs.astype(bf16)
    mixed = pair_dot(probs_b, values, 3, 2).astype(bf16)
    attn_mix = by_row(mixed.reshape(whole))
    attn_out = dot(attn_mix, output_weight)
    attn_out = scatter_pieces([attn_out[mask * rows : (mask + 1) * rows] for mask in range(parts)])
    attn_out, *pieces = lax.optimization_barrier((attn_out, *pieces))
    qkv_w = jnp.concatenate(pieces, axis=0)
    qkv_w = jnp.concatenate(
        [block_of(qkv_w, unit ^ k, units, 0) for k in range(units)], axis=0
    )

    residual = tokens.astype(f32)
    middle = residual + attn_out
    unit_two, inverse_two = rms_unit(middle)
    ffn_in = (unit_two * ffn_gain_all).astype(bf16)
    ffn_in_mixed = mixed_order(ffn_in, w_index, parts)
    gate_in, up_in, ffn_in_mixed, ffn_in = lax.optimization_barrier(
        (gate_weight, up_weight, ffn_in_mixed, ffn_in)
    )
    gate_far = gather_far(gate_in)
    up_far = gather_far(up_in)
    router_probs = softmax_rows(dot_t(ffn_in, router_t))
    expert_range = jnp.arange(experts, dtype=jnp.int32)
    named = jnp.any(expert_ids[:, :, None] == expert_range[None, None, :], axis=1)
    route_table = jnp.where(named, router_probs, 0.0)

    arrived = lax.all_gather(ffn_in_mixed, OWNER, axis=0, tiled=True)
    weights = lax.all_to_all(
        route_table.reshape(rows, owners, EXP_DEV).transpose(1, 2, 0),
        OWNER,
        split_axis=0,
        concat_axis=0,
        tiled=True,
    )
    weights = weights.transpose(1, 0, 2).reshape(EXP_DEV, owners * rows, 1)
    gate_pieces = gather_near(gate_far)
    up_pieces = gather_near(
        {m: after(p, weights, gate_pieces[-1]) if m else p for m, p in up_far.items()}
    )
    down_pieces = gather_near({m: after(p, attn_out) if m else p for m, p in down_far.items()})
    hidden_w, gate_grad_b, up_grad_b, route_part = expert_hidden(
        arrived, cot_all, weights, gate_pieces, up_pieces, down_pieces
    )
    row_partial = back_rows(gate_grad_b, up_grad_b, gate_pieces, up_pieces)
    row_grads = lax.psum_scatter(row_partial, OWNER, scatter_dimension=0, tiled=True)
    route_back = jnp.sum(route_part, axis=2)
    route_back = lax.all_to_all(
        route_back.reshape(EXP_DEV, owners, rows).transpose(1, 0, 2),
        OWNER,
        split_axis=0,
        concat_axis=0,
        tiled=True,
    )
    part_of = lambda array, mask: array[:, mask * cols : (mask + 1) * cols]
    order = sorted(range(parts), key=lambda m: (m < parts // 2, -m))

    def ordered_blocks(make):
        blocks = [None] * parts
        for mask in order:
            blocks[mask] = make(mask)
        return blocks

    gate_blocks = ordered_blocks(lambda m: t_dot(part_of(arrived, m), gate_grad_b))
    gate_near = scatter_near(gate_blocks)
    up_blocks = ordered_blocks(lambda m: t_dot(part_of(arrived, m), up_grad_b))
    up_near = scatter_near(up_blocks)
    hidden_w, qkv_w, *_ = lax.optimization_barrier((hidden_w, qkv_w, *gate_blocks, *up_blocks))
    down_blocks = ordered_blocks(lambda m: t_dot(hidden_w, part_of(cot_all, m)))
    down_near = scatter_near(down_blocks)
    gate_sum = scatter_far(gate_near)
    gate_weight_grad = jnp.stack([gate_sum[:, e * ff : (e + 1) * ff] for e in range(EXP_DEV)])
    down_all = jnp.concatenate(
        [piece.reshape(EXP_DEV * ff, cols) for piece in down_pieces], axis=1
    )
    out_partial = dot(hidden_w, down_all)
    out_partial = out_partial.astype(bf16)
    row_grads, route_back = lax.optimization_barrier((row_grads, route_back))
    moe_out = owner_scatter(out_partial.reshape(owners, rows, width))

    route_grad = route_back.reshape(experts, rows).T
    prob_grad = jnp.where(named, route_grad, 0.0)
    logit_grad = router_probs * (
        prob_grad - jnp.sum(router_probs * prob_grad, axis=1, keepdims=True)
    )
    logit_grad_b = logit_grad.astype(bf16)
    ffn_in_grad = mixed_order(row_grads, w_index, parts).astype(f32) + dot(logit_grad_b, router_t)
    middle_part, ffn_gain_grad = rms_backward(ffn_in_grad, unit_two, inverse_two, ffn_gain_all)
    middle_grad = cotangent + middle_part
    router_grad = t_dot(logit_grad_b, ffn_in)

    mid_pieces = gather_pieces(middle_grad.astype(bf16))
    mid_all = jnp.concatenate(mid_pieces, axis=0)
    output_part = t_dot(attn_mix, mid_all).astype(bf16)
    output_sum = owner_scatter(output_part.reshape(owners, final_rows, width))
    mix_grad = dot_t(mid_all, output_weight).astype(bf16)
    grad_queries, grad_keys, value_grad_b = attend_back(
        mix_grad,
        queries,
        keys,
        values,
        mixed,
        probs,
        jnp.concatenate([cosine, cosine], axis=1),
        jnp.concatenate([sine, -sine], axis=1),
    )
    query_gain_grad = jnp.sum(grad_queries * query_unit, axis=0)
    key_gain_grad = jnp.sum(grad_keys * key_unit, axis=0)
    grad_queries = grad_queries * query_gain_f
    grad_keys = grad_keys * key_gain_f
    means = jnp.stack(
        [jnp.sum(grad_queries * query_unit, axis=1), jnp.sum(grad_keys * key_unit, axis=1)], axis=0
    )
    means = group_sum(means) / width
    up_sum = scatter_far(after(up_near, means))
    up_weight_grad = jnp.stack([up_sum[:, e * ff : (e + 1) * ff] for e in range(EXP_DEV)])
    query_grad_b = (query_inverse * (grad_queries - query_unit * means[0][:, None])).astype(bf16)
    key_grad_b = (key_inverse * (grad_keys - key_unit * means[1][:, None])).astype(bf16)
    qkv_grad = jnp.concatenate([query_grad_b, key_grad_b, value_grad_b], axis=1)
    query_part = t_dot(attn_in, query_grad_b)
    key_part = t_dot(attn_in, key_grad_b)
    query_part, key_part = query_part.astype(bf16), key_part.astype(bf16)
    qkv_grad = after(qkv_grad, query_part, key_part)
    attn_in_part = dot_t(qkv_grad, qkv_w)
    attn_in_grad = scatter_pieces(
        [attn_in_part[mask * rows : (mask + 1) * rows] for mask in range(parts)]
    )
    value_part = t_dot(attn_in, value_grad_b).astype(bf16).reshape(owners, parts * final_rows, cols)
    down_weight_grad = scatter_far(after(down_near, attn_in_part)).reshape(EXP_DEV, ff, cols)
    value_sum = owner_scatter(value_part)
    cut = (owners, parts * final_rows, cols)
    query_sum = owner_scatter(query_part.reshape(cut))
    key_sum = owner_scatter(key_part.reshape(cut))

    unit_one, inverse_one = rms_unit(residual)
    input_part, attn_gain_grad = rms_backward(
        attn_in_grad, unit_one, inverse_one, attn_gain_all
    )
    tokens_grad = middle_grad + input_part
    moe_out = after(moe_out, attn_in_part)
    block_output = middle + mixed_order(moe_out, w_index, parts).astype(f32)

    qkv_sum = jnp.concatenate([query_sum, key_sum, value_sum], axis=1)
    qkv_sum = qkv_sum.reshape(parts, final_rows, 3 * cols)
    qkv_sum = lax.all_to_all(qkv_sum, SHARD, split_axis=0, concat_axis=0, tiled=True)
    qkv_sum = place(qkv_sum)
    moves = []
    for e in range(owners):
        for w in range(parts):
            moves.append((e * parts + w, w * owners + e))
    output_sum = lax.ppermute(output_sum, (OWNER, SHARD), moves).astype(f32)

    own = jnp.zeros((2, parts, cols), f32)
    own = lax.dynamic_update_slice(
        own, jnp.stack([query_gain_grad, key_gain_grad])[:, None, :], (0, w_index, 0)
    ).reshape(2, width)
    table = jnp.concatenate([attn_gain_grad[None], ffn_gain_grad[None], own, router_grad], axis=0)
    count = table.shape[0]
    table = table.reshape(count, owners, parts * final_rows).transpose(1, 0, 2)
    table = lax.all_to_all(table, OWNER, split_axis=0, concat_axis=0, tiled=True)
    table = jnp.sum(table, axis=0)
    table = table.reshape(count, parts, final_rows).transpose(1, 0, 2)
    table = jnp.sum(
        lax.all_to_all(table, SHARD, split_axis=0, concat_axis=0, tiled=True), axis=0
    )
    return (
        block_output,
        tokens_grad,
        table[0],
        qkv_sum[0],
        qkv_sum[1],
        qkv_sum[2],
        table[2],
        table[3],
        output_sum,
        table[1],
        table[4:].T,
        gate_weight_grad,
        up_weight_grad,
        down_weight_grad,
    )


def solution(mesh):
    rows = P((OWNER, SHARD), None)
    line = P((OWNER, SHARD))
    part = P(SHARD)
    wide = P(SHARD, None)
    into = P(OWNER, SHARD, None)
    back = P(OWNER, None, SHARD)
    in_specs = (rows,) * 3 + (part, wide, wide, wide, part, part, wide, part, wide)
    in_specs = in_specs + (into, into, back, rows)
    out_specs = (rows, rows, line, rows, rows, rows, line, line, rows, line, rows)
    out_specs = out_specs + (into, into, back)

    return jax.shard_map(local, mesh=mesh, in_specs=in_specs, out_specs=out_specs, check_vma=False)
```

```python
import functools

import jax
import jax.numpy as jnp
from jax import lax
from jax.experimental import pallas as pl
from jax.experimental.pallas import tpu as pltpu
from jax.sharding import PartitionSpec as P


HEADS = 16
HEAD_DIM = 128
EXP_DEV = 2
OWNER = "expert"
SHARD = "wshard"


epsilon = 1e-05
theta_base = 10000.0


def rms_unit(activation):
    inverse = lax.rsqrt(jnp.mean(activation * activation, axis=-1, keepdims=True) + epsilon)
    return (activation * inverse, inverse)


def rms_backward(grad_out, normed, inverse, gain):
    gain_grad = jnp.sum(grad_out * normed, axis=0)
    grad_normed = grad_out * gain
    centred = grad_normed - normed * jnp.mean(grad_normed * normed, axis=-1, keepdims=True)
    return (inverse * centred, gain_grad)


def block_tables(lengths, rows):
    ends = jnp.cumsum(lengths, axis=1)
    row_index = jnp.arange(rows, dtype=jnp.int32)
    passed = (row_index[None, :, None] >= ends[:, None, :]).astype(jnp.int32)
    start = jnp.sum(passed * lengths[:, None, :], axis=2)
    allowed = (row_index[None, None, :] <= row_index[None, :, None]) & (
        row_index[None, None, :] >= start[:, :, None]
    )
    offsets = (row_index[None, :] - start).reshape(-1)
    half_dim = HEAD_DIM // 2
    frequency = theta_base ** (-2.0 * jnp.arange(half_dim, dtype=jnp.float32) / HEAD_DIM)
    angles = offsets.astype(jnp.float32)[:, None] * frequency[None, :]
    return (allowed, jnp.cos(angles), jnp.sin(angles))


def rotate(rows, cosine, sine):
    half_dim = HEAD_DIM // 2
    first = rows[..., :half_dim]
    second = rows[..., half_dim:]
    cosine = cosine[None, :, :]
    sine = sine[None, :, :]
    return jnp.concatenate([first * cosine - second * sine, second * cosine + first * sine], axis=-1)


def softmax_rows(logits):
    row_max = jnp.max(logits, axis=-1, keepdims=True)
    shifted = jnp.exp(logits - row_max)
    return shifted / jnp.sum(shifted, axis=-1, keepdims=True)


def dot(a, b):
    return jnp.dot(a, b, preferred_element_type=jnp.float32)


def dot_t(a, b):
    return lax.dot_general(a, b, (((1,), (1,)), ((), ())), preferred_element_type=jnp.float32)


def t_dot(a, b):
    return lax.dot_general(a, b, (((0,), (0,)), ((), ())), preferred_element_type=jnp.float32)


def swap(values, mask, axis_name=SHARD):
    count = lax.axis_size(axis_name)
    return lax.ppermute(values, axis_name, [(i, i ^ mask) for i in range(count)])


def after(values, *others):
    return lax.optimization_barrier((values, *others))[0]


def bits_of(count):
    return [1 << k for k in range(count.bit_length() - 1)]


def gather_far(shard):
    pieces = {0: shard}
    for bit in reversed(bits_of(lax.axis_size(SHARD))[1:]):
        for mask in list(pieces):
            pieces[mask ^ bit] = swap(pieces[mask], bit)
    return pieces


def gather_near(pieces):
    pieces = dict(pieces)
    for mask in list(pieces):
        pieces[mask ^ 1] = swap(pieces[mask], 1)
    return [pieces[mask] for mask in sorted(pieces)]


def gather_pieces(shard):
    return gather_near(gather_far(shard))


def scatter_stage(blocks, bit):
    masks = sorted(blocks, reverse=True)
    arrived = {m ^ bit: swap(blocks[m].astype(jnp.bfloat16), bit) for m in masks if m & bit}
    return {m: blocks[m] + arrived[m].astype(jnp.float32) for m in arrived}


def scatter_near(blocks):
    return scatter_stage(dict(enumerate(blocks)), 1)


def scatter_far(blocks):
    for bit in bits_of(lax.axis_size(SHARD))[1:]:
        blocks = scatter_stage(blocks, bit)
    return blocks[0]


def scatter_pieces(blocks):
    return scatter_far(scatter_near(blocks))


def block_of(array, index, count, axis):
    size = array.shape[axis] // count
    return lax.dynamic_slice_in_dim(array, index * size, size, axis)


def mixed_order(array, w_index, count):
    return jnp.concatenate(
        [block_of(array, w_index ^ mask, count, array.ndim - 1) for mask in range(count)], axis=-1
    )


def pair_dot(a, b, a_axis, b_axis):
    dims = (((a_axis,), (b_axis,)), ((0, 1), (0, 1)))
    return lax.dot_general(a, b, dims, preferred_element_type=jnp.float32)


def group_sum(values):
    count = lax.axis_size(SHARD)
    blocks = values.reshape(values.shape[0], count, -1)
    total = blocks
    for mask in reversed(range(1, count)):
        arrived = swap(blocks, mask)
        total = total + jnp.stack([arrived[:, m ^ mask] for m in range(count)], axis=1)
    return total.reshape(values.shape)


def owner_bits():
    return bits_of(lax.axis_size(OWNER))[::-1]


def owner_split(values):
    return values.reshape([2] * len(owner_bits()) + list(values.shape[1:]))


def owner_stage(values, left, bit):
    index = (lax.axis_index(OWNER) // bit) % 2
    axis = left.index(bit)
    away = lax.dynamic_index_in_dim(values, 1 - index, axis, keepdims=False)
    kept = lax.dynamic_index_in_dim(values, index, axis, keepdims=False)
    arrived = swap(away, bit, OWNER)
    total = (kept.astype(jnp.float32) + arrived.astype(jnp.float32)).astype(jnp.bfloat16)
    return total, [b for b in left if b != bit]


def owner_scatter(values, turn=0):
    values, left = owner_split(values), owner_bits()
    for bit in left[::-1][turn:] + left[::-1][:turn]:
        values, left = owner_stage(values, left, bit)
    return values


def place_kernel(values_ref, *out_refs):
    parts, _, cols = values_ref.shape
    cols = cols // 3
    for k in range(3):
        for p in range(parts):
            out_refs[k][:, p * cols : (p + 1) * cols] = values_ref[
                p, :, k * cols : (k + 1) * cols
            ].astype(jnp.float32)


def place(values):
    parts, rows, cols = values.shape
    shape = jax.ShapeDtypeStruct((rows, parts * cols // 3), jnp.float32)
    return pl.pallas_call(place_kernel, out_shape=[shape] * 3)(values)


def expert_hidden_kernel(parts, x_ref, cot_ref, weight_ref, *refs):
    gates, ups, downs = refs[:parts], refs[parts : 2 * parts], refs[2 * parts : 3 * parts]
    hidden_ref, gate_grad_ref, up_grad_ref, route_ref = refs[3 * parts :]
    cols = gates[0].shape[0]
    f32 = jnp.float32
    gate_lin = up_lin = back = 0.0
    for m in range(parts):
        x = x_ref[:, m * cols : (m + 1) * cols]
        gate_lin = gate_lin + jnp.dot(x, gates[m][...], preferred_element_type=f32)
        up_lin = up_lin + jnp.dot(x, ups[m][...], preferred_element_type=f32)
        back = back + dot_t(cot_ref[:, m * cols : (m + 1) * cols], downs[m][...])
    weight = weight_ref[...]
    sigmoid = jax.nn.sigmoid(gate_lin)
    swish = gate_lin * sigmoid
    hidden = swish * up_lin
    product = hidden * back
    route = product[:, :128]
    for k in range(1, product.shape[1] // 128):
        route = route + product[:, k * 128 : (k + 1) * 128]
    hidden_ref[...] = (hidden * weight).astype(jnp.bfloat16)
    grad = back * weight
    gate_grad_ref[...] = (grad * up_lin * sigmoid * (1.0 + gate_lin * (1.0 - sigmoid))).astype(
        jnp.bfloat16
    )
    up_grad_ref[...] = (grad * swish).astype(jnp.bfloat16)

    @pl.when(pl.program_id(2) == 0)
    def _():
        route_ref[...] = route

    @pl.when(pl.program_id(2) > 0)
    def _():
        route_ref[...] += route


def attend_back_kernel(
    grad_ref, query_ref, key_ref, value_ref, mix_ref, probs_ref, cos_ref, sin_ref, *out_refs
):
    query_out, key_out, value_out = out_refs
    f32, bf16 = jnp.float32, jnp.bfloat16
    scale = HEAD_DIM ** (-0.5)
    cosine = cos_ref[...]
    sine = sin_ref[...]
    for h in range(query_ref.shape[0]):
        at = slice(h * HEAD_DIM, (h + 1) * HEAD_DIM)
        grad = grad_ref[:, at]
        probs = probs_ref[h]
        delta = jnp.sum(grad.astype(f32) * mix_ref[h].astype(f32), axis=1, keepdims=True)
        score = probs * (dot_t(grad, value_ref[h]) - delta)
        query = jnp.dot(score.astype(bf16), key_ref[h], preferred_element_type=f32) * scale
        key = jnp.dot(score.T.astype(bf16), query_ref[h], preferred_element_type=f32) * scale
        value = jnp.dot(probs.T.astype(bf16), grad, preferred_element_type=f32)
        query = query * cosine + pltpu.roll(query, HEAD_DIM // 2, 1) * sine
        key = key * cosine + pltpu.roll(key, HEAD_DIM // 2, 1) * sine
        query_out[:, at] = query
        key_out[:, at] = key
        value_out[:, at] = value.astype(bf16)


def attend_back(grad, queries, keys, values, mixed, probs, cosine, sine):
    heads, blocks, rows, _ = queries.shape
    cols = grad.shape[1]
    head = pl.BlockSpec((heads, None, rows, HEAD_DIM), lambda b: (0, b, 0, 0))
    line = pl.BlockSpec((rows, cols), lambda b: (b, 0))
    table = pl.BlockSpec((rows, HEAD_DIM), lambda b: (b, 0))
    wide = jax.ShapeDtypeStruct(grad.shape, jnp.float32)
    return pl.pallas_call(
        attend_back_kernel,
        grid=(blocks,),
        in_specs=[line] + [head] * 4
        + [pl.BlockSpec((heads, None, rows, rows), lambda b: (0, b, 0, 0)), table, table],
        out_specs=[line] * 3,
        out_shape=[wide, wide, jax.ShapeDtypeStruct(grad.shape, jnp.bfloat16)],
    )(grad, queries, keys, values, mixed, probs, cosine, sine)


def row_tile_of(rows):
    return min(rows, 1024)


def expert_hidden(x, cot, weights, gates, ups, downs, tile=256):
    rows, width = x.shape
    parts = len(gates)
    count, cols, ff = gates[0].shape
    row_tile = row_tile_of(rows)
    steps = ff // tile
    row_spec = pl.BlockSpec((row_tile, width), lambda r, e, f: (r, 0))
    in_piece = pl.BlockSpec((None, cols, tile), lambda r, e, f: (e, 0, f))
    out_piece = pl.BlockSpec((None, tile, cols), lambda r, e, f: (e, f, 0))
    wide_spec = pl.BlockSpec((row_tile, tile), lambda r, e, f: (r, e * steps + f))
    wide = jax.ShapeDtypeStruct((rows, count * ff), jnp.bfloat16)
    return pl.pallas_call(
functools.partial(expert_hidden_kernel, parts),
grid=(rows // row_tile, count, steps),
in_specs=[row_spec, row_spec, pl.BlockSpec((None, row_tile, 1), lambda r, e, f: (e, r, 0))]
+ [in_piece] * (2 * parts)
+ [out_piece] * parts,
out_specs=[wide_spec] * 3
+ [pl.BlockSpec((None, row_tile, 128), lambda r, e, f: (e, r, 0))],
out_shape=[wide] * 3 + [jax.ShapeDtypeStruct((count, rows, 128), jnp.float32)],
compiler_params=pltpu.CompilerParams(vmem_limit_bytes=60 * 1024 * 1024),
    )(x, cot, weights, *gates, *ups, *downs)


def back_rows_kernel(parts, gate_grad_ref, up_grad_ref, *refs):
    gates, ups = refs[:parts], refs[parts : 2 * parts]
    out_ref, sum_ref = refs[2 * parts :]
    cols = gates[0].shape[0]
    step = pl.program_id(1) * pl.num_programs(2) + pl.program_id(2)
    last = pl.num_programs(1) * pl.num_programs(2) - 1
    for m in range(parts):
        at = slice(m * cols, (m + 1) * cols)
        part = dot_t(gate_grad_ref[...], gates[m][...]) + dot_t(up_grad_ref[...], ups[m][...])

        @pl.when(step == 0)
        def _():
            sum_ref[:, at] = part

        @pl.when((step > 0) & (step < last))
        def _():
            sum_ref[:, at] += part

        @pl.when(step == last)
        def _():
            out_ref[:, at] = (sum_ref[:, at] + part).astype(jnp.bfloat16)


def back_rows(gate_grad, up_grad, gates, ups, tile=512):
    rows = gate_grad.shape[0]
    parts = len(gates)
    count, cols, ff = gates[0].shape
    row_tile = row_tile_of(rows)
    steps = ff // tile
    wide_spec = pl.BlockSpec((row_tile, tile), lambda r, e, f: (r, e * steps + f))
    piece = pl.BlockSpec((None, cols, tile), lambda r, e, f: (e, 0, f))
    return pl.pallas_call(
functools.partial(back_rows_kernel, parts),
grid=(rows // row_tile, count, steps),
in_specs=[wide_spec] * 2 + [piece] * (2 * parts),
out_specs=pl.BlockSpec((row_tile, parts * cols), lambda r, e, f: (r, 0)),
out_shape=jax.ShapeDtypeStruct((rows, parts * cols), jnp.bfloat16),
scratch_shapes=[pltpu.VMEM((row_tile, parts * cols), jnp.float32)],
compiler_params=pltpu.CompilerParams(vmem_limit_bytes=60 * 1024 * 1024),
    )(gate_grad, up_grad, *gates, *ups)


def local(
    tokens,
    doc_lengths,
    expert_ids,
    attn_gain,
    query_weight,
    key_weight,
    value_weight,
    query_gain,
    key_gain,
    output_weight,
    ffn_gain,
    router_weight,
    gate_weight,
    up_weight,
    down_weight,
    cotangent,
):
    bf16 = jnp.bfloat16
    f32 = jnp.float32
    rows, width = tokens.shape
    owners = lax.axis_size(OWNER)
    parts = lax.axis_size(SHARD)
    w_index = lax.axis_index(SHARD)
    experts = EXP_DEV * owners
    group = parts * rows
    cols = width // parts
    heads = HEADS // parts
    final_rows = width // (owners * parts)
    ff = gate_weight.shape[2]

    e_index = lax.axis_index(OWNER)
    half = cols // 2
    unit = 2 * w_index + e_index % 2
    units = 2 * parts

    docs = doc_lengths.shape[1]
    lengths_row = jnp.zeros((1, cols), bf16).at[:, :docs].set(doc_lengths.astype(bf16))
    small = jnp.concatenate(
        [attn_gain[None, :], ffn_gain[None, :], lengths_row, router_weight.T], axis=0
    )
    small_all = lax.all_gather(small, SHARD, axis=0)
    attn_gain_all = small_all[:, 0, :].reshape(width).astype(f32)
    ffn_gain_all = small_all[:, 1, :].reshape(width).astype(f32)
    lengths_all = small_all[:, 2, :docs].astype(jnp.int32)
    lengths_all = jnp.concatenate([block_of(lengths_all, w_index ^ m, parts, 0) for m in range(parts)])
    router_t = small_all[:, 3:, :].transpose(1, 0, 2).reshape(experts, width)

    *weights_in, tokens_in, _ = lax.optimization_barrier(
        (query_weight, key_weight, value_weight, tokens, small_all)
    )
    tokens_far = gather_far(tokens_in)
    tokens_all = jnp.concatenate(gather_near(tokens_far), axis=0)
    pieces = [None] * units
    for mask in reversed(range(parts)):
        piece = jnp.concatenate(
            [block_of(weight, w_index ^ mask, parts, 1) for weight in weights_in], axis=1
        )
        for side in range(2):
            pieces[2 * mask + side] = block_of(piece, side ^ (e_index % 2), 2, 0)
    for mask in reversed(range(1, parts)):
        pieces[2 * mask] = swap(pieces[2 * mask], mask)
        if mask == 1:
            pieces[3] = swap(pieces[3], 1)
    for mask in reversed(range(2, parts)):
        pieces[2 * mask + 1] = swap(pieces[2 * mask], 1, OWNER)
    cot_b = mixed_order(cotangent, w_index, parts).astype(bf16)
    cot_all = lax.all_gather(cot_b, OWNER, axis=0, tiled=True)
    down_in = after(down_weight, pieces[4])
    down_far = gather_far(down_in)

    unit_all, _ = rms_unit(tokens_all.astype(f32))
    attn_in = (unit_all * attn_gain_all).astype(bf16)
    attn_in_mixed = mixed_order(attn_in, unit, units)
    qkv = 0.0
    for at in [0, 1, 2, 3] + [2 * m for m in range(2, parts)] + [2 * m + 1 for m in range(2, parts)]:
        qkv = qkv + dot(attn_in_mixed[:, at * half : (at + 1) * half], pieces[at])
    query_lin, key_lin, value_lin = (qkv[:, i * cols : (i + 1) * cols] for i in range(3))
    squares = jnp.stack(
        [jnp.sum(query_lin * query_lin, axis=1), jnp.sum(key_lin * key_lin, axis=1)], axis=0
    )
    squares = group_sum(squares)
    inverses = lax.rsqrt(squares / width + epsilon)
    query_inverse = inverses[0][:, None]
    key_inverse = inverses[1][:, None]
    query_unit = query_lin * query_inverse
    key_unit = key_lin * key_inverse
    query_gain_f = query_gain.astype(f32)
    key_gain_f = key_gain.astype(f32)
    allowed, cosine, sine = block_tables(lengths_all, rows)
    scale = HEAD_DIM ** (-0.5)

    def by_head(array):
        return jnp.stack(
            [array[:, h * HEAD_DIM : (h + 1) * HEAD_DIM] for h in range(heads)], axis=0
        )

    def by_row(array):
        return jnp.concatenate([array[h] for h in range(heads)], axis=1)

    blocked = (heads, parts, rows, HEAD_DIM)
    whole = (heads, group, HEAD_DIM)
    queries = rotate(by_head(query_unit * query_gain_f), cosine, sine).astype(bf16)
    queries = queries.reshape(blocked)
    keys = rotate(by_head(key_unit * key_gain_f), cosine, sine).astype(bf16).reshape(blocked)
    values = by_head(value_lin).astype(bf16).reshape(blocked)
    scores = pair_dot(queries, keys, 3, 3) * scale
    scores = jnp.where(allowed[None, :, :, :], scores, -1e30)
    row_max = jnp.max(scores, axis=-1, keepdims=True)
    log_total = row_max + jnp.log(jnp.sum(jnp.exp(scores - row_max), axis=-1, keepdims=True))
    probs = jnp.exp(scores - log_total)
    probs_b = probs.astype(bf16)
    mixed = pair_dot(probs_b, values, 3, 2).astype(bf16)
    attn_mix = by_row(mixed.reshape(whole))
    attn_out = dot(attn_mix, output_weight)
    attn_out = scatter_pieces([attn_out[mask * rows : (mask + 1) * rows] for mask in range(parts)])
    attn_out, *pieces = lax.optimization_barrier((attn_out, *pieces))
    qkv_w = jnp.concatenate(pieces, axis=0)
    qkv_w = jnp.concatenate(
        [block_of(qkv_w, unit ^ k, units, 0) for k in range(units)], axis=0
    )

    residual = tokens.astype(f32)
    middle = residual + attn_out
    unit_two, inverse_two = rms_unit(middle)
    ffn_in = (unit_two * ffn_gain_all).astype(bf16)
    ffn_in_mixed = mixed_order(ffn_in, w_index, parts)
    gate_in, up_in, ffn_in_mixed, ffn_in = lax.optimization_barrier(
        (gate_weight, up_weight, ffn_in_mixed, ffn_in)
    )
    gate_far = gather_far(gate_in)
    up_far = gather_far(up_in)
    router_probs = softmax_rows(dot_t(ffn_in, router_t))
    expert_range = jnp.arange(experts, dtype=jnp.int32)
    named = jnp.any(expert_ids[:, :, None] == expert_range[None, None, :], axis=1)
    route_table = jnp.where(named, router_probs, 0.0)

    arrived = lax.all_gather(ffn_in_mixed, OWNER, axis=0, tiled=True)
    weights = lax.all_to_all(
        route_table.reshape(rows, owners, EXP_DEV).transpose(1, 2, 0),
        OWNER,
        split_axis=0,
        concat_axis=0,
        tiled=True,
    )
    weights = weights.transpose(1, 0, 2).reshape(EXP_DEV, owners * rows, 1)
    gate_pieces = gather_near(gate_far)
    up_pieces = gather_near(
        {m: after(p, weights, gate_pieces[-1]) if m else p for m, p in up_far.items()}
    )
    down_pieces = gather_near({m: after(p, attn_out) if m else p for m, p in down_far.items()})
    hidden_w, gate_grad_b, up_grad_b, route_part = expert_hidden(
        arrived, cot_all, weights, gate_pieces, up_pieces, down_pieces
    )
    row_partial = back_rows(gate_grad_b, up_grad_b, gate_pieces, up_pieces)
    row_grads = lax.psum_scatter(row_partial, OWNER, scatter_dimension=0, tiled=True)
    route_back = jnp.sum(route_part, axis=2)
    route_back = lax.all_to_all(
        route_back.reshape(EXP_DEV, owners, rows).transpose(1, 0, 2),
        OWNER,
        split_axis=0,
        concat_axis=0,
        tiled=True,
    )
    part_of = lambda array, mask: array[:, mask * cols : (mask + 1) * cols]
    order = sorted(range(parts), key=lambda m: (m < parts // 2, -m))

    def ordered_blocks(make):
        blocks = [None] * parts
        for mask in order:
            blocks[mask] = make(mask)
        return blocks

    gate_blocks = ordered_blocks(lambda m: t_dot(part_of(arrived, m), gate_grad_b))
    gate_near = scatter_near(gate_blocks)
    up_blocks = ordered_blocks(lambda m: t_dot(part_of(arrived, m), up_grad_b))
    up_near = scatter_near(up_blocks)
    hidden_w, qkv_w, *_ = lax.optimization_barrier((hidden_w, qkv_w, *gate_blocks, *up_blocks))
    down_blocks = ordered_blocks(lambda m: t_dot(hidden_w, part_of(cot_all, m)))
    down_near = scatter_near(down_blocks)
    gate_sum = scatter_far(gate_near)
    gate_weight_grad = jnp.stack([gate_sum[:, e * ff : (e + 1) * ff] for e in range(EXP_DEV)])
    down_all = jnp.concatenate(
        [piece.reshape(EXP_DEV * ff, cols) for piece in down_pieces], axis=1
    )
    out_partial = dot(hidden_w, down_all)
    out_partial = out_partial.astype(bf16)
    row_grads, route_back = lax.optimization_barrier((row_grads, route_back))
    moe_out = owner_scatter(out_partial.reshape(owners, rows, width))

    route_grad = route_back.reshape(experts, rows).T
    prob_grad = jnp.where(named, route_grad, 0.0)
    logit_grad = router_probs * (
        prob_grad - jnp.sum(router_probs * prob_grad, axis=1, keepdims=True)
    )
    logit_grad_b = logit_grad.astype(bf16)
    ffn_in_grad = mixed_order(row_grads, w_index, parts).astype(f32) + dot(logit_grad_b, router_t)
    middle_part, ffn_gain_grad = rms_backward(ffn_in_grad, unit_two, inverse_two, ffn_gain_all)
    middle_grad = cotangent + middle_part
    router_grad = t_dot(logit_grad_b, ffn_in)

    mid_pieces = gather_pieces(middle_grad.astype(bf16))
    mid_all = jnp.concatenate(mid_pieces, axis=0)
    output_part = t_dot(attn_mix, mid_all).astype(bf16)
    output_sum = owner_scatter(output_part.reshape(owners, final_rows, width), turn=1)
    mix_grad = dot_t(mid_all, output_weight).astype(bf16)
    grad_queries, grad_keys, value_grad_b = attend_back(
        mix_grad,
        queries,
        keys,
        values,
        mixed,
        probs,
        jnp.concatenate([cosine, cosine], axis=1),
        jnp.concatenate([sine, -sine], axis=1),
    )
    query_gain_grad = jnp.sum(grad_queries * query_unit, axis=0)
    key_gain_grad = jnp.sum(grad_keys * key_unit, axis=0)
    grad_queries = grad_queries * query_gain_f
    grad_keys = grad_keys * key_gain_f
    means = jnp.stack(
        [jnp.sum(grad_queries * query_unit, axis=1), jnp.sum(grad_keys * key_unit, axis=1)], axis=0
    )
    means = group_sum(means) / width
    up_sum = scatter_far(after(up_near, means))
    up_weight_grad = jnp.stack([up_sum[:, e * ff : (e + 1) * ff] for e in range(EXP_DEV)])
    query_grad_b = (query_inverse * (grad_queries - query_unit * means[0][:, None])).astype(bf16)
    key_grad_b = (key_inverse * (grad_keys - key_unit * means[1][:, None])).astype(bf16)
    qkv_grad = jnp.concatenate([query_grad_b, key_grad_b, value_grad_b], axis=1)
    query_part = t_dot(attn_in, query_grad_b)
    key_part = t_dot(attn_in, key_grad_b)
    query_part, key_part = query_part.astype(bf16), key_part.astype(bf16)
    qkv_grad = after(qkv_grad, query_part, key_part)
    attn_in_part = dot_t(qkv_grad, qkv_w)
    attn_in_grad = scatter_pieces(
        [attn_in_part[mask * rows : (mask + 1) * rows] for mask in range(parts)]
    )
    value_part = t_dot(attn_in, value_grad_b).astype(bf16).reshape(owners, parts * final_rows, cols)
    down_weight_grad = scatter_far(after(down_near, attn_in_part)).reshape(EXP_DEV, ff, cols)
    value_sum = owner_scatter(value_part)
    cut = (owners, parts * final_rows, cols)
    query_sum = owner_scatter(query_part.reshape(cut))
    key_sum = owner_scatter(key_part.reshape(cut))

    unit_one, inverse_one = rms_unit(residual)
    input_part, attn_gain_grad = rms_backward(
        attn_in_grad, unit_one, inverse_one, attn_gain_all
    )
    tokens_grad = middle_grad + input_part
    moe_out = after(moe_out, attn_in_part)
    block_output = middle + mixed_order(moe_out, w_index, parts).astype(f32)

    qkv_sum = jnp.concatenate([query_sum, key_sum, value_sum], axis=1)
    qkv_sum = qkv_sum.reshape(parts, final_rows, 3 * cols)
    qkv_sum = lax.all_to_all(qkv_sum, SHARD, split_axis=0, concat_axis=0, tiled=True)
    qkv_sum = place(qkv_sum)
    moves = []
    for e in range(owners):
        for w in range(parts):
            moves.append((e * parts + w, w * owners + e))
    output_sum = lax.ppermute(output_sum, (OWNER, SHARD), moves).astype(f32)

    own = jnp.zeros((2, parts, cols), f32)
    own = lax.dynamic_update_slice(
        own, jnp.stack([query_gain_grad, key_gain_grad])[:, None, :], (0, w_index, 0)
    ).reshape(2, width)
    table = jnp.concatenate([attn_gain_grad[None], ffn_gain_grad[None], own, router_grad], axis=0)
    count = table.shape[0]
    table = table.reshape(count, owners, parts * final_rows).transpose(1, 0, 2)
    table = lax.all_to_all(table, OWNER, split_axis=0, concat_axis=0, tiled=True)
    table = jnp.sum(table, axis=0)
    table = table.reshape(count, parts, final_rows).transpose(1, 0, 2)
    table = jnp.sum(
        lax.all_to_all(table, SHARD, split_axis=0, concat_axis=0, tiled=True), axis=0
    )
    return (
        block_output,
        tokens_grad,
        table[0],
        qkv_sum[0],
        qkv_sum[1],
        qkv_sum[2],
        table[2],
        table[3],
        output_sum,
        table[1],
        table[4:].T,
        gate_weight_grad,
        up_weight_grad,
        down_weight_grad,
    )


def solution(mesh):
    rows = P((OWNER, SHARD), None)
    line = P((OWNER, SHARD))
    part = P(SHARD)
    wide = P(SHARD, None)
    into = P(OWNER, SHARD, None)
    back = P(OWNER, None, SHARD)
    in_specs = (rows,) * 3 + (part, wide, wide, wide, part, part, wide, part, wide)
    in_specs = in_specs + (into, into, back, rows)
    out_specs = (rows, rows, line, rows, rows, rows, line, line, rows, line, rows)
    out_specs = out_specs + (into, into, back)

    return jax.shard_map(local, mesh=mesh, in_specs=in_specs, out_specs=out_specs, check_vma=False)
```

```python
import functools

import jax
import jax.numpy as jnp
from jax import lax
from jax.experimental import pallas as pl
from jax.experimental.pallas import tpu as pltpu
from jax.sharding import PartitionSpec as P


HEADS = 16
HEAD_DIM = 128
EXP_DEV = 2
OWNER = "expert"
SHARD = "wshard"


epsilon = 1e-05
theta_base = 10000.0


def rms_unit(activation):
    inverse = lax.rsqrt(jnp.mean(activation * activation, axis=-1, keepdims=True) + epsilon)
    return (activation * inverse, inverse)


def rms_backward(grad_out, normed, inverse, gain):
    gain_grad = jnp.sum(grad_out * normed, axis=0)
    grad_normed = grad_out * gain
    centred = grad_normed - normed * jnp.mean(grad_normed * normed, axis=-1, keepdims=True)
    return (inverse * centred, gain_grad)


def block_tables(lengths, rows):
    ends = jnp.cumsum(lengths, axis=1)
    row_index = jnp.arange(rows, dtype=jnp.int32)
    passed = (row_index[None, :, None] >= ends[:, None, :]).astype(jnp.int32)
    start = jnp.sum(passed * lengths[:, None, :], axis=2)
    allowed = (row_index[None, None, :] <= row_index[None, :, None]) & (
        row_index[None, None, :] >= start[:, :, None]
    )
    offsets = (row_index[None, :] - start).reshape(-1)
    half_dim = HEAD_DIM // 2
    frequency = theta_base ** (-2.0 * jnp.arange(half_dim, dtype=jnp.float32) / HEAD_DIM)
    angles = offsets.astype(jnp.float32)[:, None] * frequency[None, :]
    return (allowed, jnp.cos(angles), jnp.sin(angles))


def rotate(rows, cosine, sine):
    half_dim = HEAD_DIM // 2
    first = rows[..., :half_dim]
    second = rows[..., half_dim:]
    cosine = cosine[None, :, :]
    sine = sine[None, :, :]
    return jnp.concatenate([first * cosine - second * sine, second * cosine + first * sine], axis=-1)


def softmax_rows(logits):
    row_max = jnp.max(logits, axis=-1, keepdims=True)
    shifted = jnp.exp(logits - row_max)
    return shifted / jnp.sum(shifted, axis=-1, keepdims=True)


def dot(a, b):
    return jnp.dot(a, b, preferred_element_type=jnp.float32)


def dot_t(a, b):
    return lax.dot_general(a, b, (((1,), (1,)), ((), ())), preferred_element_type=jnp.float32)


def t_dot(a, b):
    return lax.dot_general(a, b, (((0,), (0,)), ((), ())), preferred_element_type=jnp.float32)


def swap(values, mask, axis_name=SHARD):
    count = lax.axis_size(axis_name)
    return lax.ppermute(values, axis_name, [(i, i ^ mask) for i in range(count)])


def after(values, *others):
    return lax.optimization_barrier((values, *others))[0]


def bits_of(count):
    return [1 << k for k in range(count.bit_length() - 1)]


def gather_far(shard):
    pieces = {0: shard}
    for bit in reversed(bits_of(lax.axis_size(SHARD))[1:]):
        for mask in list(pieces):
            pieces[mask ^ bit] = swap(pieces[mask], bit)
    return pieces


def gather_near(pieces):
    pieces = dict(pieces)
    for mask in list(pieces):
        pieces[mask ^ 1] = swap(pieces[mask], 1)
    return [pieces[mask] for mask in sorted(pieces)]


def gather_pieces(shard):
    return gather_near(gather_far(shard))


def scatter_stage(blocks, bit):
    masks = sorted(blocks, reverse=True)
    arrived = {m ^ bit: swap(blocks[m].astype(jnp.bfloat16), bit) for m in masks if m & bit}
    return {m: blocks[m] + arrived[m].astype(jnp.float32) for m in arrived}


def scatter_near(blocks):
    return scatter_stage(dict(enumerate(blocks)), 1)


def scatter_far(blocks):
    for bit in bits_of(lax.axis_size(SHARD))[1:]:
        blocks = scatter_stage(blocks, bit)
    return blocks[0]


def scatter_pieces(blocks):
    return scatter_far(scatter_near(blocks))


def block_of(array, index, count, axis):
    size = array.shape[axis] // count
    return lax.dynamic_slice_in_dim(array, index * size, size, axis)


def mixed_order(array, w_index, count):
    return jnp.concatenate(
        [block_of(array, w_index ^ mask, count, array.ndim - 1) for mask in range(count)], axis=-1
    )


def pair_dot(a, b, a_axis, b_axis):
    dims = (((a_axis,), (b_axis,)), ((0, 1), (0, 1)))
    return lax.dot_general(a, b, dims, preferred_element_type=jnp.float32)


def group_sum(values):
    count = lax.axis_size(SHARD)
    blocks = values.reshape(values.shape[0], count, -1)
    total = blocks
    for mask in reversed(range(1, count)):
        arrived = swap(blocks, mask)
        total = total + jnp.stack([arrived[:, m ^ mask] for m in range(count)], axis=1)
    return total.reshape(values.shape)


def owner_bits():
    return bits_of(lax.axis_size(OWNER))[::-1]


def owner_split(values):
    return values.reshape([2] * len(owner_bits()) + list(values.shape[1:]))


def owner_stage(values, left, bit):
    index = (lax.axis_index(OWNER) // bit) % 2
    axis = left.index(bit)
    away = lax.dynamic_index_in_dim(values, 1 - index, axis, keepdims=False)
    kept = lax.dynamic_index_in_dim(values, index, axis, keepdims=False)
    arrived = swap(away, bit, OWNER)
    total = (kept.astype(jnp.float32) + arrived.astype(jnp.float32)).astype(jnp.bfloat16)
    return total, [b for b in left if b != bit]


def owner_scatter(values, turn=0):
    values, left = owner_split(values), owner_bits()
    for bit in left[::-1][turn:] + left[::-1][:turn]:
        values, left = owner_stage(values, left, bit)
    return values


def place_kernel(values_ref, *out_refs):
    parts, _, cols = values_ref.shape
    cols = cols // 3
    for k in range(3):
        for p in range(parts):
            out_refs[k][:, p * cols : (p + 1) * cols] = values_ref[
                p, :, k * cols : (k + 1) * cols
            ].astype(jnp.float32)


def place(values):
    parts, rows, cols = values.shape
    shape = jax.ShapeDtypeStruct((rows, parts * cols // 3), jnp.float32)
    return pl.pallas_call(place_kernel, out_shape=[shape] * 3)(values)


def expert_hidden_kernel(parts, x_ref, cot_ref, weight_ref, *refs):
    gates, ups, downs = refs[:parts], refs[parts : 2 * parts], refs[2 * parts : 3 * parts]
    hidden_ref, gate_grad_ref, up_grad_ref, route_ref = refs[3 * parts :]
    cols = gates[0].shape[0]
    f32 = jnp.float32
    gate_lin = up_lin = back = 0.0
    for m in range(parts):
        x = x_ref[:, m * cols : (m + 1) * cols]
        gate_lin = gate_lin + jnp.dot(x, gates[m][...], preferred_element_type=f32)
        up_lin = up_lin + jnp.dot(x, ups[m][...], preferred_element_type=f32)
        back = back + dot_t(cot_ref[:, m * cols : (m + 1) * cols], downs[m][...])
    weight = weight_ref[...]
    sigmoid = jax.nn.sigmoid(gate_lin)
    swish = gate_lin * sigmoid
    hidden = swish * up_lin
    product = hidden * back
    route = product[:, :128]
    for k in range(1, product.shape[1] // 128):
        route = route + product[:, k * 128 : (k + 1) * 128]
    hidden_ref[...] = (hidden * weight).astype(jnp.bfloat16)
    grad = back * weight
    gate_grad_ref[...] = (grad * up_lin * sigmoid * (1.0 + gate_lin * (1.0 - sigmoid))).astype(
        jnp.bfloat16
    )
    up_grad_ref[...] = (grad * swish).astype(jnp.bfloat16)

    @pl.when(pl.program_id(2) == 0)
    def _():
        route_ref[...] = route

    @pl.when(pl.program_id(2) > 0)
    def _():
        route_ref[...] += route


def attend_back_kernel(
    grad_ref, query_ref, key_ref, value_ref, mix_ref, probs_ref, cos_ref, sin_ref, *out_refs
):
    query_out, key_out, value_out = out_refs
    f32, bf16 = jnp.float32, jnp.bfloat16
    scale = HEAD_DIM ** (-0.5)
    cosine = cos_ref[...]
    sine = sin_ref[...]
    for h in range(query_ref.shape[0]):
        at = slice(h * HEAD_DIM, (h + 1) * HEAD_DIM)
        grad = grad_ref[:, at]
        probs = probs_ref[h]
        delta = jnp.sum(grad.astype(f32) * mix_ref[h].astype(f32), axis=1, keepdims=True)
        score = probs * (dot_t(grad, value_ref[h]) - delta)
        query = jnp.dot(score.astype(bf16), key_ref[h], preferred_element_type=f32) * scale
        key = jnp.dot(score.T.astype(bf16), query_ref[h], preferred_element_type=f32) * scale
        value = jnp.dot(probs.T.astype(bf16), grad, preferred_element_type=f32)
        query = query * cosine + pltpu.roll(query, HEAD_DIM // 2, 1) * sine
        key = key * cosine + pltpu.roll(key, HEAD_DIM // 2, 1) * sine
        query_out[:, at] = query
        key_out[:, at] = key
        value_out[:, at] = value.astype(bf16)


def attend_back(grad, queries, keys, values, mixed, probs, cosine, sine):
    heads, blocks, rows, _ = queries.shape
    cols = grad.shape[1]
    head = pl.BlockSpec((heads, None, rows, HEAD_DIM), lambda b: (0, b, 0, 0))
    line = pl.BlockSpec((rows, cols), lambda b: (b, 0))
    table = pl.BlockSpec((rows, HEAD_DIM), lambda b: (b, 0))
    wide = jax.ShapeDtypeStruct(grad.shape, jnp.float32)
    return pl.pallas_call(
        attend_back_kernel,
        grid=(blocks,),
        in_specs=[line] + [head] * 4
        + [pl.BlockSpec((heads, None, rows, rows), lambda b: (0, b, 0, 0)), table, table],
        out_specs=[line] * 3,
        out_shape=[wide, wide, jax.ShapeDtypeStruct(grad.shape, jnp.bfloat16)],
    )(grad, queries, keys, values, mixed, probs, cosine, sine)


def row_tile_of(rows):
    return min(rows, 1024)


def expert_hidden(x, cot, weights, gates, ups, downs, tile=256):
    rows, width = x.shape
    parts = len(gates)
    count, cols, ff = gates[0].shape
    row_tile = row_tile_of(rows)
    steps = ff // tile
    row_spec = pl.BlockSpec((row_tile, width), lambda r, e, f: (r, 0))
    in_piece = pl.BlockSpec((None, cols, tile), lambda r, e, f: (e, 0, f))
    out_piece = pl.BlockSpec((None, tile, cols), lambda r, e, f: (e, f, 0))
    wide_spec = pl.BlockSpec((row_tile, tile), lambda r, e, f: (r, e * steps + f))
    wide = jax.ShapeDtypeStruct((rows, count * ff), jnp.bfloat16)
    return pl.pallas_call(
functools.partial(expert_hidden_kernel, parts),
grid=(rows // row_tile, count, steps),
in_specs=[row_spec, row_spec, pl.BlockSpec((None, row_tile, 1), lambda r, e, f: (e, r, 0))]
+ [in_piece] * (2 * parts)
+ [out_piece] * parts,
out_specs=[wide_spec] * 3
+ [pl.BlockSpec((None, row_tile, 128), lambda r, e, f: (e, r, 0))],
out_shape=[wide] * 3 + [jax.ShapeDtypeStruct((count, rows, 128), jnp.float32)],
compiler_params=pltpu.CompilerParams(vmem_limit_bytes=60 * 1024 * 1024),
    )(x, cot, weights, *gates, *ups, *downs)


def back_rows_kernel(parts, gate_grad_ref, up_grad_ref, *refs):
    gates, ups = refs[:parts], refs[parts : 2 * parts]
    out_ref, sum_ref = refs[2 * parts :]
    cols = gates[0].shape[0]
    step = pl.program_id(1) * pl.num_programs(2) + pl.program_id(2)
    last = pl.num_programs(1) * pl.num_programs(2) - 1
    for m in range(parts):
        at = slice(m * cols, (m + 1) * cols)
        part = dot_t(gate_grad_ref[...], gates[m][...]) + dot_t(up_grad_ref[...], ups[m][...])

        @pl.when(step == 0)
        def _():
            sum_ref[:, at] = part

        @pl.when((step > 0) & (step < last))
        def _():
            sum_ref[:, at] += part

        @pl.when(step == last)
        def _():
            out_ref[:, at] = (sum_ref[:, at] + part).astype(jnp.bfloat16)


def back_rows(gate_grad, up_grad, gates, ups, tile=512):
    rows = gate_grad.shape[0]
    parts = len(gates)
    count, cols, ff = gates[0].shape
    row_tile = row_tile_of(rows)
    steps = ff // tile
    wide_spec = pl.BlockSpec((row_tile, tile), lambda r, e, f: (r, e * steps + f))
    piece = pl.BlockSpec((None, cols, tile), lambda r, e, f: (e, 0, f))
    return pl.pallas_call(
functools.partial(back_rows_kernel, parts),
grid=(rows // row_tile, count, steps),
in_specs=[wide_spec] * 2 + [piece] * (2 * parts),
out_specs=pl.BlockSpec((row_tile, parts * cols), lambda r, e, f: (r, 0)),
out_shape=jax.ShapeDtypeStruct((rows, parts * cols), jnp.bfloat16),
scratch_shapes=[pltpu.VMEM((row_tile, parts * cols), jnp.float32)],
compiler_params=pltpu.CompilerParams(vmem_limit_bytes=60 * 1024 * 1024),
    )(gate_grad, up_grad, *gates, *ups)


def local(
    tokens,
    doc_lengths,
    expert_ids,
    attn_gain,
    query_weight,
    key_weight,
    value_weight,
    query_gain,
    key_gain,
    output_weight,
    ffn_gain,
    router_weight,
    gate_weight,
    up_weight,
    down_weight,
    cotangent,
):
    bf16 = jnp.bfloat16
    f32 = jnp.float32
    rows, width = tokens.shape
    owners = lax.axis_size(OWNER)
    parts = lax.axis_size(SHARD)
    w_index = lax.axis_index(SHARD)
    experts = EXP_DEV * owners
    group = parts * rows
    cols = width // parts
    heads = HEADS // parts
    final_rows = width // (owners * parts)
    ff = gate_weight.shape[2]

    e_index = lax.axis_index(OWNER)
    half = cols // 2
    unit = 2 * w_index + e_index % 2
    units = 2 * parts

    docs = doc_lengths.shape[1]
    lengths_row = jnp.zeros((1, cols), bf16).at[:, :docs].set(doc_lengths.astype(bf16))
    small = jnp.concatenate(
        [attn_gain[None, :], ffn_gain[None, :], lengths_row, router_weight.T], axis=0
    )
    small_all = lax.all_gather(small, SHARD, axis=0)
    attn_gain_all = small_all[:, 0, :].reshape(width).astype(f32)
    ffn_gain_all = small_all[:, 1, :].reshape(width).astype(f32)
    lengths_all = small_all[:, 2, :docs].astype(jnp.int32)
    lengths_all = jnp.concatenate([block_of(lengths_all, w_index ^ m, parts, 0) for m in range(parts)])
    router_t = small_all[:, 3:, :].transpose(1, 0, 2).reshape(experts, width)

    *weights_in, tokens_in, _ = lax.optimization_barrier(
        (query_weight, key_weight, value_weight, tokens, small_all)
    )
    tokens_far = gather_far(tokens_in)
    tokens_all = jnp.concatenate(gather_near(tokens_far), axis=0)
    pieces = [None] * units
    for mask in reversed(range(parts)):
        piece = jnp.concatenate(
            [block_of(weight, w_index ^ mask, parts, 1) for weight in weights_in], axis=1
        )
        for side in range(2):
            pieces[2 * mask + side] = block_of(piece, side ^ (e_index % 2), 2, 0)
    for mask in reversed(range(1, parts)):
        pieces[2 * mask] = swap(pieces[2 * mask], mask)
        if mask == 1:
            pieces[3] = swap(pieces[3], 1)
    for mask in reversed(range(2, parts)):
        pieces[2 * mask + 1] = swap(pieces[2 * mask], 1, OWNER)
    cot_b = mixed_order(cotangent, w_index, parts).astype(bf16)
    cot_all = lax.all_gather(cot_b, OWNER, axis=0, tiled=True)
    down_in = after(down_weight, pieces[4])
    down_far = gather_far(down_in)

    unit_all, _ = rms_unit(tokens_all.astype(f32))
    attn_in = (unit_all * attn_gain_all).astype(bf16)
    attn_in_mixed = mixed_order(attn_in, unit, units)
    qkv = 0.0
    for at in [0, 1, 2, 3] + [2 * m for m in range(2, parts)] + [2 * m + 1 for m in range(2, parts)]:
        qkv = qkv + dot(attn_in_mixed[:, at * half : (at + 1) * half], pieces[at])
    query_lin, key_lin, value_lin = (qkv[:, i * cols : (i + 1) * cols] for i in range(3))
    squares = jnp.stack(
        [jnp.sum(query_lin * query_lin, axis=1), jnp.sum(key_lin * key_lin, axis=1)], axis=0
    )
    squares = group_sum(squares)
    inverses = lax.rsqrt(squares / width + epsilon)
    query_inverse = inverses[0][:, None]
    key_inverse = inverses[1][:, None]
    query_unit = query_lin * query_inverse
    key_unit = key_lin * key_inverse
    query_gain_f = query_gain.astype(f32)
    key_gain_f = key_gain.astype(f32)
    allowed, cosine, sine = block_tables(lengths_all, rows)
    scale = HEAD_DIM ** (-0.5)

    def by_head(array):
        return jnp.stack(
            [array[:, h * HEAD_DIM : (h + 1) * HEAD_DIM] for h in range(heads)], axis=0
        )

    def by_row(array):
        return jnp.concatenate([array[h] for h in range(heads)], axis=1)

    blocked = (heads, parts, rows, HEAD_DIM)
    whole = (heads, group, HEAD_DIM)
    queries = rotate(by_head(query_unit * query_gain_f), cosine, sine).astype(bf16)
    queries = queries.reshape(blocked)
    keys = rotate(by_head(key_unit * key_gain_f), cosine, sine).astype(bf16).reshape(blocked)
    values = by_head(value_lin).astype(bf16).reshape(blocked)
    scores = pair_dot(queries, keys, 3, 3) * scale
    scores = jnp.where(allowed[None, :, :, :], scores, -1e30)
    row_max = jnp.max(scores, axis=-1, keepdims=True)
    log_total = row_max + jnp.log(jnp.sum(jnp.exp(scores - row_max), axis=-1, keepdims=True))
    probs = jnp.exp(scores - log_total)
    probs_b = probs.astype(bf16)
    mixed = pair_dot(probs_b, values, 3, 2).astype(bf16)
    attn_mix = by_row(mixed.reshape(whole))
    attn_out = dot(attn_mix, output_weight)
    attn_out = scatter_pieces([attn_out[mask * rows : (mask + 1) * rows] for mask in range(parts)])
    attn_out, *pieces = lax.optimization_barrier((attn_out, *pieces))
    qkv_w = jnp.concatenate(pieces, axis=0)
    qkv_w = jnp.concatenate(
        [block_of(qkv_w, unit ^ k, units, 0) for k in range(units)], axis=0
    )

    residual = tokens.astype(f32)
    middle = residual + attn_out
    unit_two, inverse_two = rms_unit(middle)
    ffn_in = (unit_two * ffn_gain_all).astype(bf16)
    ffn_in_mixed = mixed_order(ffn_in, w_index, parts)
    gate_in, up_in, ffn_in_mixed, ffn_in = lax.optimization_barrier(
        (gate_weight, up_weight, ffn_in_mixed, ffn_in)
    )
    gate_far = gather_far(gate_in)
    up_far = gather_far(up_in)
    router_probs = softmax_rows(dot_t(ffn_in, router_t))
    expert_range = jnp.arange(experts, dtype=jnp.int32)
    named = jnp.any(expert_ids[:, :, None] == expert_range[None, None, :], axis=1)
    route_table = jnp.where(named, router_probs, 0.0)

    arrived = lax.all_gather(ffn_in_mixed, OWNER, axis=0, tiled=True)
    weights = lax.all_to_all(
        route_table.reshape(rows, owners, EXP_DEV).transpose(1, 2, 0),
        OWNER,
        split_axis=0,
        concat_axis=0,
        tiled=True,
    )
    weights = weights.transpose(1, 0, 2).reshape(EXP_DEV, owners * rows, 1)
    gate_pieces = gather_near(gate_far)
    up_pieces = gather_near(
        {m: after(p, weights, gate_pieces[-1]) if m else p for m, p in up_far.items()}
    )
    down_pieces = gather_near({m: after(p, attn_out) if m else p for m, p in down_far.items()})
    hidden_w, gate_grad_b, up_grad_b, route_part = expert_hidden(
        arrived, cot_all, weights, gate_pieces, up_pieces, down_pieces
    )
    row_partial = back_rows(gate_grad_b, up_grad_b, gate_pieces, up_pieces)
    row_grads = lax.psum_scatter(row_partial, OWNER, scatter_dimension=0, tiled=True)
    route_back = jnp.sum(route_part, axis=2)
    route_back = lax.all_to_all(
        route_back.reshape(EXP_DEV, owners, rows).transpose(1, 0, 2),
        OWNER,
        split_axis=0,
        concat_axis=0,
        tiled=True,
    )
    part_of = lambda array, mask: array[:, mask * cols : (mask + 1) * cols]
    order = sorted(range(parts), key=lambda m: (m < parts // 2, -m))

    def ordered_blocks(make):
        blocks = [None] * parts
        for mask in order:
            blocks[mask] = make(mask)
        return blocks

    gate_blocks = ordered_blocks(lambda m: t_dot(part_of(arrived, m), gate_grad_b))
    gate_near = scatter_near(gate_blocks)
    up_blocks = ordered_blocks(lambda m: t_dot(part_of(arrived, m), up_grad_b))
    up_near = scatter_near(up_blocks)
    hidden_w, qkv_w, *_ = lax.optimization_barrier((hidden_w, qkv_w, *gate_blocks, *up_blocks))
    down_blocks = ordered_blocks(lambda m: t_dot(hidden_w, part_of(cot_all, m)))
    down_near = scatter_near(down_blocks)
    gate_sum = scatter_far(gate_near)
    gate_weight_grad = jnp.stack([gate_sum[:, e * ff : (e + 1) * ff] for e in range(EXP_DEV)])
    down_all = jnp.concatenate(
        [piece.reshape(EXP_DEV * ff, cols) for piece in down_pieces], axis=1
    )
    out_partial = dot(hidden_w, down_all)
    out_partial = out_partial.astype(bf16)
    row_grads, route_back = lax.optimization_barrier((row_grads, route_back))
    moe_out = owner_scatter(out_partial.reshape(owners, rows, width))

    route_grad = route_back.reshape(experts, rows).T
    prob_grad = jnp.where(named, route_grad, 0.0)
    logit_grad = router_probs * (
        prob_grad - jnp.sum(router_probs * prob_grad, axis=1, keepdims=True)
    )
    logit_grad_b = logit_grad.astype(bf16)
    ffn_in_grad = mixed_order(row_grads, w_index, parts).astype(f32) + dot(logit_grad_b, router_t)
    middle_part, ffn_gain_grad = rms_backward(ffn_in_grad, unit_two, inverse_two, ffn_gain_all)
    middle_grad = cotangent + middle_part
    router_grad = t_dot(logit_grad_b, ffn_in)

    mid_pieces = gather_pieces(middle_grad.astype(bf16))
    mid_all = jnp.concatenate(mid_pieces, axis=0)
    output_part = t_dot(attn_mix, mid_all).astype(bf16)
    output_sum = owner_scatter(output_part.reshape(owners, final_rows, width), turn=1)
    mix_grad = dot_t(mid_all, output_weight).astype(bf16)
    grad_queries, grad_keys, value_grad_b = attend_back(
        mix_grad,
        queries,
        keys,
        values,
        mixed,
        probs,
        jnp.concatenate([cosine, cosine], axis=1),
        jnp.concatenate([sine, -sine], axis=1),
    )
    query_gain_grad = jnp.sum(grad_queries * query_unit, axis=0)
    key_gain_grad = jnp.sum(grad_keys * key_unit, axis=0)
    grad_queries = grad_queries * query_gain_f
    grad_keys = grad_keys * key_gain_f
    means = jnp.stack(
        [jnp.sum(grad_queries * query_unit, axis=1), jnp.sum(grad_keys * key_unit, axis=1)], axis=0
    )
    means = group_sum(means) / width
    up_sum = scatter_far(after(up_near, means))
    up_weight_grad = jnp.stack([up_sum[:, e * ff : (e + 1) * ff] for e in range(EXP_DEV)])
    query_grad_b = (query_inverse * (grad_queries - query_unit * means[0][:, None])).astype(bf16)
    key_grad_b = (key_inverse * (grad_keys - key_unit * means[1][:, None])).astype(bf16)
    qkv_grad = jnp.concatenate([query_grad_b, key_grad_b, value_grad_b], axis=1)
    query_part = t_dot(attn_in, query_grad_b)
    key_part = t_dot(attn_in, key_grad_b)
    query_part, key_part = query_part.astype(bf16), key_part.astype(bf16)
    qkv_grad = after(qkv_grad, query_part, key_part)
    attn_in_part = dot_t(qkv_grad, qkv_w)
    attn_in_grad = scatter_pieces(
        [attn_in_part[mask * rows : (mask + 1) * rows] for mask in range(parts)]
    )
    value_part = t_dot(attn_in, value_grad_b).astype(bf16).reshape(owners, parts * final_rows, cols)
    down_weight_grad = scatter_far(after(down_near, attn_in_part)).reshape(EXP_DEV, ff, cols)
    value_sum = owner_scatter(value_part)
    cut = (owners, parts * final_rows, cols)
    query_sum = owner_scatter(query_part.reshape(cut))
    key_sum = owner_scatter(key_part.reshape(cut))

    unit_one, inverse_one = rms_unit(residual)
    input_part, attn_gain_grad = rms_backward(attn_in_grad, unit_one, inverse_one, attn_gain_all)
    tokens_grad = middle_grad + input_part
    moe_out = after(moe_out, attn_in_part)
    block_output = middle + mixed_order(moe_out, w_index, parts).astype(f32)

    qkv_sum = jnp.concatenate([query_sum, key_sum, value_sum], axis=1)
    qkv_sum = qkv_sum.reshape(parts, final_rows, 3 * cols)
    qkv_sum = lax.all_to_all(qkv_sum, SHARD, split_axis=0, concat_axis=0, tiled=True)
    qkv_sum = place(qkv_sum)
    moves = []
    for e in range(owners):
        for w in range(parts):
            moves.append((e * parts + w, w * owners + e))
    output_sum = lax.ppermute(output_sum, (OWNER, SHARD), moves).astype(f32)

    own = jnp.zeros((2, parts, cols), f32)
    own = lax.dynamic_update_slice(
        own, jnp.stack([query_gain_grad, key_gain_grad])[:, None, :], (0, w_index, 0)
    ).reshape(2, width)
    table = jnp.concatenate([attn_gain_grad[None], ffn_gain_grad[None], own, router_grad], axis=0)
    count = table.shape[0]
    table = table.reshape(count, owners, parts * final_rows).transpose(1, 0, 2)
    table = lax.all_to_all(table, OWNER, split_axis=0, concat_axis=0, tiled=True)
    table = jnp.sum(table, axis=0)
    table = table.reshape(count, parts, final_rows).transpose(1, 0, 2)
    table = lax.all_to_all(table, SHARD, split_axis=0, concat_axis=0, tiled=True)
    table = jnp.sum(table, axis=0)
    return (
        block_output,
        tokens_grad,
        table[0],
        qkv_sum[0],
        qkv_sum[1],
        qkv_sum[2],
        table[2],
        table[3],
        output_sum,
        table[1],
        table[4:].T,
        gate_weight_grad,
        up_weight_grad,
        down_weight_grad,
    )


def solution(mesh):
    rows = P((OWNER, SHARD), None)
    line = P((OWNER, SHARD))
    part = P(SHARD)
    wide = P(SHARD, None)
    into = P(OWNER, SHARD, None)
    back = P(OWNER, None, SHARD)
    in_specs = (rows,) * 3 + (part, wide, wide, wide, part, part, wide, part, wide)
    in_specs = in_specs + (into, into, back, rows)
    out_specs = (rows, rows, line, rows, rows, rows, line, line, rows, line, rows)
    out_specs = out_specs + (into, into, back)

    return jax.shard_map(local, mesh=mesh, in_specs=in_specs, out_specs=out_specs, check_vma=False)
```
